32 devices in a mesh: dp: 8 (over z, x), tensor: 4 (over y, core).
Axes of the slice: x: 2, y: 2, z: 4, core: 2. Of those that a mesh axis runs over, the one named last changes fastest.
Arguments:
- tokens: bfloat16 [8192, 768], P('dp'), may hold values from -6 to 6
- gain_one: float32 [768], replicated, may hold values from 0.5 to 1.5
- bias_one: float32 [768], replicated, may hold values from -1 to 1
- w_attn: bfloat16 [3, 768, 768], P(None, None, 'tensor'), may hold values from -0.21875 to 0.21875
- w_out: bfloat16 [768, 768], P('tensor'), may hold values from -0.4375 to 0.4375
- gain_two: float32 [768], replicated, may hold values from 0.5 to 1.5
- bias_two: float32 [768], replicated, may hold values from -1 to 1
- w_up: bfloat16 [768, 3072], P(None, 'tensor'), may hold values from -0.21875 to 0.21875
- w_down: bfloat16 [3072, 768], P('tensor'), may hold values from -0.109375 to 0.109375
- piece_lengths: int32 [8, 8], P('dp'), may hold values from 1 to 256, 1024 in all within a row
- cotangent: float32 [8192, 768], P('dp'), may hold values from -6 to 6
Outputs:
- output: float32 [8192, 768], P('dp')
- input_grad: float32 [8192, 768], P('dp')
- grad_attn: float32 [3, 768, 768], P(None, 'dp', 'tensor')
- grad_out: float32 [768, 768], P('tensor', 'dp')
- grad_up: float32 [768, 3072], P('dp', 'tensor')
- grad_down: float32 [3072, 768], P('tensor', 'dp')
- grad_gain_one: float32 [768], P('dp')
- grad_bias_one: float32 [768], P('dp')
- grad_gain_two: float32 [768], P('dp')
- grad_bias_two: float32 [768], P('dp')
The draws below stay inside these ranges and needn't reach their ends.
Inputs may be any that keep to these rules, and one draw needn't show every extreme that they name: `piece_lengths`: in each row the entries are the lengths of its consecutive pieces, the last entry its padding tail; they sum to 1024 and one entry of each row equals 256.
All inputs are finite; a program needn't handle non-finite values.
Results may differ from the reference program's by a relative error of at most 0.022.
Values may be sent and summed in bfloat16 or wider, within the bound.
A program may use at most 128 MiB of HBM per device.

```python
import math
import jax
import jax.numpy as jnp
import numpy as np
from jax import lax

D = 768
HEADS = 12
HEAD = 64
FF = 3072
SEQ = 1024
MAXPIECE = 256
NPIECE = 8
SEQS = 8
TOKENS = 8192


def levels(own_key, shape, shards, low, high):
    def one(dim, parts):
        heights = jax.random.uniform(jax.random.fold_in(jax.random.fold_in(own_key, 6), dim), (parts,), jnp.float32, low / len(shards), high / len(shards))
        return jnp.repeat(jnp.exp(heights), shape[dim] // parts).reshape((-1,) + (1,) * (len(shape) - dim - 1))

    level = one(*shards[0])
    for cut in shards[1:]:
        level = level * one(*cut)
    return level


def length_profile(amount, total, most, slope):
    portions = [(1 << 20) // math.isqrt(standing ** slope) + 1 for standing in range(2, amount + 1)]
    surplus, holding = total - most - (amount - 1), [1] * (amount - 1)
    while surplus > 0:
        movable = [i for i in range(amount - 1) if holding[i] < most]
        whole, left = sum([portions[i] for i in movable]), surplus
        for i in movable:
            extra = min(most - holding[i], max(1, left * portions[i] // whole), surplus)
            holding[i] = holding[i] + extra
            surplus = surplus - extra
    return np.array([most] + holding)


def ragged(rng, number_of, total, most, slope):
    if number_of == 2:
        one = jax.random.randint(rng, (), max(1, total - most), min(most, total - 1) + 1)
        return jnp.stack([one, total - one])
    sizes = jnp.asarray(length_profile(number_of, total, most, slope), jnp.int32)
    twos = (number_of - 1) // 2
    source_of, receiver = sizes[1:1 + 2 * twos:2], sizes[2:2 + 2 * twos:2]
    room = jnp.minimum(source_of - 1, most - receiver)
    passed = jax.random.randint(jax.random.fold_in(rng, 1), (twos,), 0, 1 << 20) % (room + 1)
    sizes = sizes.at[1:1 + 2 * twos:2].set(source_of - passed).at[2:2 + 2 * twos:2].set(receiver + passed)
    return sizes[jax.random.permutation(jax.random.fold_in(rng, 2), number_of)]


def noise(own_key, shape, scale, most, cuts=(), kind=jnp.bfloat16):
    drawn = scale * jax.random.normal(own_key, shape, jnp.float32)
    if cuts:
        drawn = drawn * levels(own_key, shape, cuts, -0.22, 0.18)
    return jnp.clip(drawn, -most, most).astype(kind)


def setup_inputs(seed: int = 0) -> dict:
    arg_keys = jax.random.split(jax.random.key(seed), 12)
    tokens = noise(arg_keys[0], (TOKENS, D), 1.0, 6.0, ((0, 8),))
    gain_one = jnp.clip(1.0 + 0.1 * jax.random.normal(arg_keys[1], (D,), jnp.float32), 0.5, 1.5)
    bias_one = noise(arg_keys[2], (D,), 0.2, 1.0, (), jnp.float32)
    w_attn = noise(arg_keys[3], (3, D, D), D ** -0.5, 0.21875, ((2, 4),))
    w_out = noise(arg_keys[4], (D, D), (D // 4) ** -0.5, 0.4375, ((0, 4),))
    gain_two = jnp.clip(1.0 + 0.1 * jax.random.normal(arg_keys[5], (D,), jnp.float32), 0.5, 1.5)
    bias_two = noise(arg_keys[6], (D,), 0.2, 1.0, (), jnp.float32)
    w_up = noise(arg_keys[7], (D, FF), D ** -0.5, 0.21875, ((1, 4),))
    w_down = noise(arg_keys[8], (FF, D), FF ** -0.5, 0.109375, ((0, 4),))
    piece_lengths = jax.vmap(lambda own: ragged(own, NPIECE, SEQ, MAXPIECE, 2))(jax.random.split(arg_keys[9], SEQS)).reshape((SEQS, NPIECE)).astype(jnp.int32)
    cotangent = noise(arg_keys[10], (TOKENS, D), 1.0, 6.0, ((0, 8),), jnp.float32)
    return {"tokens": tokens, "gain_one": gain_one, "bias_one": bias_one, "w_attn": w_attn, "w_out": w_out, "gain_two": gain_two, "bias_two": bias_two, "w_up": w_up, "w_down": w_down, "piece_lengths": piece_lengths, "cotangent": cotangent}


@jax.custom_vjp
def low(v):
    return lax.optimization_barrier(v.astype(jnp.bfloat16)).astype(jnp.float32)

@jax.custom_vjp
def low_back(v):
    return v

def low_keep(v):
    return (low(v), None)

def low_pass(kept, grad):
    return (grad,)

def back_keep(v):
    return (v, None)

def back_low(kept, grad):
    return (low(grad),)
low.defvjp(low_keep, low_pass)
low_back.defvjp(back_keep, back_low)
EPSILON = 1e-05
HIGHEST = lax.Precision.HIGHEST

def normalize(inputs, gain, bias):
    center = inputs - lax.optimization_barrier(jnp.mean(inputs, axis=-1, keepdims=True))
    spread = lax.optimization_barrier(jnp.mean(center * center, axis=-1, keepdims=True))
    return center * lax.rsqrt(spread + EPSILON) * gain + bias

def piece_tables(lengths):
    piece_ends = jnp.cumsum(lengths).astype(jnp.int32)
    position = jnp.arange(SEQ, dtype=jnp.int32)
    piece_of = lax.optimization_barrier(jnp.sum((position[:, None] >= piece_ends[None, :]).astype(jnp.int32), axis=1)).astype(jnp.int32)
    starts = (piece_ends - lengths).astype(jnp.int32)
    numbers = jnp.arange(NPIECE, dtype=jnp.int32)
    piece_first = lax.optimization_barrier(jnp.sum(jnp.where(piece_of[:, None] == numbers[None, :], starts[None, :], 0), axis=1)).astype(jnp.int32)
    same_piece = piece_of[:, None] == piece_of[None, :]
    earlier = position[None, :] < position[:, None]
    allowed = same_piece & (earlier | (position[None, :] == position[:, None]))
    chosen = (same_piece & earlier & (position[None, :] != piece_first[None, :])).astype(jnp.float32)
    carry = (same_piece & earlier).astype(jnp.float32)
    valid = (piece_of < NPIECE - 1).astype(jnp.float32)
    return (allowed, chosen, carry, valid)

def attend(packed):
    query_rows, key_rows, value_rows, lengths = packed
    allowed, chosen, carry, valid = piece_tables(lengths)
    scaling = HEAD ** (-0.5)
    query_zero = query_rows[:, :HEAD]
    key_zero = key_rows[:, :HEAD]
    score = low_back(jnp.dot(query_zero, key_zero.T, precision=HIGHEST) * scaling)
    selected = low(jnp.maximum(score, 0.0) * chosen)
    penalty = low_back(jnp.dot(carry, selected, precision=HIGHEST))
    split_query = query_rows.reshape(SEQ, HEADS, HEAD)
    split_key = key_rows.reshape(SEQ, HEADS, HEAD)
    split_value = value_rows.reshape(SEQ, HEADS, HEAD)
    raw_scores = low_back(jnp.einsum('ihd,jhd->hij', split_query, split_key, precision=HIGHEST) * scaling)
    logits = jnp.where(allowed[None], raw_scores - penalty[None], -1e+30)
    weights = low(jax.nn.softmax(logits, axis=-1))
    mixed = jnp.einsum('hij,jhd->ihd', weights, split_value, precision=HIGHEST)
    return (mixed * valid[:, None, None]).reshape(SEQ, D)

def layer(inputs, gain_one, bias_one, w_attn, w_out, gain_two, bias_two, w_up, w_down, lengths):
    act_one = low(normalize(inputs, gain_one, bias_one))
    queries = low(low_back(jnp.dot(act_one, w_attn[0], precision=HIGHEST)))
    key_all = low(low_back(jnp.dot(act_one, w_attn[1], precision=HIGHEST)))
    value_all = low(low_back(jnp.dot(act_one, w_attn[2], precision=HIGHEST)))
    row_count = inputs.shape[0] // SEQ
    mixed = lax.map(jax.checkpoint(attend), (queries.reshape(row_count, SEQ, D), key_all.reshape(row_count, SEQ, D), value_all.reshape(row_count, SEQ, D), lengths))
    mixed = low(low_back(mixed.reshape(-1, D)))
    branch = low_back(jnp.dot(mixed, w_out, precision=HIGHEST))
    hidden_one = inputs + branch
    act_two = low(normalize(hidden_one, gain_two, bias_two))
    up_all = low_back(jnp.dot(act_two, w_up, precision=HIGHEST))
    hidden = low(jax.nn.gelu(up_all, approximate=True))
    feed = low_back(jnp.dot(hidden, w_down, precision=HIGHEST))
    return hidden_one + feed

def reference(tokens, gain_one, bias_one, w_attn, w_out, gain_two, bias_two, w_up, w_down, piece_lengths, cotangent):
    inputs = tokens.astype(jnp.float32)
    params = (inputs, gain_one, bias_one, w_attn.astype(jnp.float32), w_out.astype(jnp.float32), gain_two, bias_two, w_up.astype(jnp.float32), w_down.astype(jnp.float32))

    def forward(*values_in):
        return layer(*values_in, piece_lengths)
    output, pull = jax.vjp(forward, *params)
    grads = pull(cotangent)
    return (output, grads[0], grads[3], grads[4], grads[7], grads[8], grads[1], grads[2], grads[5], grads[6])
```

```python
import functools

import jax
import jax.numpy as jnp
from jax import lax
from jax.experimental import pallas as pl
from jax.experimental.pallas import tpu as pltpu
from jax.sharding import PartitionSpec as P

F32 = jnp.float32
BF16 = jnp.bfloat16
MESH = pl.DeviceIdType.MESH
HEAD = 64
EPSILON = 1e-05
BLOCK = 128
BAND = 384
PAD = BAND - BLOCK
CHUNK = 256
SCALING = HEAD ** (-0.5)
NT = (((1,), (1,)), ((), ()))
TN = (((0,), (0,)), ((), ()))


def dot(a, b):
    return jnp.dot(a, b, preferred_element_type=F32)


def dot_nt(a, b):
    return lax.dot_general(a, b, NT, preferred_element_type=F32)


def dot_tn(a, b):
    return lax.dot_general(a, b, TN, preferred_element_type=F32)


def rows_at(index, size):
    return pl.ds(pl.multiple_of(index * size, size), size)


def first_of(position, lengths, pieces):
    first = jnp.zeros_like(position)
    end = jnp.int32(0)
    for piece in range(pieces - 1):
        size = lengths[0, piece]
        end = end + size
        first = jnp.where(position >= end, end, first)
    return first, position < end


def norm_stats(x):
    center = x - jnp.mean(x, axis=-1, keepdims=True)
    spread = jnp.mean(center * center, axis=-1, keepdims=True)
    return center, lax.rsqrt(spread + EPSILON)


def remote(src, dst, send, recv, peer):
    return pltpu.make_async_remote_copy(
        src_ref=src, dst_ref=dst, send_sem=send, recv_sem=recv, device_id=peer, device_id_type=MESH
    )


def greet(peers):
    barrier = pltpu.get_barrier_semaphore()
    for peer in peers:
        pl.semaphore_signal(barrier, inc=1, device_id=peer, device_id_type=MESH)
    pl.semaphore_wait(barrier, len(peers))


def forward_kernel(
    pieces,
    lengths, tokens, gain, bias, w_attn, w_out,
    act, query, key, value, query0, key0, probs, selected, mixed, w_out_all, w_zero,
    zero_send, zero_recv, out_send, out_recv, mix_send, mix_recv, local_sem,
):
    seq, width = tokens.shape
    local = w_attn.shape[2]
    heads = local // HEAD
    blocks = seq // BLOCK
    chunks = seq // CHUNK
    mine = lax.axis_index("tensor")
    twin = {"tensor": mine ^ 1}
    across = {"tensor": mine ^ 2}
    greet((twin, across))

    own = pltpu.make_async_copy(w_out, w_out_all.at[mine], local_sem.at[0])
    own.start()

    def out_copy(stage, slot, peer):
        block = w_out_all.at[slot]
        return remote(block, block, out_send.at[stage], out_recv.at[stage], peer)

    def zero_copy(stage, peer, source):
        return remote(source, w_zero, zero_send.at[stage], zero_recv.at[0], peer)

    head_cols = w_attn.at[pl.ds(0, 2), :, pl.ds(0, BLOCK)]

    @pl.when(mine == 0)
    def _():
        zero_copy(0, across, head_cols).start()
        zero_copy(1, twin, head_cols).start()
        w_zero[...] = w_attn[0:2, :, 0:BLOCK]

    own.wait()
    out_copy(0, mine, across).start()
    out_copy(1, mine, twin).start()

    lane = lax.broadcasted_iota(jnp.int32, (1, local), 1)
    for ref in (key, value, key0, selected):
        ref[0:PAD, :] = jnp.zeros((PAD, ref.shape[1]), ref.dtype)

    def project(step, carry):
        rows = rows_at(step, CHUNK)
        padded = pl.ds(pl.multiple_of(step * CHUNK + PAD, CHUNK), CHUNK)
        center, scale = norm_stats(tokens[rows, :].astype(F32))
        low = (center * scale * gain[...] + bias[...]).astype(BF16)
        act[rows, :] = low
        query[rows, :] = dot(low, w_attn[0]).astype(BF16)
        key[padded, :] = dot(low, w_attn[1]).astype(BF16)
        value[padded, :] = dot(low, w_attn[2]).astype(BF16)
        return carry

    lax.fori_loop(0, chunks, project, 0)

    @pl.when(mine != 0)
    def _():
        zero_copy(0, twin, w_zero).wait_recv()

    @pl.when(mine == 2)
    def _():
        zero_copy(0, twin, w_zero).start()

    lane0 = lax.broadcasted_iota(jnp.int32, (1, BLOCK), 1)
    keep0 = jnp.where(lane0 < HEAD, SCALING, 0.0)

    def project0(step, carry):
        rows = rows_at(step, CHUNK)
        padded = pl.ds(pl.multiple_of(step * CHUNK + PAD, CHUNK), CHUNK)
        low = act[rows, :]
        found = dot(low, w_zero[0]).astype(BF16).astype(F32)
        query0[rows, :] = (found * keep0).astype(BF16)
        key0[padded, :] = dot(low, w_zero[1]).astype(BF16)
        return carry

    lax.fori_loop(0, chunks, project0, 0)

    row = lax.broadcasted_iota(jnp.int32, (BLOCK, 1), 0)
    column = lax.broadcasted_iota(jnp.int32, (1, BAND), 1) - PAD

    def select(block, carry):
        rows = rows_at(block, BLOCK)
        first, _ = first_of(row + block * BLOCK, lengths, pieces)
        first = first - block * BLOCK
        band = rows_at(block, BLOCK).start
        score = dot_nt(query0[rows, :], key0[pl.ds(band, BAND), :])
        keep = (column > first) & (column < row)
        selected[pl.ds(band + PAD, BLOCK), :] = jnp.where(
            keep, jnp.maximum(score, 0.0), 0.0
        ).astype(BF16)
        return carry

    lax.fori_loop(0, blocks, select, 0)

    def mix_copy(stage, slot, block, peer):
        part = mixed.at[slot, rows_at(block, BLOCK)]
        return remote(part, part, mix_send.at[stage, block], mix_recv.at[stage, block], peer)

    def attend(step, carry):
        block = blocks - 1 - step
        rows = rows_at(block, BLOCK)
        band = rows.start
        first, valid = first_of(row + block * BLOCK, lengths, pieces)
        first = first - block * BLOCK
        inside = column >= first
        carried = (inside & (column < row)).astype(BF16)
        parts = [
            dot(
                carried[:, part * BLOCK:(part + 1) * BLOCK],
                selected[pl.ds(band + part * BLOCK, BLOCK), BAND - (part + 1) * BLOCK:],
            )
            for part in range(BAND // BLOCK)
        ]
        penalty = jnp.concatenate(
            [
                sum(parts[part][:, at * BLOCK:(at + 1) * BLOCK] for part in range(at, BAND // BLOCK))
                for at in range(BAND // BLOCK)
            ],
            axis=1,
        )
        offset = jnp.where(inside & (column <= row), -penalty, -1e30)
        queries = query[rows, :].astype(F32)
        keys = key[pl.ds(band, BAND), :]
        values = value[pl.ds(band, BAND), :]
        total = jnp.zeros((BLOCK, local), F32)
        for head in range(heads):
            here = (lane >= head * HEAD) & (lane < (head + 1) * HEAD)
            logits = dot_nt((queries * jnp.where(here, SCALING, 0.0)).astype(BF16), keys) + offset
            raised = jnp.exp(logits - jnp.max(logits, axis=-1, keepdims=True))
            low = (raised * (1.0 / jnp.sum(raised, axis=-1, keepdims=True))).astype(BF16)
            probs[block, head] = low
            total = jnp.where(here, dot(low, values), total)
        mixed[mine, rows, :] = (total * valid.astype(F32)).astype(BF16)
        mix_copy(0, mine, block, across).start()
        mix_copy(1, mine, block, twin).start()
        return carry

    lax.fori_loop(0, blocks, attend, 0)

    out_copy(0, mine ^ 2, across).wait_recv()
    out_copy(2, mine ^ 2, twin).start()

    def relay(step, carry):
        block = blocks - 1 - step
        mix_copy(0, mine ^ 2, block, across).wait_recv()
        mix_copy(2, mine ^ 2, block, twin).start()
        return carry

    lax.fori_loop(0, blocks, relay, 0)

    def drain(step, carry):
        block = blocks - 1 - step
        mix_copy(1, mine ^ 1, block, twin).wait_recv()
        mix_copy(2, mine ^ 3, block, twin).wait_recv()
        mix_copy(0, mine, block, across).wait_send()
        mix_copy(1, mine, block, twin).wait_send()
        mix_copy(2, mine ^ 2, block, twin).wait_send()
        return carry

    lax.fori_loop(0, blocks, drain, 0)
    out_copy(1, mine ^ 1, twin).wait_recv()
    out_copy(2, mine ^ 3, twin).wait_recv()
    out_copy(0, mine, across).wait_send()
    out_copy(1, mine, twin).wait_send()
    out_copy(2, mine ^ 2, twin).wait_send()

    @pl.when(mine == 0)
    def _():
        zero_copy(0, across, head_cols).wait_send()
        zero_copy(1, twin, head_cols).wait_send()

    @pl.when(mine == 2)
    def _():
        zero_copy(0, twin, w_zero).wait_send()


VMEM = pl.BlockSpec(memory_space=pltpu.VMEM)
SMEM = pl.BlockSpec(memory_space=pltpu.SMEM)
DMA = pltpu.SemaphoreType.DMA
LIMIT = 66_000_000


def forward_call(tokens, gain, bias, w_attn, w_out, lengths):
    seq, width = tokens.shape
    local = w_attn.shape[2]
    heads = local // HEAD
    blocks = seq // BLOCK
    shards = lax.axis_size("tensor")
    shape = jax.ShapeDtypeStruct
    outs = (
        shape((seq, width), BF16),
        shape((seq, local), BF16),
        shape((seq + PAD, local), BF16),
        shape((seq + PAD, local), BF16),
        shape((seq, BLOCK), BF16),
        shape((seq + PAD, BLOCK), BF16),
        shape((blocks, heads, BLOCK, BAND), BF16),
        shape((seq + PAD, BAND), BF16),
        shape((shards, seq, local), BF16),
        shape((shards, local, width), BF16),
        shape((2, width, BLOCK), BF16),
    )
    return pl.pallas_call(
        functools.partial(forward_kernel, lengths.shape[1]),
        out_shape=outs,
        in_specs=[SMEM] + [VMEM] * 5,
        out_specs=(VMEM,) * len(outs),
        scratch_shapes=[DMA((2,)), DMA((1,)), DMA((3,)), DMA((3,)), DMA((3, blocks)), DMA((3, blocks)), DMA((1,))],
        compiler_params=pltpu.CompilerParams(
            collective_id=0, has_side_effects=True, vmem_limit_bytes=LIMIT
        ),
        name="forward",
    )(lengths, tokens, gain, bias, w_attn, w_out)


SEQ = 1024
NPIECE = 8


def from_root(block, axis, source):
    block = jnp.where(lax.axis_index(axis) == source, block, jnp.zeros_like(block))
    return lax.psum(block, axis)


def normalize(inputs, gain, bias):
    center = inputs - jnp.mean(inputs, axis=-1, keepdims=True)
    spread = jnp.mean(center * center, axis=-1, keepdims=True)
    return center * lax.rsqrt(spread + EPSILON) * gain + bias


def piece_tables(lengths):
    piece_ends = jnp.cumsum(lengths)
    position = jnp.arange(SEQ, dtype=jnp.int32)
    piece_of = jnp.sum((position[:, None] >= piece_ends[None, :]).astype(jnp.int32), axis=1)
    starts = piece_ends - lengths
    numbers = jnp.arange(NPIECE, dtype=jnp.int32)
    piece_first = jnp.sum(
        jnp.where(piece_of[:, None] == numbers[None, :], starts[None, :], 0), axis=1
    )
    same_piece = piece_of[:, None] == piece_of[None, :]
    earlier = position[None, :] < position[:, None]
    allowed = same_piece & (earlier | (position[None, :] == position[:, None]))
    chosen = (same_piece & earlier & (position[None, :] != piece_first[None, :])).astype(
        jnp.float32
    )
    carry_low = (same_piece & earlier).astype(jnp.bfloat16)
    valid = (piece_of < NPIECE - 1).astype(jnp.float32)
    return (allowed, chosen, carry_low, valid)


def selection(query_zero, key_zero, chosen, carry_low, scaling):
    score = (
        jnp.einsum("id,jd->ij", query_zero, key_zero, preferred_element_type=jnp.float32) * scaling
    )
    selected = (jnp.maximum(score, 0.0) * chosen).astype(jnp.bfloat16)
    penalty = jnp.dot(carry_low, selected, preferred_element_type=jnp.float32)
    return (score, penalty)


def attention_logits(query_rows, key_rows, penalty, allowed, scaling):
    raw_scores = (
        jnp.einsum("ihd,jhd->hij", query_rows, key_rows, preferred_element_type=jnp.float32)
        * scaling
    )
    return jnp.where(allowed[None], raw_scores - penalty[None], -1e30)


def forward_row(packed):
    query_rows, key_rows, value_rows, query_zero, key_zero, lengths = packed
    allowed, chosen, carry_low, valid = piece_tables(lengths)
    scaling = HEAD ** (-0.5)
    score, penalty = selection(query_zero, key_zero, chosen, carry_low, scaling)
    logits = attention_logits(query_rows, key_rows, penalty, allowed, scaling)
    peak = jnp.max(logits, axis=-1, keepdims=True)
    shifted = jnp.exp(logits - peak)
    total = jnp.sum(shifted, axis=-1, keepdims=True)
    weights = (shifted / total).astype(jnp.bfloat16)
    mixed = (
        jnp.einsum("hij,jhd->ihd", weights, value_rows, preferred_element_type=jnp.float32)
        * valid[:, None, None]
    )
    return (mixed.astype(jnp.bfloat16), (peak + jnp.log(total))[..., 0])


def body(
    tokens,
    gain_one,
    bias_one,
    w_attn,
    w_out,
    gain_two,
    bias_two,
    w_up,
    w_down,
    piece_lengths,
    cotangent,
):
    scaling = HEAD ** (-0.5)
    local_width = w_attn.shape[2]
    local_heads = local_width // HEAD
    row_count = tokens.shape[0] // SEQ
    leader = lax.axis_index("tensor") == 0
    inputs = tokens.astype(jnp.float32)
    normed_one = normalize(inputs, gain_one, bias_one)
    act_one = normed_one.astype(jnp.bfloat16)
    (
        act_one, query_flat, key_flat, value_flat, query_zero, key_zero, probs_band, selected_band, mixed_all, w_out_all, _
    ) = forward_call(
        tokens, gain_one.reshape(1, -1), bias_one.reshape(1, -1), w_attn, w_out, piece_lengths
    )
    query_all = query_flat.reshape(row_count, SEQ, local_heads, HEAD)
    key_all = key_flat[PAD:].reshape(row_count, SEQ, local_heads, HEAD)
    value_all = value_flat[PAD:].reshape(row_count, SEQ, local_heads, HEAD)
    query_zero = (query_zero[:, :HEAD] * 8).reshape(row_count, SEQ, HEAD)
    key_zero = key_zero[PAD:, :HEAD].reshape(row_count, SEQ, HEAD)
    mixed, log_total = lax.map(
        forward_row, (query_all, key_all, value_all, query_zero, key_zero, piece_lengths)
    )
    mixed = lax.dynamic_index_in_dim(mixed_all, lax.axis_index("tensor"), 0, keepdims=False)
    branch = jnp.einsum("sre,sed->rd", mixed_all, w_out_all, preferred_element_type=jnp.float32)
    hidden_one = inputs + branch
    act_two = normalize(hidden_one, gain_two, bias_two).astype(jnp.bfloat16)
    up_all = jnp.dot(act_two, w_up, preferred_element_type=jnp.float32)
    hidden = jax.nn.gelu(up_all, approximate=True).astype(jnp.bfloat16)
    feed = lax.psum(
        jnp.dot(hidden, w_down, preferred_element_type=jnp.float32).astype(jnp.bfloat16), "tensor"
    ).astype(jnp.float32)
    output = hidden_one + feed
    grad_mlp = cotangent.astype(jnp.bfloat16)
    grad_hidden = jnp.einsum("rd,fd->rf", grad_mlp, w_down, preferred_element_type=jnp.float32)
    grad_down = jnp.einsum("rf,rd->fd", hidden, grad_mlp, preferred_element_type=jnp.float32)

    def gelu_tanh(values_in):
        return jax.nn.gelu(values_in, approximate=True)

    gelu_pull = jax.vjp(gelu_tanh, up_all)[1]
    grad_pre = gelu_pull(grad_hidden)[0].astype(jnp.bfloat16)
    grad_up = jnp.einsum("rd,rf->df", act_two, grad_pre, preferred_element_type=jnp.float32)
    grad_act_two = jnp.einsum("rf,df->rd", grad_pre, w_up, preferred_element_type=jnp.float32)
    grad_act_two = lax.psum(grad_act_two.astype(jnp.bfloat16), "tensor").astype(jnp.float32)
    norm_pull = jax.vjp(normalize, hidden_one, gain_two, bias_two)[1]
    grad_norm_two, grad_gain_two, grad_bias_two = norm_pull(grad_act_two)
    grad_hidden_one = cotangent + grad_norm_two
    grad_branch = grad_hidden_one.astype(jnp.bfloat16)
    grad_out = jnp.einsum("re,rd->ed", mixed, grad_branch, preferred_element_type=jnp.float32)
    grad_mixed = jnp.einsum(
        "rd,ed->re", grad_branch, w_out, preferred_element_type=jnp.float32
    ).astype(jnp.bfloat16)
    grad_mixed = grad_mixed.reshape(row_count, SEQ, local_heads, HEAD)
    head_mask = jnp.where(leader, jnp.arange(local_heads) == 0, False).astype(jnp.float32)

    def backward_row(packed):
        query_rows, key_rows, value_rows, query_one, key_one, log_row, grad_rows, lengths = packed
        allowed, chosen, carry_low, valid = piece_tables(lengths)
        score, penalty = selection(query_one, key_one, chosen, carry_low, scaling)
        logits = attention_logits(query_rows, key_rows, penalty, allowed, scaling)
        probs = jnp.exp(logits - log_row[..., None])
        weights = probs.astype(jnp.bfloat16)
        grad_masked = grad_rows * valid[:, None, None].astype(jnp.bfloat16)
        grad_probs = jnp.einsum(
            "ihd,jhd->hij", grad_masked, value_rows, preferred_element_type=jnp.float32
        )
        grad_value = jnp.einsum(
            "hij,ihd->jhd", weights, grad_masked, preferred_element_type=jnp.float32
        )
        inner = jnp.sum(probs * grad_probs, axis=-1, keepdims=True)
        grad_logits = probs * (grad_probs - inner)
        penalty_term = -jnp.sum(grad_logits, axis=0)
        grad_penalty = lax.psum(penalty_term.astype(jnp.bfloat16), "tensor")
        grad_low = grad_logits.astype(jnp.bfloat16)
        grad_query = (
            jnp.einsum("hij,jhd->ihd", grad_low, key_rows, preferred_element_type=jnp.float32)
            * scaling
        )
        grad_key = (
            jnp.einsum("hij,ihd->jhd", grad_low, query_rows, preferred_element_type=jnp.float32)
            * scaling
        )
        grad_select = jnp.einsum(
            "ik,ij->kj", carry_low, grad_penalty, preferred_element_type=jnp.float32
        )
        grad_score = (grad_select * chosen * (score > 0.0).astype(jnp.float32)).astype(jnp.bfloat16)
        extra_query = (
            jnp.einsum("ij,jd->id", grad_score, key_one, preferred_element_type=jnp.float32)
            * scaling
        )
        extra_key = (
            jnp.einsum("ij,id->jd", grad_score, query_one, preferred_element_type=jnp.float32)
            * scaling
        )
        grad_query = grad_query + extra_query[:, None, :] * head_mask[None, :, None]
        grad_key = grad_key + extra_key[:, None, :] * head_mask[None, :, None]
        return jnp.stack([grad_query, grad_key, grad_value]).astype(jnp.bfloat16)

    grad_rows_all = lax.map(
        backward_row,
        (query_all, key_all, value_all, query_zero, key_zero, log_total, grad_mixed, piece_lengths),
    )
    grad_proj = jnp.moveaxis(grad_rows_all, 1, 0).reshape(3, -1, local_width)
    grad_attn = jnp.einsum("rd,cre->cde", act_one, grad_proj, preferred_element_type=jnp.float32)
    grad_act_one = jnp.einsum("cre,cde->rd", grad_proj, w_attn, preferred_element_type=jnp.float32)
    grad_act_one = lax.psum(grad_act_one.astype(jnp.bfloat16), "tensor").astype(jnp.float32)
    first_pull = jax.vjp(normalize, inputs, gain_one, bias_one)[1]
    grad_norm_one, grad_gain_one, grad_bias_one = first_pull(grad_act_one)
    input_grad = grad_hidden_one + grad_norm_one
    summed = (
        lax.psum_scatter(grad_attn, "dp", scatter_dimension=1, tiled=True),
        lax.psum_scatter(grad_out, "dp", scatter_dimension=1, tiled=True),
        lax.psum_scatter(grad_up, "dp", scatter_dimension=0, tiled=True),
        lax.psum_scatter(grad_down, "dp", scatter_dimension=1, tiled=True),
        lax.psum_scatter(grad_gain_one, "dp", scatter_dimension=0, tiled=True),
        lax.psum_scatter(grad_bias_one, "dp", scatter_dimension=0, tiled=True),
        lax.psum_scatter(grad_gain_two, "dp", scatter_dimension=0, tiled=True),
        lax.psum_scatter(grad_bias_two, "dp", scatter_dimension=0, tiled=True),
    )
    (
        summed_attn,
        summed_out,
        summed_up,
        summed_down,
        summed_gain_one,
        summed_bias_one,
        summed_gain_two,
        summed_bias_two,
    ) = summed
    return (
        output,
        input_grad,
        summed_attn,
        summed_out,
        summed_up,
        summed_down,
        summed_gain_one,
        summed_bias_one,
        summed_gain_two,
        summed_bias_two,
    )


def solution(mesh):
    placed = (
        P("dp", None),
        P(),
        P(),
        P(None, None, "tensor"),
        P("tensor", None),
        P(),
        P(),
        P(None, "tensor"),
        P("tensor", None),
        P("dp", None),
        P("dp", None),
    )
    return jax.shard_map(
        body,
        mesh=mesh,
        in_specs=placed,
        out_specs=(
            P("dp", None),
            P("dp", None),
            P(None, "dp", "tensor"),
            P("tensor", "dp"),
            P("dp", "tensor"),
            P("tensor", "dp"),
            P("dp"),
            P("dp"),
            P("dp"),
            P("dp"),
        ),
        check_vma=False,
    )
```

```python
import functools

import jax
import jax.numpy as jnp
from jax import lax
from jax.experimental import pallas as pl
from jax.experimental.pallas import tpu as pltpu
from jax.sharding import PartitionSpec as P

F32 = jnp.float32
BF16 = jnp.bfloat16
MESH = pl.DeviceIdType.MESH
HEAD = 64
EPSILON = 1e-05
BLOCK = 128
BAND = 384
PAD = BAND - BLOCK
CHUNK = 256
SCALING = HEAD ** (-0.5)
NT = (((1,), (1,)), ((), ()))
TN = (((0,), (0,)), ((), ()))


def dot(a, b):
    return jnp.dot(a, b, preferred_element_type=F32)


def dot_nt(a, b):
    return lax.dot_general(a, b, NT, preferred_element_type=F32)


def dot_tn(a, b):
    return lax.dot_general(a, b, TN, preferred_element_type=F32)


def rows_at(index, size):
    return pl.ds(pl.multiple_of(index * size, size), size)


def first_of(position, lengths, pieces):
    first = jnp.zeros_like(position)
    end = jnp.int32(0)
    for piece in range(pieces - 1):
        size = lengths[0, piece]
        end = end + size
        first = jnp.where(position >= end, end, first)
    return first, position < end


def norm_stats(x):
    center = x - jnp.mean(x, axis=-1, keepdims=True)
    spread = jnp.mean(center * center, axis=-1, keepdims=True)
    return center, lax.rsqrt(spread + EPSILON)


def remote(src, dst, send, recv, peer):
    return pltpu.make_async_remote_copy(
        src_ref=src, dst_ref=dst, send_sem=send, recv_sem=recv, device_id=peer, device_id_type=MESH
    )


def greet(peers):
    barrier = pltpu.get_barrier_semaphore()
    for peer in peers:
        pl.semaphore_signal(barrier, inc=1, device_id=peer, device_id_type=MESH)
    pl.semaphore_wait(barrier, len(peers))


def forward_kernel(
    pieces,
    lengths, tokens, gain, bias, w_attn, w_out,
    act, query, key, value, query0, key0, probs, selected, mixed, w_out_all, w_zero,
    zero_send, zero_recv, out_send, out_recv, mix_send, mix_recv, local_sem,
):
    seq, width = tokens.shape
    local = w_attn.shape[2]
    heads = local // HEAD
    blocks = seq // BLOCK
    chunks = seq // CHUNK
    mine = lax.axis_index("tensor")
    twin = {"tensor": mine ^ 1}
    across = {"tensor": mine ^ 2}
    greet((twin, across))

    own = pltpu.make_async_copy(w_out, w_out_all.at[mine], local_sem.at[0])
    own.start()

    def out_copy(stage, slot, peer):
        block = w_out_all.at[slot]
        return remote(block, block, out_send.at[stage], out_recv.at[stage], peer)

    def zero_copy(stage, peer, source):
        return remote(source, w_zero, zero_send.at[stage], zero_recv.at[0], peer)

    head_cols = w_attn.at[pl.ds(0, 2), :, pl.ds(0, BLOCK)]

    @pl.when(mine == 0)
    def _():
        zero_copy(0, across, head_cols).start()
        zero_copy(1, twin, head_cols).start()
        w_zero[...] = w_attn[0:2, :, 0:BLOCK]

    own.wait()
    out_copy(0, mine, across).start()
    out_copy(1, mine, twin).start()

    lane = lax.broadcasted_iota(jnp.int32, (1, local), 1)
    for ref in (key, value, key0, selected):
        ref[0:PAD, :] = jnp.zeros((PAD, ref.shape[1]), ref.dtype)

    def project(step, carry):
        rows = rows_at(step, CHUNK)
        padded = pl.ds(pl.multiple_of(step * CHUNK + PAD, CHUNK), CHUNK)
        center, scale = norm_stats(tokens[rows, :].astype(F32))
        low = (center * scale * gain[...] + bias[...]).astype(BF16)
        act[rows, :] = low
        query[rows, :] = dot(low, w_attn[0]).astype(BF16)
        key[padded, :] = dot(low, w_attn[1]).astype(BF16)
        value[padded, :] = dot(low, w_attn[2]).astype(BF16)
        return carry

    lax.fori_loop(0, chunks, project, 0)

    @pl.when(mine != 0)
    def _():
        zero_copy(0, twin, w_zero).wait_recv()

    @pl.when(mine == 2)
    def _():
        zero_copy(0, twin, w_zero).start()

    lane0 = lax.broadcasted_iota(jnp.int32, (1, BLOCK), 1)
    keep0 = jnp.where(lane0 < HEAD, SCALING, 0.0)

    def project0(step, carry):
        rows = rows_at(step, CHUNK)
        padded = pl.ds(pl.multiple_of(step * CHUNK + PAD, CHUNK), CHUNK)
        low = act[rows, :]
        found = dot(low, w_zero[0]).astype(BF16).astype(F32)
        query0[rows, :] = (found * keep0).astype(BF16)
        key0[padded, :] = dot(low, w_zero[1]).astype(BF16)
        return carry

    lax.fori_loop(0, chunks, project0, 0)

    row = lax.broadcasted_iota(jnp.int32, (BLOCK, 1), 0)
    column = lax.broadcasted_iota(jnp.int32, (1, BAND), 1) - PAD

    def select(block, carry):
        rows = rows_at(block, BLOCK)
        first, _ = first_of(row + block * BLOCK, lengths, pieces)
        first = first - block * BLOCK
        band = rows_at(block, BLOCK).start
        score = dot_nt(query0[rows, :], key0[pl.ds(band, BAND), :])
        keep = (column > first) & (column < row)
        selected[pl.ds(band + PAD, BLOCK), :] = jnp.where(
            keep, jnp.maximum(score, 0.0), 0.0
        ).astype(BF16)
        return carry

    lax.fori_loop(0, blocks, select, 0)

    def mix_copy(stage, slot, block, peer):
        part = mixed.at[slot, rows_at(block, BLOCK)]
        return remote(part, part, mix_send.at[stage, block], mix_recv.at[stage, block], peer)

    def attend(step, carry):
        block = blocks - 1 - step
        rows = rows_at(block, BLOCK)
        band = rows.start
        first, valid = first_of(row + block * BLOCK, lengths, pieces)
        first = first - block * BLOCK
        inside = column >= first
        carried = (inside & (column < row)).astype(BF16)
        parts = [
            dot(
                carried[:, part * BLOCK:(part + 1) * BLOCK],
                selected[pl.ds(band + part * BLOCK, BLOCK), BAND - (part + 1) * BLOCK:],
            )
            for part in range(BAND // BLOCK)
        ]
        penalty = jnp.concatenate(
            [
                sum(parts[part][:, at * BLOCK:(at + 1) * BLOCK] for part in range(at, BAND // BLOCK))
                for at in range(BAND // BLOCK)
            ],
            axis=1,
        )
        offset = jnp.where(inside & (column <= row), -penalty, -1e30)
        queries = query[rows, :].astype(F32)
        keys = key[pl.ds(band, BAND), :]
        values = value[pl.ds(band, BAND), :]
        total = jnp.zeros((BLOCK, local), F32)
        for head in range(heads):
            here = (lane >= head * HEAD) & (lane < (head + 1) * HEAD)
            logits = dot_nt((queries * jnp.where(here, SCALING, 0.0)).astype(BF16), keys) + offset
            raised = jnp.exp(logits - jnp.max(logits, axis=-1, keepdims=True))
            low = (raised * (1.0 / jnp.sum(raised, axis=-1, keepdims=True))).astype(BF16)
            probs[block, head] = low
            total = jnp.where(here, dot(low, values), total)
        mixed[mine, rows, :] = (total * valid.astype(F32)).astype(BF16)
        mix_copy(0, mine, block, across).start()
        mix_copy(1, mine, block, twin).start()
        return carry

    lax.fori_loop(0, blocks, attend, 0)

    out_copy(0, mine ^ 2, across).wait_recv()
    out_copy(2, mine ^ 2, twin).start()

    def relay(step, carry):
        block = blocks - 1 - step
        mix_copy(0, mine ^ 2, block, across).wait_recv()
        mix_copy(2, mine ^ 2, block, twin).start()
        return carry

    lax.fori_loop(0, blocks, relay, 0)

    def drain(step, carry):
        block = blocks - 1 - step
        mix_copy(1, mine ^ 1, block, twin).wait_recv()
        mix_copy(2, mine ^ 3, block, twin).wait_recv()
        mix_copy(0, mine, block, across).wait_send()
        mix_copy(1, mine, block, twin).wait_send()
        mix_copy(2, mine ^ 2, block, twin).wait_send()
        return carry

    lax.fori_loop(0, blocks, drain, 0)
    out_copy(1, mine ^ 1, twin).wait_recv()
    out_copy(2, mine ^ 3, twin).wait_recv()
    out_copy(0, mine, across).wait_send()
    out_copy(1, mine, twin).wait_send()
    out_copy(2, mine ^ 2, twin).wait_send()

    @pl.when(mine == 0)
    def _():
        zero_copy(0, across, head_cols).wait_send()
        zero_copy(1, twin, head_cols).wait_send()

    @pl.when(mine == 2)
    def _():
        zero_copy(0, twin, w_zero).wait_send()


VMEM = pl.BlockSpec(memory_space=pltpu.VMEM)
SMEM = pl.BlockSpec(memory_space=pltpu.SMEM)
DMA = pltpu.SemaphoreType.DMA
LIMIT = 67_000_000


def forward_call(tokens, gain, bias, w_attn, w_out, lengths):
    seq, width = tokens.shape
    local = w_attn.shape[2]
    heads = local // HEAD
    blocks = seq // BLOCK
    shards = lax.axis_size("tensor")
    shape = jax.ShapeDtypeStruct
    outs = (
        shape((seq, width), BF16),
        shape((seq, local), BF16),
        shape((seq + PAD, local), BF16),
        shape((seq + PAD, local), BF16),
        shape((seq, BLOCK), BF16),
        shape((seq + PAD, BLOCK), BF16),
        shape((blocks, heads, BLOCK, BAND), BF16),
        shape((seq + PAD, BAND), BF16),
        shape((shards, seq, local), BF16),
        shape((shards, local, width), BF16),
        shape((2, width, BLOCK), BF16),
    )
    return pl.pallas_call(
        functools.partial(forward_kernel, lengths.shape[1]),
        out_shape=outs,
        in_specs=[SMEM] + [VMEM] * 5,
        out_specs=(VMEM,) * len(outs),
        scratch_shapes=[DMA((2,)), DMA((1,)), DMA((3,)), DMA((3,)), DMA((3, blocks)), DMA((3, blocks)), DMA((1,))],
        compiler_params=pltpu.CompilerParams(
            collective_id=0, has_side_effects=True, vmem_limit_bytes=LIMIT
        ),
        name="forward",
    )(lengths, tokens, gain, bias, w_attn, w_out)


GELU_ROOT = 0.7978845608028654
GELU_CUBE = 0.044715


def bit_reverse(value, bits):
    return sum(((value >> at) & 1) << (bits - 1 - at) for at in range(bits))


def groups_of_eight(x):
    return jnp.sum(x.reshape(x.shape[0] // 8, 8, x.shape[1]), axis=0)


class Sum:
    def __init__(self, source, pair, other, result, send, recv):
        self.refs = source, pair, other, result
        self.send, self.recv = send, recv
        mine = lax.axis_index("tensor")
        self.core = mine & 1
        self.twin, self.across = {"tensor": mine ^ 1}, {"tensor": mine ^ 2}

    def half(self, chunk, core):
        return pl.ds(pl.multiple_of(chunk * CHUNK + core * BLOCK, BLOCK), BLOCK)

    def copy(self, stage, chunk):
        source, pair, other, result = self.refs
        own, theirs = self.half(chunk, self.core), self.half(chunk, 1 - self.core)
        src, dst, peer = (
            (source.at[theirs], pair.at[chunk], self.twin),
            (pair.at[chunk], other.at[chunk], self.across),
            (result.at[own], result.at[own], self.twin),
        )[stage]
        return remote(src, dst, self.send.at[stage, chunk], self.recv.at[stage, chunk], peer)

    def first(self, chunk):
        self.copy(0, chunk).start()

    def second(self, chunk):
        source, pair, other, result = self.refs
        self.copy(0, chunk).wait_recv()
        own = source[self.half(chunk, self.core), :].astype(F32)
        pair[chunk] = (own + pair[chunk].astype(F32)).astype(BF16)
        self.copy(1, chunk).start()

    def third(self, chunk):
        source, pair, other, result = self.refs
        self.copy(1, chunk).wait_recv()
        total = pair[chunk].astype(F32) + other[chunk].astype(F32)
        result[self.half(chunk, self.core), :] = total.astype(BF16)
        self.copy(2, chunk).start()

    def ready(self, chunk):
        self.copy(2, chunk).wait_recv()

    def drain(self, chunks):
        def one(chunk, carry):
            for stage in range(3):
                self.copy(stage, chunk).wait_send()
            return carry

        lax.fori_loop(0, chunks, one, 0)


class Scatter:
    def __init__(self, start, lands, send, recv):
        self.refs = (start, *lands)
        self.send, self.recv = send, recv
        self.parts = start.shape[0]
        self.me = lax.axis_index("dp")

    def copy(self, level):
        size = self.parts >> (level + 1)
        bit = (self.me >> level) & 1
        return remote(
            self.refs[level].at[pl.ds((1 - bit) * size, size)],
            self.refs[level + 1],
            self.send.at[level],
            self.recv.at[level],
            {"dp": self.me ^ (1 << level)},
        )

    def go(self, level):
        self.copy(level).start()

    def add(self, level):
        size = self.parts >> (level + 1)
        bit = (self.me >> level) & 1
        here, landed = self.refs[level], self.refs[level + 1]
        self.copy(level).wait_recv()

        def one(part, carry):
            total = here[bit * size + part].astype(F32) + landed[part].astype(F32)
            landed[part] = total.astype(landed.dtype)
            return carry

        lax.fori_loop(0, size, one, 0)

    def drain(self):
        for level in range(len(self.refs) - 1):
            self.copy(level).wait_send()


def backward_kernel(
    pieces, levels,
    lengths, tokens, gain_one, gain_two, bias_two, w_attn, w_up, w_down, cotangent,
    act, query, key, value, query0, key0, probs, selected, mixed, w_out_all, w_zero,
    out_delta, grad_in, out_attn, out_out, out_up, out_down, out_gains,
    hidden_one, act_two, hidden, grad_pre, grad_branch, grad_mixed,
    feed_s, feed_a, feed_b, two_s, two_a, two_b, two_r, one_s, one_a, one_b, one_r,
    grad_key, grad_value, grad_sel, grad_key0, grad_proj, gain_sum, grad_query0,
    exchange, *rest,
):
    seq, width = tokens.shape
    local = w_attn.shape[2]
    heads = local // HEAD
    blocks, chunks = seq // BLOCK, seq // CHUNK
    parts = 1 << levels
    own_rows = width // parts
    rest = list(rest)
    take = lambda count: [rest.pop(0) for _ in range(count)]
    mlp_refs, attn_refs, gain_refs = take(levels + 1), take(levels + 1), take(levels + 1)
    sums_send, sums_recv, scat_send, scat_recv, ex_send, ex_recv = take(6)
    mine = lax.axis_index("tensor")
    me = lax.axis_index("dp")
    peers = [{"tensor": mine ^ step} for step in (1, 2, 3)]
    greet(tuple(peers) + tuple({"dp": me ^ (1 << level)} for level in range(levels)))

    feed = Sum(feed_s, feed_a, feed_b, out_delta, sums_send.at[0], sums_recv.at[0])
    two = Sum(two_s, two_a, two_b, two_r, sums_send.at[1], sums_recv.at[1])
    one = Sum(one_s, one_a, one_b, one_r, sums_send.at[2], sums_recv.at[2])
    mlp = Scatter(mlp_refs[0], mlp_refs[1:], scat_send.at[0], scat_recv.at[0])
    attn = Scatter(attn_refs[0], attn_refs[1:], scat_send.at[1], scat_recv.at[1])
    gains = Scatter(gain_refs[0], gain_refs[1:], scat_send.at[2], scat_recv.at[2])

    for ref in (grad_key, grad_value, grad_sel, grad_key0):
        ref[...] = jnp.zeros(ref.shape, ref.dtype)
    gain_sum[...] = jnp.zeros(gain_sum.shape, F32)

    def feed_forward(step, carry):
        chunk = chunks - 1 - step
        rows = rows_at(chunk, CHUNK)
        branch = sum(dot(mixed[shard, rows, :], w_out_all[shard]) for shard in range(mixed.shape[0]))
        after = tokens[rows, :].astype(F32) + branch
        hidden_one[rows, :] = after
        center, scale = norm_stats(after)
        low = (center * scale * gain_two[...] + bias_two[...]).astype(BF16)
        act_two[rows, :] = low
        up = dot(low, w_up[...])
        square = up * up
        bent = jnp.tanh(GELU_ROOT * (up + GELU_CUBE * (square * up)))
        units = (0.5 * up * (1.0 + bent)).astype(BF16)
        hidden[rows, :] = units
        slope = 0.5 * (1.0 + bent) + (0.5 * GELU_ROOT) * up * (1.0 - bent * bent) * (
            1.0 + (3.0 * GELU_CUBE) * square
        )
        low_cot = cotangent[rows, :].astype(BF16)
        before = (dot_nt(low_cot, w_down[...]) * slope).astype(BF16)
        grad_pre[rows, :] = before
        two_s[rows, :] = dot_nt(before, w_up[...]).astype(BF16)
        two.first(chunk)
        feed_s[rows, :] = (dot(units, w_down[...]) + branch * (1.0 / mixed.shape[0])).astype(BF16)
        feed.first(chunk)

        @pl.when(step > 0)
        def _():
            two.second(chunk + 1)

        return carry

    lax.fori_loop(0, chunks, feed_forward, 0)
    two.second(0)

    def spread(target, columns, found, offset):
        for at in range(found.shape[0] // own_rows):
            part = bit_reverse(offset // own_rows + at, levels)
            target[part, :, columns[0]:columns[1]] = found[at * own_rows:(at + 1) * own_rows].astype(BF16)

    half = width // 2
    for strip in range(2):
        cut = slice(strip * half, (strip + 1) * half)
        spread(mlp_refs[0], (0, w_up.shape[1]), dot_tn(act_two[:, cut], grad_pre[...]), strip * half)
        spread(
            mlp_refs[0], (w_up.shape[1], 2 * w_up.shape[1]),
            dot_tn(cotangent[:, cut].astype(BF16), hidden[...]), strip * half,
        )
    mlp.go(0)

    row = lax.broadcasted_iota(jnp.int32, (BLOCK, 1), 0)
    across_row = lax.broadcasted_iota(jnp.int32, (1, BLOCK), 1)
    down_band = lax.broadcasted_iota(jnp.int32, (BAND, 1), 0) - PAD
    lane = lax.broadcasted_iota(jnp.int32, (1, local), 1)
    here = [(lane >= head * HEAD) & (lane < (head + 1) * HEAD) for head in range(heads)]
    lane0 = lax.broadcasted_iota(jnp.int32, (1, BLOCK), 1)

    def pick(found):
        total = found[-1]
        for head in range(heads - 1):
            total = jnp.where(here[head], found[head], total)
        return total

    def attend_back(block):
        rows = rows_at(block, BLOCK)
        band = pl.ds(rows.start, BAND)
        first, _ = first_of(across_row + block * BLOCK, lengths, pieces)
        first = first - block * BLOCK
        carried = ((down_band >= first) & (down_band < across_row)).astype(BF16)
        grads = grad_mixed[rows, :]
        wide = grads.astype(F32)
        queries, keys, values = query[rows, :], key[band, :], value[band, :]
        loss = jnp.zeros((BLOCK, BAND), F32)
        queried, keyed, valued = [], [], []
        for head in range(heads):
            low = probs[block, head]
            chance = low.astype(F32)
            grad = dot_nt((wide * here[head].astype(F32)).astype(BF16), values)
            inner = jnp.sum(chance * grad, axis=-1, keepdims=True)
            logits = chance * (grad - inner)
            loss = loss - logits
            logits = logits.astype(BF16)
            queried.append(dot(logits, keys))
            keyed.append(dot_tn(logits, queries))
            valued.append(dot_tn(low, grads))
        grad_key[band, :] = grad_key[band, :] + pick(keyed)
        grad_value[band, :] = grad_value[band, :] + pick(valued)
        loss = loss.astype(BF16)
        for part in range(BAND // BLOCK):
            reach = (part + 1) * BLOCK
            rows_k = pl.ds(pl.multiple_of(rows.start + part * BLOCK, BLOCK), BLOCK)
            grad_sel[rows_k, BAND - reach:] = grad_sel[rows_k, BAND - reach:] + dot(
                carried[part * BLOCK:(part + 1) * BLOCK], loss[:, :reach]
            )
        own = pl.ds(pl.multiple_of(rows.start + PAD, BLOCK), BLOCK)
        score = jnp.where(selected[own, :] > 0, grad_sel[own, :], 0.0).astype(BF16)
        from_key = dot(score, key0[band, :])
        grad_query0[rows, :] = jnp.where(lane0 < HEAD, from_key * SCALING, 0.0).astype(BF16)
        grad_key0[band, :] = grad_key0[band, :] + dot_tn(score, query0[rows, :])
        return (pick(queried) * SCALING).astype(BF16)

    def back(step, carry):
        chunk = chunks - 1 - step
        rows = rows_at(chunk, CHUNK)
        padded = pl.ds(pl.multiple_of(chunk * CHUNK + PAD, CHUNK), CHUNK)
        two.third(chunk)
        center, scale = norm_stats(hidden_one[rows, :])
        unit = center * scale
        two.ready(chunk)
        grad = two_r[rows, :].astype(F32)
        gain_sum[2] = gain_sum[2] + groups_of_eight(grad * unit)
        gain_sum[3] = gain_sum[3] + groups_of_eight(grad)
        e = grad * gain_two[...]
        total = cotangent[rows, :] + scale * (
            e - jnp.mean(e, axis=-1, keepdims=True) - unit * jnp.mean(e * unit, axis=-1, keepdims=True)
        )
        hidden_one[rows, :] = total
        low = total.astype(BF16)
        grad_branch[rows, :] = low
        position = lax.broadcasted_iota(jnp.int32, (CHUNK, 1), 0) + chunk * CHUNK
        _, valid = first_of(position, lengths, pieces)
        grad_mixed[rows, :] = (
            dot_nt(low, w_out_all[mine]).astype(BF16).astype(F32) * valid.astype(F32)
        ).astype(BF16)
        upper = attend_back(2 * chunk + 1)
        lower = attend_back(2 * chunk)
        grad_q = jnp.concatenate([lower, upper], axis=0)
        grad_k = (grad_key[padded, :] * SCALING).astype(BF16)
        grad_v = grad_value[padded, :].astype(BF16)
        grad_q0 = grad_query0[rows, :]
        grad_k0 = grad_key0[padded, :]
        extra = grad_q0.astype(F32) + pltpu.roll(grad_k0, HEAD, 1)
        grad_proj[rows, :] = jnp.concatenate(
            [extra, grad_q.astype(F32), grad_k.astype(F32), grad_v.astype(F32)], axis=1
        ).astype(BF16)
        partial = (
            dot_nt(grad_q, w_attn[0])
            + dot_nt(grad_k, w_attn[1])
            + dot_nt(grad_v, w_attn[2])
            + dot_nt(grad_q0, w_zero[0])
            + dot_nt(grad_k0.astype(BF16), w_zero[1])
        )
        one_s[rows, :] = partial.astype(BF16)
        one.first(chunk)
        center, scale = norm_stats(tokens[rows, :].astype(F32))
        gain_sum[0] = gain_sum[0] + groups_of_eight(partial * (center * scale))
        gain_sum[1] = gain_sum[1] + groups_of_eight(partial)

        @pl.when(step > 0)
        def _():
            one.second(chunk + 1)

        feed.second(chunk)
        return carry

    lax.fori_loop(0, chunks, back, 0)
    one.second(0)

    packed = grad_proj.shape[1]
    for strip in range(2):
        cut = slice(strip * half, (strip + 1) * half)
        spread(attn_refs[0], (0, packed), dot_tn(act[:, cut], grad_proj[...]), strip * half)
        spread(attn_refs[0], (packed, packed + local), dot_tn(grad_branch[:, cut], mixed[mine]), strip * half)
    attn.go(0)
    sums = [jnp.sum(gain_sum[at], axis=0, keepdims=True) for at in range(4)]
    sums = jnp.concatenate(sums[:2] + [found * (1.0 / mixed.shape[0]) for found in sums[2:]], axis=0)
    gain_refs[0][...] = jnp.zeros(gain_refs[0].shape, F32)
    for at in range(parts):
        gain_refs[0][bit_reverse(at, levels), 0:4, 0:own_rows] = sums[:, at * own_rows:(at + 1) * own_rows]
    gains.go(0)

    for level in range(levels):
        for scatter in (mlp, gains, attn):
            scatter.add(level)
            if level < levels - 1:
                scatter.go(level + 1)

    final = attn_refs[-1][0].astype(F32)
    exchange[mine, 0:8, :] = gain_refs[-1][0]
    exchange[mine, 8:8 + own_rows, :] = final[:, 0:BLOCK]

    def ex_copy(step, slot, peer):
        block = exchange.at[slot]
        return remote(block, block, ex_send.at[step], ex_recv.at[step], peer)

    for step, peer in enumerate(peers):
        ex_copy(step, mine, peer).start()

    def finish(step, carry):
        chunk = chunks - 1 - step
        rows = rows_at(chunk, CHUNK)
        one.third(chunk)
        center, scale = norm_stats(tokens[rows, :].astype(F32))
        unit = center * scale
        feed.third(chunk)
        one.ready(chunk)
        e = one_r[rows, :].astype(F32) * gain_one[...]
        grad_in[rows, :] = (
            hidden_one[rows, :]
            + scale
            * (e - jnp.mean(e, axis=-1, keepdims=True) - unit * jnp.mean(e * unit, axis=-1, keepdims=True))
        ).astype(BF16)
        return carry

    lax.fori_loop(0, chunks, finish, 0)

    ending = mlp_refs[-1][0].astype(F32)
    out_up[...] = ending[:, :w_up.shape[1]]
    out_down[...] = ending[:, w_up.shape[1]:]
    out_out[...] = final[:, packed:]
    for step, peer in enumerate(peers):
        ex_copy(step, mine ^ (step + 1), peer).wait_recv()
    total = exchange[0]
    for shard in range(1, mixed.shape[0]):
        total = total + exchange[shard]
    out_gains[...] = total[0:8]
    lead = (mine == 0).astype(F32)
    extra = total[8:8 + own_rows] * lead
    adds = (jnp.where(lane0 < HEAD, extra, 0.0), jnp.where(lane0 < HEAD, pltpu.roll(extra, HEAD, 1), 0.0))
    for at in range(3):
        base = final[:, BLOCK + at * local:BLOCK + (at + 1) * local]
        if at < 2:
            base = jnp.concatenate([base[:, :BLOCK] + adds[at], base[:, BLOCK:]], axis=1)
        out_attn[at] = base

    def settle(chunk, carry):
        feed.ready(chunk)
        return carry

    lax.fori_loop(0, chunks, settle, 0)
    for each in (feed, two, one):
        each.drain(chunks)
    for scatter in (mlp, attn, gains):
        scatter.drain()
    for step, peer in enumerate(peers):
        ex_copy(step, mine, peer).wait_send()


def backward_call(lengths, tokens, gain_one, gain_two, bias_two, w_attn, w_up, w_down, cotangent, saved):
    seq, width = tokens.shape
    local = w_attn.shape[2]
    units = w_up.shape[1]
    parts = lax.axis_size("dp")
    levels = parts.bit_length() - 1
    own_rows = width // parts
    chunks = seq // CHUNK
    shards = lax.axis_size("tensor")
    shape = jax.ShapeDtypeStruct
    packed = BLOCK + 3 * local
    outs = (
        shape((seq, width), BF16),
        shape((seq, width), BF16),
        shape((3, own_rows, local), F32),
        shape((own_rows, local), F32),
        shape((own_rows, units), F32),
        shape((own_rows, units), F32),
        shape((8, BLOCK), F32),
    )

    def scatter(columns, rows, dtype):
        return [
            pltpu.VMEM((max(parts >> level, 1), rows, columns), dtype) for level in range(levels + 1)
        ]

    full = lambda dtype: pltpu.VMEM((seq, width), dtype)
    half = lambda: pltpu.VMEM((chunks, BLOCK, width), BF16)
    high = -(-own_rows // 8) * 8
    scratch = (
        [full(F32), full(BF16), full(BF16), full(BF16), full(BF16), pltpu.VMEM((seq, local), BF16)]
        + [full(BF16), half(), half()]
        + [full(BF16), half(), half(), full(BF16)]
        + [full(BF16), half(), half(), full(BF16)]
        + [pltpu.VMEM((seq + PAD, local), F32)] * 2
        + [pltpu.VMEM((seq + PAD, BAND), F32), pltpu.VMEM((seq + PAD, BLOCK), F32)]
        + [pltpu.VMEM((seq, packed), BF16), pltpu.VMEM((4, 8, width), F32), pltpu.VMEM((seq, BLOCK), BF16)]
        + [pltpu.VMEM((shards, 8 + high, BLOCK), F32)]
        + scatter(2 * units, own_rows, BF16)
        + scatter(packed + local, own_rows, BF16)
        + scatter(BLOCK, 8, F32)
        + [DMA((3, 3, chunks)), DMA((3, 3, chunks)), DMA((3, levels)), DMA((3, levels)), DMA((3,)), DMA((3,))]
    )
    operands = (lengths, tokens, gain_one, gain_two, bias_two, w_attn, w_up, w_down, cotangent, *saved)
    return pl.pallas_call(
        functools.partial(backward_kernel, lengths.shape[1], levels),
        out_shape=outs,
        in_specs=[SMEM] + [VMEM] * (len(operands) - 1),
        out_specs=(VMEM,) * len(outs),
        scratch_shapes=scratch,
        compiler_params=pltpu.CompilerParams(
            collective_id=1, has_side_effects=True, vmem_limit_bytes=LIMIT
        ),
        name="backward",
    )(*operands)


def body(
    tokens, gain_one, bias_one, w_attn, w_out, gain_two, bias_two, w_up, w_down, piece_lengths, cotangent
):
    flat = lambda vector: vector.reshape(1, -1)
    saved = forward_call(tokens, flat(gain_one), flat(bias_one), w_attn, w_out, piece_lengths)
    delta, grad_in, grad_attn, grad_out, grad_up, grad_down, gains = backward_call(
        piece_lengths, tokens, flat(gain_one), flat(gain_two), flat(bias_two), w_attn, w_up, w_down, cotangent, saved
    )
    own = grad_up.shape[0]
    return (
        tokens.astype(F32) + delta.astype(F32),
        grad_in.astype(F32),
        grad_attn,
        grad_out.T,
        grad_up,
        grad_down.T,
        gains[0, :own],
        gains[1, :own],
        gains[2, :own],
        gains[3, :own],
    )


def solution(mesh):
    placed = (
        P("dp", None), P(), P(), P(None, None, "tensor"), P("tensor", None), P(), P(),
        P(None, "tensor"), P("tensor", None), P("dp", None), P("dp", None),
    )
    return jax.shard_map(
        body,
        mesh=mesh,
        in_specs=placed,
        out_specs=(
            P("dp", None), P("dp", None), P(None, "dp", "tensor"), P("tensor", "dp"), P("dp", "tensor"),
            P("tensor", "dp"), P("dp"), P("dp"), P("dp"), P("dp"),
        ),
        check_vma=False,
    )
```

```python
import functools

import jax
import jax.numpy as jnp
from jax import lax
from jax.experimental import pallas as pl
from jax.experimental.pallas import tpu as pltpu
from jax.sharding import PartitionSpec as P

F32 = jnp.float32
BF16 = jnp.bfloat16
MESH = pl.DeviceIdType.MESH
HEAD = 64
EPSILON = 1e-05
BLOCK = 128
BAND = 384
PAD = BAND - BLOCK
CHUNK = 256
SCALING = HEAD ** (-0.5)
NT = (((1,), (1,)), ((), ()))
TN = (((0,), (0,)), ((), ()))


def dot(a, b):
    return jnp.dot(a, b, preferred_element_type=F32)


def dot_nt(a, b):
    return lax.dot_general(a, b, NT, preferred_element_type=F32)


def dot_tn(a, b):
    return lax.dot_general(a, b, TN, preferred_element_type=F32)


def rows_at(index, size):
    return pl.ds(pl.multiple_of(index * size, size), size)


def first_of(position, lengths, pieces):
    first = jnp.zeros_like(position)
    end = jnp.int32(0)
    for piece in range(pieces - 1):
        size = lengths[0, piece]
        end = end + size
        first = jnp.where(position >= end, end, first)
    return first, position < end


def norm_stats(x):
    center = x - jnp.mean(x, axis=-1, keepdims=True)
    spread = jnp.mean(center * center, axis=-1, keepdims=True)
    return center, lax.rsqrt(spread + EPSILON)


def remote(src, dst, send, recv, peer):
    return pltpu.make_async_remote_copy(
        src_ref=src, dst_ref=dst, send_sem=send, recv_sem=recv, device_id=peer, device_id_type=MESH
    )


def greet(peers):
    barrier = pltpu.get_barrier_semaphore()
    for peer in peers:
        pl.semaphore_signal(barrier, inc=1, device_id=peer, device_id_type=MESH)
    pl.semaphore_wait(barrier, len(peers))


GELU_ROOT = 0.7978845608028654
GELU_CUBE = 0.044715


def bit_reverse(value, bits):
    return sum(((value >> at) & 1) << (bits - 1 - at) for at in range(bits))


def groups_of_eight(x):
    return jnp.sum(x.reshape(x.shape[0] // 8, 8, x.shape[1]), axis=0)


class Sum:
    def __init__(self, source, pair, other, result, send, recv):
        self.refs = source, pair, other, result
        self.send, self.recv = send, recv
        mine = lax.axis_index("tensor")
        self.core = mine & 1
        self.twin, self.across = {"tensor": mine ^ 1}, {"tensor": mine ^ 2}

    def half(self, chunk, core):
        return pl.ds(pl.multiple_of(chunk * CHUNK + core * BLOCK, BLOCK), BLOCK)

    def copy(self, stage, chunk):
        source, pair, other, result = self.refs
        own, theirs = self.half(chunk, self.core), self.half(chunk, 1 - self.core)
        src, dst, peer = (
            (source.at[theirs], pair.at[chunk], self.twin),
            (pair.at[chunk], other.at[chunk], self.across),
            (result.at[own], result.at[own], self.twin),
        )[stage]
        return remote(src, dst, self.send.at[stage, chunk], self.recv.at[stage, chunk], peer)

    def first(self, chunk):
        self.copy(0, chunk).start()

    def second(self, chunk):
        source, pair, other, result = self.refs
        self.copy(0, chunk).wait_recv()
        own = source[self.half(chunk, self.core), :].astype(F32)
        pair[chunk] = (own + pair[chunk].astype(F32)).astype(BF16)
        self.copy(1, chunk).start()

    def third(self, chunk):
        source, pair, other, result = self.refs
        self.copy(1, chunk).wait_recv()
        self.copy(1, chunk).wait_send()
        total = pair[chunk].astype(F32) + other[chunk].astype(F32)
        result[self.half(chunk, self.core), :] = total.astype(BF16)
        self.copy(2, chunk).start()

    def ready(self, chunk):
        self.copy(2, chunk).wait_recv()

    def sent(self, chunk, *stages):
        for stage in stages:
            self.copy(stage, chunk).wait_send()


class Scatter:
    def __init__(self, start, lands, send, recv):
        self.refs = (start, *lands)
        self.send, self.recv = send, recv
        self.parts = start.shape[0]
        self.me = lax.axis_index("dp")

    def copy(self, level):
        size = self.parts >> (level + 1)
        bit = (self.me >> level) & 1
        return remote(
            self.refs[level].at[pl.ds((1 - bit) * size, size)],
            self.refs[level + 1],
            self.send.at[level],
            self.recv.at[level],
            {"dp": self.me ^ (1 << level)},
        )

    def go(self, level):
        self.copy(level).start()

    def add(self, level):
        size = self.parts >> (level + 1)
        bit = (self.me >> level) & 1
        here, landed = self.refs[level], self.refs[level + 1]
        self.copy(level).wait_recv()

        def one(part, carry):
            total = here[bit * size + part].astype(F32) + landed[part].astype(F32)
            landed[part] = total.astype(landed.dtype)
            return carry

        lax.fori_loop(0, size, one, 0)

    def drain(self):
        for level in range(len(self.refs) - 1):
            self.copy(level).wait_send()


def layer_kernel(
    pieces, levels,
    lengths, gain_one, bias_one, gain_two, bias_two,
    tokens_hbm, w_attn_hbm, w_out_hbm, w_up_hbm, w_down_hbm, cotangent_hbm,
    out_delta, grad_in, out_attn, out_out, out_up, out_down, out_gains,
    tokens, w_attn, w_out_all, w_zero, w_up, w_down, cotangent,
    act, query, key, value, query0, key0, probs, selected, mixed,
    stacks, scores, chances, offsets, lost,
    hidden_one, act_two, hidden, grad_pre, grad_mixed,
    feed_s, feed_a, feed_b, two_s, two_a, two_b, one_b,
    grad_key, grad_value, grad_sel, grad_key0, grad_proj, gain_sum, grad_query0,
    exchange, *rest,
):
    seq, width = tokens.shape
    local = w_attn.shape[1]
    heads = local // HEAD
    blocks, chunks = seq // BLOCK, seq // CHUNK
    shards = mixed.shape[0]
    parts = 1 << levels
    own_rows = width // parts
    rest = list(rest)
    take = lambda count: [rest.pop(0) for _ in range(count)]
    mlp_refs, attn_refs, gain_refs = take(levels + 1), take(levels + 1), take(levels + 1)
    zero_send, zero_recv, out_send, out_recv, mix_send, mix_recv = take(6)
    sums_send, sums_recv, scat_send, scat_recv, ex_send, ex_recv, load_sem, tokens_sem = take(8)
    mine = lax.axis_index("tensor")
    me = lax.axis_index("dp")
    twin = {"tensor": mine ^ 1}
    across = {"tensor": mine ^ 2}
    peers = [{"tensor": mine ^ step} for step in (1, 2, 3)]

    loads = [
        pltpu.make_async_copy(source, target, load_sem.at[at])
        for at, (source, target) in enumerate((
            (w_attn_hbm, w_attn), (w_out_hbm, w_out_all.at[mine]),
            (w_up_hbm, w_up), (w_down_hbm, w_down), (cotangent_hbm, cotangent),
        ))
    ]
    attn_load, out_load, up_load, down_load, cot_load = loads

    def token_load(chunk):
        rows = rows_at(chunk, CHUNK)
        return pltpu.make_async_copy(tokens_hbm.at[rows], tokens.at[rows], tokens_sem.at[chunk])

    out_load.start()
    token_load(0).start()
    attn_load.start()
    for chunk in range(1, chunks):
        token_load(chunk).start()
    greet(tuple(peers) + tuple({"dp": me ^ (1 << level)} for level in range(levels)))
    for load in loads[2:]:
        load.start()

    def out_copy(stage, slot, peer):
        block = w_out_all.at[slot]
        return remote(block, block, out_send.at[stage], out_recv.at[stage], peer)

    def zero_copy(stage, peer, source):
        return remote(source, w_zero, zero_send.at[stage], zero_recv.at[0], peer)

    head_rows = w_attn.at[pl.ds(0, 2), pl.ds(0, BLOCK)]
    out_load.wait()
    out_copy(1, mine, twin).start()
    attn_load.wait()

    @pl.when(mine == 0)
    def _():
        zero_copy(0, across, head_rows).start()
        zero_copy(1, twin, head_rows).start()
        w_zero[...] = w_attn[0:2, 0:BLOCK]

    out_copy(0, mine, across).start()

    lane = lax.broadcasted_iota(jnp.int32, (1, local), 1)
    here = [(lane >= head * HEAD) & (lane < (head + 1) * HEAD) for head in range(heads)]
    lane0 = lax.broadcasted_iota(jnp.int32, (1, BLOCK), 1)
    row = lax.broadcasted_iota(jnp.int32, (BLOCK, 1), 0)
    column = lax.broadcasted_iota(jnp.int32, (1, BAND), 1) - PAD
    for ref in (key, value, key0, selected):
        ref[0:PAD, :] = jnp.zeros((PAD, ref.shape[1]), ref.dtype)
    for ref in (grad_key, grad_value, grad_sel, grad_key0):
        ref[...] = jnp.zeros(ref.shape, ref.dtype)
    gain_sum[...] = jnp.zeros(gain_sum.shape, F32)

    def pick(found):
        total = found[(heads - 1) * BLOCK:]
        for head in range(heads - 1):
            total = jnp.where(here[head], found[head * BLOCK:(head + 1) * BLOCK], total)
        return total

    def stack(target, wide, scale):
        for head in range(heads):
            target[head * BLOCK:(head + 1) * BLOCK, :] = jnp.where(here[head], wide * scale, 0.0).astype(BF16)

    def project(step, carry):
        rows = rows_at(step, CHUNK)
        padded = pl.ds(pl.multiple_of(step * CHUNK + PAD, CHUNK), CHUNK)
        token_load(step).wait()
        center, scale = norm_stats(tokens[rows, :].astype(F32))
        low = (center * scale * gain_one[...] + bias_one[...]).astype(BF16)
        act[rows, :] = low
        query[rows, :] = dot_nt(low, w_attn[0]).astype(BF16)
        key[padded, :] = dot_nt(low, w_attn[1]).astype(BF16)
        value[padded, :] = dot_nt(low, w_attn[2]).astype(BF16)
        return carry

    lax.fori_loop(0, chunks, project, 0)

    @pl.when(mine != 0)
    def _():
        zero_copy(0, twin, w_zero).wait_recv()

    @pl.when(mine == 2)
    def _():
        zero_copy(0, twin, w_zero).start()

    keep0 = jnp.where(lane0 < HEAD, SCALING, 0.0)

    def project0(step, carry):
        rows = rows_at(step, CHUNK)
        padded = pl.ds(pl.multiple_of(step * CHUNK + PAD, CHUNK), CHUNK)
        low = act[rows, :]
        found = dot_nt(low, w_zero[0]).astype(BF16).astype(F32)
        query0[rows, :] = (found * keep0).astype(BF16)
        key0[padded, :] = dot_nt(low, w_zero[1]).astype(BF16)
        return carry

    lax.fori_loop(0, chunks, project0, 0)

    def select(block, carry):
        rows = rows_at(block, BLOCK)
        first, _ = first_of(row + block * BLOCK, lengths, pieces)
        first = first - block * BLOCK
        score = dot_nt(query0[rows, :], key0[pl.ds(rows.start, BAND), :])
        keep = (column > first) & (column < row)
        own = pl.ds(pl.multiple_of(rows.start + PAD, BLOCK), BLOCK)
        selected[own, :] = jnp.where(keep, jnp.maximum(score, 0.0), 0.0).astype(BF16)
        return carry

    lax.fori_loop(0, blocks, select, 0)

    def mix_copy(stage, slot, block, peer):
        part = mixed.at[slot, rows_at(block, BLOCK)]
        return remote(part, part, mix_send.at[stage, block], mix_recv.at[stage, block], peer)

    GROUP = 32
    places = BAND // BLOCK

    def attend_block(block, lot):
        rows = rows_at(block, BLOCK)
        band = rows.start
        first, valid = first_of(row + block * BLOCK, lengths, pieces)
        first = first - block * BLOCK
        inside = column >= first
        carried = (inside & (column < row)).astype(BF16)
        found = [
            dot(
                carried[:, part * BLOCK:(part + 1) * BLOCK],
                selected[pl.ds(pl.multiple_of(band + part * BLOCK, BLOCK), BLOCK), BAND - (part + 1) * BLOCK:],
            )
            for part in range(places)
        ]
        for at in range(places):
            cut = slice(at * BLOCK, (at + 1) * BLOCK)
            penalty = sum(found[part][:, cut] for part in range(at, places))
            offsets[lot, :, cut] = jnp.where((inside & (column <= row))[:, cut], -penalty, -1e30)
        stack(stacks.at[lot], query[rows, :].astype(F32), SCALING)
        scores[lot] = dot_nt(stacks[lot], key[pl.ds(band, BAND), :])
        for group in range(heads * BLOCK // GROUP):
            cut = slice(group * GROUP, (group + 1) * GROUP)
            at = group * GROUP % BLOCK
            logits = scores[lot, cut, :] + offsets[lot, at:at + GROUP, :]
            raised = jnp.exp(logits - jnp.max(logits, axis=-1, keepdims=True))
            chances[lot, cut, :] = (raised * (1.0 / jnp.sum(raised, axis=-1, keepdims=True))).astype(BF16)
        low = chances[lot]
        total = pick(dot(low, value[pl.ds(band, BAND), :]))
        return low, (total * valid.astype(F32)).astype(BF16)

    def attend(step, carry):
        chunk = chunks - 1 - step
        done = [attend_block(2 * chunk + lot, lot) for lot in range(2)]
        for lot in (1, 0):
            block = 2 * chunk + lot
            probs[block] = done[lot][0]
            mixed[mine, rows_at(block, BLOCK), :] = done[lot][1]
            mix_copy(0, mine, block, across).start()
            mix_copy(1, mine, block, twin).start()
        return carry

    lax.fori_loop(0, chunks, attend, 0)

    out_copy(0, mine ^ 2, across).wait_recv()
    out_copy(2, mine ^ 2, twin).start()

    def relay(chunk):
        for lot in (1, 0):
            block = 2 * chunk + lot
            mix_copy(0, mine ^ 2, block, across).wait_recv()
            mix_copy(2, mine ^ 2, block, twin).start()

    relay(chunks - 1)
    out_copy(1, mine ^ 1, twin).wait_recv()
    out_copy(2, mine ^ 3, twin).wait_recv()
    for load in loads[2:]:
        load.wait()

    feed = Sum(feed_s, feed_a, feed_b, out_delta, sums_send.at[0], sums_recv.at[0])
    two = Sum(two_s, two_a, two_b, grad_in, sums_send.at[1], sums_recv.at[1])
    one = Sum(two_s, two_a, one_b, grad_in, sums_send.at[2], sums_recv.at[2])
    mlp = Scatter(mlp_refs[0], mlp_refs[1:], scat_send.at[0], scat_recv.at[0])
    attn = Scatter(attn_refs[0], attn_refs[1:], scat_send.at[1], scat_recv.at[1])
    gains = Scatter(gain_refs[0], gain_refs[1:], scat_send.at[2], scat_recv.at[2])

    def feed_forward(step, carry):
        chunk = chunks - 1 - step
        rows = rows_at(chunk, CHUNK)

        @pl.when(chunk > 0)
        def _():
            relay(chunk - 1)

        for lot in (1, 0):
            block = 2 * chunk + lot
            mix_copy(1, mine ^ 1, block, twin).wait_recv()
            mix_copy(2, mine ^ 3, block, twin).wait_recv()
        branch = sum(dot(mixed[shard, rows, :], w_out_all[shard]) for shard in range(shards))
        after = tokens[rows, :].astype(F32) + branch
        hidden_one[rows, :] = after
        center, scale = norm_stats(after)
        low = (center * scale * gain_two[...] + bias_two[...]).astype(BF16)
        act_two[rows, :] = low
        up = dot(low, w_up[...])
        square = up * up
        bent = jnp.tanh(GELU_ROOT * (up + GELU_CUBE * (square * up)))
        units = (0.5 * up * (1.0 + bent)).astype(BF16)
        hidden[rows, :] = units
        slope = 0.5 * (1.0 + bent) + (0.5 * GELU_ROOT) * up * (1.0 - bent * bent) * (
            1.0 + (3.0 * GELU_CUBE) * square
        )
        before = (dot_nt(cotangent[rows, :].astype(BF16), w_down[...]) * slope).astype(BF16)
        grad_pre[rows, :] = before
        two_s[rows, :] = dot_nt(before, w_up[...]).astype(BF16)
        two.first(chunk)
        feed_s[rows, :] = (dot(units, w_down[...]) + branch * (1.0 / shards)).astype(BF16)
        feed.first(chunk)
        two.second(chunk)
        return carry

    lax.fori_loop(0, chunks, feed_forward, 0)

    def spread(target, columns, found, offset):
        for at in range(found.shape[0] // own_rows):
            part = bit_reverse(offset // own_rows + at, levels)
            target[part, :, columns[0]:columns[1]] = found[at * own_rows:(at + 1) * own_rows].astype(BF16)

    half = width // 2
    units = w_up.shape[1]
    for strip in range(2):
        cut = slice(strip * half, (strip + 1) * half)
        spread(mlp_refs[0], (0, units), dot_tn(act_two[:, cut], grad_pre[...]), strip * half)
        spread(mlp_refs[0], (units, 2 * units), dot_tn(cotangent[:, cut].astype(BF16), hidden[...]), strip * half)
    mlp.go(0)

    across_row = lax.broadcasted_iota(jnp.int32, (1, BLOCK), 1)
    down_band = lax.broadcasted_iota(jnp.int32, (BAND, 1), 0) - PAD

    def attend_back(block, lot):
        rows = rows_at(block, BLOCK)
        band = pl.ds(rows.start, BAND)
        first, _ = first_of(across_row + block * BLOCK, lengths, pieces)
        first = first - block * BLOCK
        carried = ((down_band >= first) & (down_band < across_row)).astype(BF16)
        stack(stacks.at[lot], grad_mixed[rows, :].astype(F32), 1.0)
        stack(stacks.at[2 + lot], query[rows, :].astype(F32), SCALING)
        scores[lot] = dot_nt(stacks[lot], value[band, :])
        for group in range(BLOCK // GROUP):
            loss = jnp.zeros((GROUP, BAND), F32)
            for head in range(heads):
                cut = slice(head * BLOCK + group * GROUP, head * BLOCK + (group + 1) * GROUP)
                chance = probs[block, cut, :].astype(F32)
                grad = scores[lot, cut, :]
                weighed = chance * grad
                logits = weighed - chance * jnp.sum(weighed, axis=-1, keepdims=True)
                loss = loss - logits
                chances[lot, cut, :] = logits.astype(BF16)
            lost[lot, group * GROUP:(group + 1) * GROUP, :] = loss.astype(BF16)
        logits = chances[lot]
        queried = pick(dot(logits, key[band, :]))
        keyed = dot_tn(logits, stacks[2 + lot])
        valued = dot_tn(probs[block], stacks[lot])
        selects = [
            dot(carried[part * BLOCK:(part + 1) * BLOCK], lost[lot, :, :(part + 1) * BLOCK])
            for part in range(places)
        ]
        return (queried * SCALING).astype(BF16), keyed, valued, selects

    def attend_add(block, lot, keyed, valued, selects):
        rows = rows_at(block, BLOCK)
        band = pl.ds(rows.start, BAND)
        grad_key[band, :] = grad_key[band, :] + keyed
        grad_value[band, :] = grad_value[band, :] + valued
        for part in range(places):
            reach = (part + 1) * BLOCK
            rows_k = pl.ds(pl.multiple_of(rows.start + part * BLOCK, BLOCK), BLOCK)
            grad_sel[rows_k, BAND - reach:] = grad_sel[rows_k, BAND - reach:] + selects[part]
        own = pl.ds(pl.multiple_of(rows.start + PAD, BLOCK), BLOCK)
        score = jnp.where(selected[own, :] > 0, grad_sel[own, :], 0.0).astype(BF16)
        from_key = dot(score, key0[band, :])
        grad_query0[rows, :] = jnp.where(lane0 < HEAD, from_key * SCALING, 0.0).astype(BF16)
        grad_key0[band, :] = grad_key0[band, :] + dot_tn(score, query0[rows, :])

    def back(step, carry):
        chunk = chunks - 1 - step
        rows = rows_at(chunk, CHUNK)
        padded = pl.ds(pl.multiple_of(chunk * CHUNK + PAD, CHUNK), CHUNK)
        two.third(chunk)
        center, scale = norm_stats(hidden_one[rows, :])
        unit = center * scale
        two.ready(chunk)
        grad = grad_in[rows, :].astype(F32)
        gain_sum[2] = gain_sum[2] + groups_of_eight(grad * unit)
        gain_sum[3] = gain_sum[3] + groups_of_eight(grad)
        e = grad * gain_two[...]
        total = cotangent[rows, :] + scale * (
            e - jnp.mean(e, axis=-1, keepdims=True) - unit * jnp.mean(e * unit, axis=-1, keepdims=True)
        )
        hidden_one[rows, :] = total
        position = lax.broadcasted_iota(jnp.int32, (CHUNK, 1), 0) + chunk * CHUNK
        _, valid = first_of(position, lengths, pieces)
        grad_mixed[rows, :] = (
            dot_nt(total.astype(BF16), w_out_all[mine]).astype(BF16).astype(F32) * valid.astype(F32)
        ).astype(BF16)
        upper, *upper_adds = attend_back(2 * chunk + 1, 1)
        lower, *lower_adds = attend_back(2 * chunk, 0)
        attend_add(2 * chunk + 1, 1, *upper_adds)
        attend_add(2 * chunk, 0, *lower_adds)
        grad_q = jnp.concatenate([lower, upper], axis=0)
        grad_k = grad_key[padded, :].astype(BF16)
        grad_v = grad_value[padded, :].astype(BF16)
        grad_q0 = grad_query0[rows, :]
        grad_k0 = grad_key0[padded, :]
        extra = grad_q0.astype(F32) + pltpu.roll(grad_k0, HEAD, 1)
        grad_proj[rows, :] = jnp.concatenate(
            [extra, grad_q.astype(F32), grad_k.astype(F32), grad_v.astype(F32)], axis=1
        ).astype(BF16)
        partial = (
            dot(grad_q, w_attn[0])
            + dot(grad_k, w_attn[1])
            + dot(grad_v, w_attn[2])
            + dot(grad_q0, w_zero[0])
            + dot(grad_k0.astype(BF16), w_zero[1])
        )
        two.sent(chunk, 0, 2)
        two_s[rows, :] = partial.astype(BF16)
        one.first(chunk)
        center, scale = norm_stats(tokens[rows, :].astype(F32))
        gain_sum[0] = gain_sum[0] + groups_of_eight(partial * (center * scale))
        gain_sum[1] = gain_sum[1] + groups_of_eight(partial)
        one.second(chunk)
        feed.second(chunk)
        return carry

    lax.fori_loop(0, chunks, back, 0)

    packed = grad_proj.shape[1]
    for strip in range(2):
        cut = slice(strip * half, (strip + 1) * half)
        spread(attn_refs[0], (0, packed), dot_tn(act[:, cut], grad_proj[...]), strip * half)
        spread(
            attn_refs[0], (packed, packed + local),
            dot_tn(hidden_one[:, cut].astype(BF16), mixed[mine]), strip * half,
        )
    attn.go(0)
    sums = [jnp.sum(gain_sum[at], axis=0, keepdims=True) for at in range(4)]
    sums = jnp.concatenate(sums[:2] + [found * (1.0 / shards) for found in sums[2:]], axis=0)
    gain_refs[0][...] = jnp.zeros(gain_refs[0].shape, F32)
    for at in range(parts):
        gain_refs[0][bit_reverse(at, levels), 0:4, 0:own_rows] = sums[:, at * own_rows:(at + 1) * own_rows]
    gains.go(0)

    for level in range(levels):
        for scatter in (mlp, gains, attn):
            scatter.add(level)
            if level < levels - 1:
                scatter.go(level + 1)

    final = attn_refs[-1][0].astype(F32)
    exchange[mine, 0:8, :] = gain_refs[-1][0]
    exchange[mine, 8:8 + own_rows, :] = final[:, 0:BLOCK]

    def ex_copy(step, slot, peer):
        block = exchange.at[slot]
        return remote(block, block, ex_send.at[step], ex_recv.at[step], peer)

    for step, peer in enumerate(peers):
        ex_copy(step, mine, peer).start()

    def finish(step, carry):
        chunk = chunks - 1 - step
        rows = rows_at(chunk, CHUNK)
        one.third(chunk)
        center, scale = norm_stats(tokens[rows, :].astype(F32))
        unit = center * scale
        feed.third(chunk)
        one.ready(chunk)
        e = grad_in[rows, :].astype(F32) * gain_one[...]
        found = (
            hidden_one[rows, :]
            + scale
            * (e - jnp.mean(e, axis=-1, keepdims=True) - unit * jnp.mean(e * unit, axis=-1, keepdims=True))
        ).astype(BF16)
        one.sent(chunk, 2)
        grad_in[rows, :] = found
        return carry

    lax.fori_loop(0, chunks, finish, 0)

    ending = mlp_refs[-1][0].astype(F32)
    out_up[...] = ending[:, :units]
    out_down[...] = ending[:, units:]
    out_out[...] = final[:, packed:]
    for step, peer in enumerate(peers):
        ex_copy(step, mine ^ (step + 1), peer).wait_recv()
    total = exchange[0]
    for shard in range(1, shards):
        total = total + exchange[shard]
    out_gains[...] = total[0:8]
    lead = (mine == 0).astype(F32)
    extra = total[8:8 + own_rows] * lead
    adds = (jnp.where(lane0 < HEAD, extra, 0.0), jnp.where(lane0 < HEAD, pltpu.roll(extra, HEAD, 1), 0.0))
    for at in range(3):
        base = final[:, BLOCK + at * local:BLOCK + (at + 1) * local]
        if at < 2:
            base = jnp.concatenate([base[:, :BLOCK] + adds[at], base[:, BLOCK:]], axis=1)
        out_attn[at] = base

    def settle(chunk, carry):
        feed.ready(chunk)
        feed.sent(chunk, 0, 2)
        one.sent(chunk, 0)
        for lot in range(2):
            block = 2 * chunk + lot
            mix_copy(0, mine, block, across).wait_send()
            mix_copy(1, mine, block, twin).wait_send()
            mix_copy(2, mine ^ 2, block, twin).wait_send()
        return carry

    lax.fori_loop(0, chunks, settle, 0)
    for scatter in (mlp, attn, gains):
        scatter.drain()
    for step, peer in enumerate(peers):
        ex_copy(step, mine, peer).wait_send()
    out_copy(0, mine, across).wait_send()
    out_copy(1, mine, twin).wait_send()
    out_copy(2, mine ^ 2, twin).wait_send()

    @pl.when(mine == 0)
    def _():
        zero_copy(0, across, head_rows).wait_send()
        zero_copy(1, twin, head_rows).wait_send()

    @pl.when(mine == 2)
    def _():
        zero_copy(0, twin, w_zero).wait_send()


VMEM = pl.BlockSpec(memory_space=pltpu.VMEM)
SMEM = pl.BlockSpec(memory_space=pltpu.SMEM)
ANY = pl.BlockSpec(memory_space=pl.ANY)
DMA = pltpu.SemaphoreType.DMA
LIMIT = 67_000_000


def layer_call(tokens, gain_one, bias_one, w_attn, w_out, gain_two, bias_two, w_up, w_down, lengths, cotangent):
    seq, width = tokens.shape
    local = w_attn.shape[1]
    units = w_up.shape[1]
    heads = local // HEAD
    parts = lax.axis_size("dp")
    levels = parts.bit_length() - 1
    own_rows = width // parts
    blocks, chunks = seq // BLOCK, seq // CHUNK
    shards = lax.axis_size("tensor")
    shape = jax.ShapeDtypeStruct
    packed = BLOCK + 3 * local
    outs = (
        shape((seq, width), BF16),
        shape((seq, width), BF16),
        shape((3, own_rows, local), F32),
        shape((own_rows, local), F32),
        shape((own_rows, units), F32),
        shape((own_rows, units), F32),
        shape((8, BLOCK), F32),
    )

    def scatter(columns, rows, dtype):
        return [
            pltpu.VMEM((max(parts >> level, 1), rows, columns), dtype) for level in range(levels + 1)
        ]

    low = lambda *dims: pltpu.VMEM(dims, BF16)
    wide = lambda *dims: pltpu.VMEM(dims, F32)
    high = -(-own_rows // 8) * 8
    stacked = heads * BLOCK
    scratch = (
        [low(seq, width), low(3, local, width), low(shards, local, width), low(2, BLOCK, width)]
        + [low(width, units), low(units, width), wide(seq, width)]
        + [low(seq, width), low(seq, local), low(seq + PAD, local), low(seq + PAD, local)]
        + [low(seq, BLOCK), low(seq + PAD, BLOCK), low(blocks, stacked, BAND), low(seq + PAD, BAND)]
        + [low(shards, seq, local)]
        + [low(4, stacked, local), wide(2, stacked, BAND), low(2, stacked, BAND), wide(2, BLOCK, BAND), low(2, BLOCK, BAND)]
        + [wide(seq, width), low(seq, width), low(seq, units), low(seq, units), low(seq, local)]
        + [low(seq, width), low(chunks, BLOCK, width), low(chunks, BLOCK, width)]
        + [low(seq, width), low(chunks, BLOCK, width), low(chunks, BLOCK, width), low(chunks, BLOCK, width)]
        + [wide(seq + PAD, local)] * 2
        + [wide(seq + PAD, BAND), wide(seq + PAD, BLOCK)]
        + [low(seq, packed), wide(4, 8, width), low(seq, BLOCK)]
        + [wide(shards, 8 + high, BLOCK)]
        + scatter(2 * units, own_rows, BF16)
        + scatter(packed + local, own_rows, BF16)
        + scatter(BLOCK, 8, F32)
        + [DMA((2,)), DMA((1,)), DMA((3,)), DMA((3,)), DMA((3, blocks)), DMA((3, blocks))]
        + [DMA((3, 3, chunks)), DMA((3, 3, chunks)), DMA((3, levels)), DMA((3, levels)), DMA((3,)), DMA((3,))]
        + [DMA((5,)), DMA((chunks,))]
    )
    operands = (
        lengths, gain_one, bias_one, gain_two, bias_two, tokens, w_attn, w_out, w_up, w_down, cotangent,
    )
    return pl.pallas_call(
        functools.partial(layer_kernel, lengths.shape[1], levels),
        out_shape=outs,
        in_specs=[SMEM] + [VMEM] * 4 + [ANY] * 6,
        out_specs=(VMEM,) * len(outs),
        scratch_shapes=scratch,
        compiler_params=pltpu.CompilerParams(
            collective_id=0, has_side_effects=True, vmem_limit_bytes=LIMIT
        ),
        name="layer",
    )(*operands)


def body(
    tokens, gain_one, bias_one, w_attn, w_out, gain_two, bias_two, w_up, w_down, piece_lengths, cotangent
):
    flat = lambda vector: vector.reshape(1, -1)
    delta, grad_in, grad_attn, grad_out, grad_up, grad_down, gains = layer_call(
        tokens, flat(gain_one), flat(bias_one), jnp.swapaxes(w_attn, 1, 2), w_out, flat(gain_two), flat(bias_two),
        w_up, w_down, piece_lengths, cotangent,
    )
    own = grad_up.shape[0]
    return (
        tokens.astype(F32) + delta.astype(F32),
        grad_in.astype(F32),
        grad_attn,
        grad_out.T,
        grad_up,
        grad_down.T,
        gains[0, :own],
        gains[1, :own],
        gains[2, :own],
        gains[3, :own],
    )


def solution(mesh):
    placed = (
        P("dp", None), P(), P(), P(None, None, "tensor"), P("tensor", None), P(), P(),
        P(None, "tensor"), P("tensor", None), P("dp", None), P("dp", None),
    )
    return jax.shard_map(
        body,
        mesh=mesh,
        in_specs=placed,
        out_specs=(
            P("dp", None), P("dp", None), P(None, "dp", "tensor"), P("tensor", "dp"), P("dp", "tensor"),
            P("tensor", "dp"), P("dp"), P("dp"), P("dp"), P("dp"),
        ),
        check_vma=False,
    )
```

```python
import functools

import jax
import jax.numpy as jnp
from jax import lax
from jax.experimental import pallas as pl
from jax.experimental.pallas import tpu as pltpu
from jax.sharding import PartitionSpec as P

F32 = jnp.float32
BF16 = jnp.bfloat16
MESH = pl.DeviceIdType.MESH
HEAD = 64
EPSILON = 1e-05
BLOCK = 128
BAND = 384
PAD = BAND - BLOCK
CHUNK = 256
SCALING = HEAD ** (-0.5)
NT = (((1,), (1,)), ((), ()))
TN = (((0,), (0,)), ((), ()))


def dot(a, b):
    return jnp.dot(a, b, preferred_element_type=F32)


def dot_nt(a, b):
    return lax.dot_general(a, b, NT, preferred_element_type=F32)


def dot_tn(a, b):
    return lax.dot_general(a, b, TN, preferred_element_type=F32)


def rows_at(index, size):
    return pl.ds(pl.multiple_of(index * size, size), size)


def first_of(position, lengths, pieces):
    first = jnp.zeros_like(position)
    end = jnp.int32(0)
    for piece in range(pieces - 1):
        size = lengths[0, piece]
        end = end + size
        first = jnp.where(position >= end, end, first)
    return first, position < end


def norm_stats(x):
    center = x - jnp.mean(x, axis=-1, keepdims=True)
    spread = jnp.mean(center * center, axis=-1, keepdims=True)
    return center, lax.rsqrt(spread + EPSILON)


def remote(src, dst, send, recv, peer):
    return pltpu.make_async_remote_copy(
        src_ref=src, dst_ref=dst, send_sem=send, recv_sem=recv, device_id=peer, device_id_type=MESH
    )


def greet(peers):
    barrier = pltpu.get_barrier_semaphore()
    for peer in peers:
        pl.semaphore_signal(barrier, inc=1, device_id=peer, device_id_type=MESH)
    pl.semaphore_wait(barrier, len(peers))


GELU_ROOT = 0.7978845608028654
GELU_CUBE = 0.044715


def place(value, order):
    return sum(((value >> bit) & 1) << (len(order) - 1 - at) for at, bit in enumerate(order))


def groups_of_eight(x):
    return jnp.sum(x.reshape(x.shape[0] // 8, 8, x.shape[1]), axis=0)


class Sum:
    def __init__(self, source, pair, other, result, send, recv):
        self.refs = source, pair, other, result
        self.send, self.recv = send, recv
        mine = lax.axis_index("tensor")
        self.core = mine & 1
        self.twin, self.across = {"tensor": mine ^ 1}, {"tensor": mine ^ 2}

    def half(self, chunk, core):
        return pl.ds(pl.multiple_of(chunk * CHUNK + core * BLOCK, BLOCK), BLOCK)

    def copy(self, stage, chunk):
        source, pair, other, result = self.refs
        own, theirs = self.half(chunk, self.core), self.half(chunk, 1 - self.core)
        src, dst, peer = (
            (source.at[theirs], pair.at[chunk], self.twin),
            (pair.at[chunk], other.at[chunk], self.across),
            (result.at[own], result.at[own], self.twin),
        )[stage]
        return remote(src, dst, self.send.at[stage, chunk], self.recv.at[stage, chunk], peer)

    def first(self, chunk):
        self.copy(0, chunk).start()

    def second(self, chunk):
        source, pair, other, result = self.refs
        self.copy(0, chunk).wait_recv()
        own = source[self.half(chunk, self.core), :].astype(F32)
        pair[chunk] = (own + pair[chunk].astype(F32)).astype(BF16)
        self.copy(1, chunk).start()

    def third(self, chunk):
        source, pair, other, result = self.refs
        self.copy(1, chunk).wait_recv()
        self.copy(1, chunk).wait_send()
        total = pair[chunk].astype(F32) + other[chunk].astype(F32)
        result[self.half(chunk, self.core), :] = total.astype(BF16)
        self.copy(2, chunk).start()

    def ready(self, chunk):
        self.copy(2, chunk).wait_recv()

    def sent(self, chunk, *stages):
        for stage in stages:
            self.copy(stage, chunk).wait_send()


class Scatter:
    def __init__(self, refs, order, send, recv):
        self.refs, self.order = refs, order
        self.send, self.recv = send, recv
        self.parts = refs[0].shape[0]
        self.me = lax.axis_index("dp")

    def copy(self, level):
        size = self.parts >> (level + 1)
        bit = (self.me >> self.order[level]) & 1
        return remote(
            self.refs[level].at[pl.ds((1 - bit) * size, size)],
            self.refs[level + 1],
            self.send.at[level],
            self.recv.at[level],
            {"dp": self.me ^ (1 << self.order[level])},
        )

    def go(self, level):
        self.copy(level).start()

    def add(self, level):
        size = self.parts >> (level + 1)
        bit = (self.me >> self.order[level]) & 1
        here, landed = self.refs[level], self.refs[level + 1]
        self.copy(level).wait_recv()

        def one(part, carry):
            total = here[bit * size + part].astype(F32) + landed[part].astype(F32)
            landed[part] = total.astype(landed.dtype)
            return carry

        lax.fori_loop(0, size, one, 0)

    def put(self, columns, found, offset):
        rows = self.refs[0].shape[1]
        for at in range(found.shape[0] // rows):
            part = place(offset // rows + at, self.order)
            self.refs[0][part, :, columns] = found[at * rows:(at + 1) * rows].astype(BF16)

    def step(self, level):
        self.add(level)
        if level + 1 < len(self.order):
            self.go(level + 1)

    def drain(self):
        for level in range(len(self.refs) - 1):
            self.copy(level).wait_send()


def layer_kernel(
    pieces, levels,
    lengths, gain_one, bias_one, gain_two, bias_two,
    tokens_hbm, w_attn_hbm, w_out_hbm, w_up_hbm, w_down_hbm, cotangent_hbm,
    out_delta, grad_in, out_attn, out_out, out_up, out_down, out_gains,
    tokens, w_attn, w_out_all, w_zero, w_up, w_down, cotangent,
    act, query, key, value, query0, key0, probs, selected, mixed,
    stacks, scores, chances, offsets, lost,
    hidden_one, act_two, hidden, grad_pre, grad_mixed,
    feed_s, feed_a, feed_b, two_s, two_a, two_b, one_b,
    grad_key, grad_value, grad_sel, grad_key0, grad_proj, gain_sum, grad_query0,
    exchange, *rest,
):
    seq, width = tokens.shape
    local = w_attn.shape[1]
    heads = local // HEAD
    blocks, chunks = seq // BLOCK, seq // CHUNK
    shards = mixed.shape[0]
    parts = 1 << levels
    own_rows = width // parts
    rest = list(rest)
    take = lambda count: [rest.pop(0) for _ in range(count)]
    scatter_refs = [take(levels + 1) for _ in range(5)]
    zero_send, zero_recv, out_send, out_recv, mix_send, mix_recv = take(6)
    sums_send, sums_recv, scat_send, scat_recv, ex_send, ex_recv, load_sem, tokens_sem = take(8)
    mine = lax.axis_index("tensor")
    me = lax.axis_index("dp")
    twin = {"tensor": mine ^ 1}
    across = {"tensor": mine ^ 2}
    peers = [{"tensor": mine ^ step} for step in (1, 2, 3)]

    loads = [
        pltpu.make_async_copy(source, target, load_sem.at[at])
        for at, (source, target) in enumerate((
            (w_attn_hbm, w_attn), (w_out_hbm, w_out_all.at[mine]),
            (w_up_hbm, w_up), (w_down_hbm, w_down), (cotangent_hbm, cotangent),
        ))
    ]
    attn_load, out_load, up_load, down_load, cot_load = loads

    def token_load(chunk):
        rows = rows_at(chunk, CHUNK)
        return pltpu.make_async_copy(tokens_hbm.at[rows], tokens.at[rows], tokens_sem.at[chunk])

    out_load.start()
    token_load(0).start()
    attn_load.start()
    for chunk in range(1, chunks):
        token_load(chunk).start()
    greet(tuple(peers) + tuple({"dp": me ^ (1 << level)} for level in range(levels)))
    for load in loads[2:]:
        load.start()

    def out_copy(stage, slot, peer):
        block = w_out_all.at[slot]
        return remote(block, block, out_send.at[stage], out_recv.at[stage], peer)

    def zero_copy(stage, peer, source):
        return remote(source, w_zero, zero_send.at[stage], zero_recv.at[0], peer)

    head_rows = w_attn.at[pl.ds(0, 2), pl.ds(0, HEAD)]
    out_load.wait()
    out_copy(1, mine, twin).start()
    attn_load.wait()

    @pl.when(mine == 0)
    def _():
        zero_copy(0, across, head_rows).start()
        zero_copy(1, twin, head_rows).start()
        w_zero[...] = w_attn[0:2, 0:HEAD]

    out_copy(0, mine, across).start()

    lane = lax.broadcasted_iota(jnp.int32, (1, local), 1)
    here = [(lane >= head * HEAD) & (lane < (head + 1) * HEAD) for head in range(heads)]
    row = lax.broadcasted_iota(jnp.int32, (BLOCK, 1), 0)
    column = lax.broadcasted_iota(jnp.int32, (1, BAND), 1) - PAD
    for ref in (key, value, key0, selected):
        ref[0:PAD, :] = jnp.zeros((PAD, ref.shape[1]), ref.dtype)
    for ref in (grad_key, grad_value, grad_sel, grad_key0):
        ref[...] = jnp.zeros(ref.shape, ref.dtype)
    gain_sum[...] = jnp.zeros(gain_sum.shape, F32)

    def pick(found):
        total = found[(heads - 1) * BLOCK:]
        for head in range(heads - 1):
            total = jnp.where(here[head], found[head * BLOCK:(head + 1) * BLOCK], total)
        return total

    def stack(target, wide, scale):
        for head in range(heads):
            target[head * BLOCK:(head + 1) * BLOCK, :] = jnp.where(here[head], wide * scale, 0.0).astype(BF16)

    def project(step, carry):
        rows = rows_at(step, CHUNK)
        padded = pl.ds(pl.multiple_of(step * CHUNK + PAD, CHUNK), CHUNK)
        token_load(step).wait()
        center, scale = norm_stats(tokens[rows, :].astype(F32))
        low = (center * scale * gain_one[...].reshape(1, width) + bias_one[...].reshape(1, width)).astype(BF16)
        act[rows, :] = low
        query[rows, :] = dot_nt(low, w_attn[0]).astype(BF16)
        key[padded, :] = dot_nt(low, w_attn[1]).astype(BF16)
        value[padded, :] = dot_nt(low, w_attn[2]).astype(BF16)
        return carry

    lax.fori_loop(0, chunks, project, 0)

    @pl.when(mine != 0)
    def _():
        zero_copy(0, twin, w_zero).wait_recv()

    @pl.when(mine == 2)
    def _():
        zero_copy(0, twin, w_zero).start()

    def project0(step, carry):
        rows = rows_at(step, CHUNK)
        padded = pl.ds(pl.multiple_of(step * CHUNK + PAD, CHUNK), CHUNK)
        low = act[rows, :]
        found = dot_nt(low, w_zero[0]).astype(BF16).astype(F32)
        query0[rows, :] = (found * SCALING).astype(BF16)
        key0[padded, :] = dot_nt(low, w_zero[1]).astype(BF16)
        return carry

    lax.fori_loop(0, chunks, project0, 0)

    def select(block, carry):
        rows = rows_at(block, BLOCK)
        first, _ = first_of(row + block * BLOCK, lengths, pieces)
        first = first - block * BLOCK
        score = dot_nt(query0[rows, :], key0[pl.ds(rows.start, BAND), :])
        keep = (column > first) & (column < row)
        own = pl.ds(pl.multiple_of(rows.start + PAD, BLOCK), BLOCK)
        selected[own, :] = jnp.where(keep, jnp.maximum(score, 0.0), 0.0).astype(BF16)
        return carry

    lax.fori_loop(0, blocks, select, 0)

    def mix_copy(stage, slot, block, peer):
        part = mixed.at[slot, rows_at(block, BLOCK)]
        return remote(part, part, mix_send.at[stage, block], mix_recv.at[stage, block], peer)

    GROUP = 32
    places = BAND // BLOCK

    def attend_block(block, lot):
        rows = rows_at(block, BLOCK)
        band = rows.start
        first, valid = first_of(row + block * BLOCK, lengths, pieces)
        first = first - block * BLOCK
        inside = column >= first
        carried = (inside & (column < row)).astype(BF16)
        found = [
            dot(
                carried[:, part * BLOCK:(part + 1) * BLOCK],
                selected[pl.ds(pl.multiple_of(band + part * BLOCK, BLOCK), BLOCK), BAND - (part + 1) * BLOCK:],
            )
            for part in range(places)
        ]
        for at in range(places):
            cut = slice(at * BLOCK, (at + 1) * BLOCK)
            penalty = sum(found[part][:, cut] for part in range(at, places))
            offsets[lot, :, cut] = jnp.where((inside & (column <= row))[:, cut], -penalty, -1e30)
        stack(stacks.at[lot], query[rows, :].astype(F32), SCALING)
        scores[lot] = dot_nt(stacks[lot], key[pl.ds(band, BAND), :])
        for group in range(heads * BLOCK // GROUP):
            cut = slice(group * GROUP, (group + 1) * GROUP)
            at = group * GROUP % BLOCK
            logits = scores[lot, cut, :] + offsets[lot, at:at + GROUP, :]
            raised = jnp.exp(logits - jnp.max(logits, axis=-1, keepdims=True))
            chances[lot, cut, :] = (raised * (1.0 / jnp.sum(raised, axis=-1, keepdims=True))).astype(BF16)
        low = chances[lot]
        total = pick(dot(low, value[pl.ds(band, BAND), :]))
        return low, (total * valid.astype(F32)).astype(BF16)

    def attend(step, carry):
        chunk = chunks - 1 - step
        done = [attend_block(2 * chunk + lot, lot) for lot in range(2)]
        for lot in (1, 0):
            block = 2 * chunk + lot
            probs[block] = done[lot][0]
            mixed[mine, rows_at(block, BLOCK), :] = done[lot][1]
            mix_copy(0, mine, block, across).start()
            mix_copy(1, mine, block, twin).start()
        return carry

    lax.fori_loop(0, chunks, attend, 0)

    out_copy(0, mine ^ 2, across).wait_recv()
    out_copy(2, mine ^ 2, twin).start()

    def relay(chunk):
        for lot in (1, 0):
            block = 2 * chunk + lot
            mix_copy(0, mine ^ 2, block, across).wait_recv()
            mix_copy(2, mine ^ 2, block, twin).start()

    relay(chunks - 1)
    out_copy(1, mine ^ 1, twin).wait_recv()
    out_copy(2, mine ^ 3, twin).wait_recv()
    for load in loads[2:]:
        load.wait()

    feed = Sum(feed_s, feed_a, feed_b, out_delta, sums_send.at[0], sums_recv.at[0])
    two = Sum(two_s, two_a, two_b, grad_in, sums_send.at[1], sums_recv.at[1])
    one = Sum(two_s, two_a, one_b, grad_in, sums_send.at[2], sums_recv.at[2])
    straight = tuple(range(levels))
    turned = (1, 0, *straight[2:]) if levels > 1 else straight
    ups, downs, firsts, lasts, gains = (
        Scatter(refs, order, scat_send.at[at], scat_recv.at[at])
        for at, (refs, order) in enumerate(zip(scatter_refs, (straight, turned, straight, turned, straight)))
    )
    gain_refs = gains.refs

    def feed_forward(step, carry):
        chunk = chunks - 1 - step
        rows = rows_at(chunk, CHUNK)

        @pl.when(chunk > 0)
        def _():
            relay(chunk - 1)

        for lot in (1, 0):
            block = 2 * chunk + lot
            mix_copy(1, mine ^ 1, block, twin).wait_recv()
            mix_copy(2, mine ^ 3, block, twin).wait_recv()
        branch = sum(dot(mixed[shard, rows, :], w_out_all[shard]) for shard in range(shards))
        after = tokens[rows, :].astype(F32) + branch
        hidden_one[rows, :] = after
        center, scale = norm_stats(after)
        low = (center * scale * gain_two[...].reshape(1, width) + bias_two[...].reshape(1, width)).astype(BF16)
        act_two[rows, :] = low
        up = dot(low, w_up[...])
        square = up * up
        bent = jnp.tanh(GELU_ROOT * (up + GELU_CUBE * (square * up)))
        units = (0.5 * up * (1.0 + bent)).astype(BF16)
        hidden[rows, :] = units
        slope = 0.5 * (1.0 + bent) + (0.5 * GELU_ROOT) * up * (1.0 - bent * bent) * (
            1.0 + (3.0 * GELU_CUBE) * square
        )
        before = (dot_nt(cotangent[rows, :].astype(BF16), w_down[...]) * slope).astype(BF16)
        grad_pre[rows, :] = before
        two_s[rows, :] = dot_nt(before, w_up[...]).astype(BF16)
        two.first(chunk)
        feed_s[rows, :] = (dot(units, w_down[...]) + branch * (1.0 / shards)).astype(BF16)
        feed.first(chunk)
        two.second(chunk)
        return carry

    lax.fori_loop(0, chunks, feed_forward, 0)

    half = width // 2
    units = w_up.shape[1]
    every = slice(None)
    cuts = [slice(strip * half, (strip + 1) * half) for strip in range(2)]
    for cut in cuts:
        ups.put(every, dot_tn(act_two[:, cut], grad_pre[...]), cut.start)
    ups.go(0)
    for cut in cuts:
        downs.put(every, dot_tn(cotangent[:, cut].astype(BF16), hidden[...]), cut.start)
    downs.go(0)

    across_row = lax.broadcasted_iota(jnp.int32, (1, BLOCK), 1)
    down_band = lax.broadcasted_iota(jnp.int32, (BAND, 1), 0) - PAD

    def attend_back(block, lot):
        rows = rows_at(block, BLOCK)
        band = pl.ds(rows.start, BAND)
        first, _ = first_of(across_row + block * BLOCK, lengths, pieces)
        first = first - block * BLOCK
        carried = ((down_band >= first) & (down_band < across_row)).astype(BF16)
        stack(stacks.at[lot], grad_mixed[rows, :].astype(F32), 1.0)
        stack(stacks.at[2 + lot], query[rows, :].astype(F32), SCALING)
        scores[lot] = dot_nt(stacks[lot], value[band, :])
        for group in range(BLOCK // GROUP):
            loss = jnp.zeros((GROUP, BAND), F32)
            for head in range(heads):
                cut = slice(head * BLOCK + group * GROUP, head * BLOCK + (group + 1) * GROUP)
                chance = probs[block, cut, :].astype(F32)
                grad = scores[lot, cut, :]
                weighed = chance * grad
                logits = weighed - chance * jnp.sum(weighed, axis=-1, keepdims=True)
                loss = loss - logits
                chances[lot, cut, :] = logits.astype(BF16)
            lost[lot, group * GROUP:(group + 1) * GROUP, :] = loss.astype(BF16)
        logits = chances[lot]
        queried = pick(dot(logits, key[band, :]))
        keyed = dot_tn(logits, stacks[2 + lot])
        valued = dot_tn(probs[block], stacks[lot])
        selects = [
            dot(carried[part * BLOCK:(part + 1) * BLOCK], lost[lot, :, :(part + 1) * BLOCK])
            for part in range(places)
        ]
        return (queried * SCALING).astype(BF16), keyed, valued, selects

    def attend_add(block, lot, keyed, valued, selects):
        rows = rows_at(block, BLOCK)
        band = pl.ds(rows.start, BAND)
        grad_key[band, :] = grad_key[band, :] + keyed
        grad_value[band, :] = grad_value[band, :] + valued
        for part in range(places):
            reach = (part + 1) * BLOCK
            rows_k = pl.ds(pl.multiple_of(rows.start + part * BLOCK, BLOCK), BLOCK)
            grad_sel[rows_k, BAND - reach:] = grad_sel[rows_k, BAND - reach:] + selects[part]
        own = pl.ds(pl.multiple_of(rows.start + PAD, BLOCK), BLOCK)
        score = jnp.where(selected[own, :] > 0, grad_sel[own, :], 0.0).astype(BF16)
        from_key = dot(score, key0[band, :])
        grad_query0[rows, :] = (from_key * SCALING).astype(BF16)
        grad_key0[band, :] = grad_key0[band, :] + dot_tn(score, query0[rows, :])

    def back(step, carry):
        chunk = chunks - 1 - step
        rows = rows_at(chunk, CHUNK)
        padded = pl.ds(pl.multiple_of(chunk * CHUNK + PAD, CHUNK), CHUNK)
        two.third(chunk)
        center, scale = norm_stats(hidden_one[rows, :])
        unit = center * scale
        two.ready(chunk)
        grad = grad_in[rows, :].astype(F32)
        gain_sum[2] = gain_sum[2] + groups_of_eight(grad * unit)
        gain_sum[3] = gain_sum[3] + groups_of_eight(grad)
        e = grad * gain_two[...].reshape(1, width)
        total = cotangent[rows, :] + scale * (
            e - jnp.mean(e, axis=-1, keepdims=True) - unit * jnp.mean(e * unit, axis=-1, keepdims=True)
        )
        hidden_one[rows, :] = total
        position = lax.broadcasted_iota(jnp.int32, (CHUNK, 1), 0) + chunk * CHUNK
        _, valid = first_of(position, lengths, pieces)
        grad_mixed[rows, :] = (
            dot_nt(total.astype(BF16), w_out_all[mine]).astype(BF16).astype(F32) * valid.astype(F32)
        ).astype(BF16)
        upper, *upper_adds = attend_back(2 * chunk + 1, 1)
        lower, *lower_adds = attend_back(2 * chunk, 0)
        attend_add(2 * chunk + 1, 1, *upper_adds)
        attend_add(2 * chunk, 0, *lower_adds)
        grad_q = jnp.concatenate([lower, upper], axis=0)
        grad_k = grad_key[padded, :].astype(BF16)
        grad_v = grad_value[padded, :].astype(BF16)
        grad_q0 = grad_query0[rows, :]
        grad_k0 = grad_key0[padded, :]
        grad_proj[rows, :] = jnp.concatenate(
            [grad_q0.astype(F32), grad_k0, grad_q.astype(F32), grad_k.astype(F32), grad_v.astype(F32)], axis=1
        ).astype(BF16)
        partial = (
            dot(grad_q, w_attn[0])
            + dot(grad_k, w_attn[1])
            + dot(grad_v, w_attn[2])
            + dot(grad_q0, w_zero[0])
            + dot(grad_k0.astype(BF16), w_zero[1])
        )
        two.sent(chunk, 0, 2)
        two_s[rows, :] = partial.astype(BF16)
        one.first(chunk)
        center, scale = norm_stats(tokens[rows, :].astype(F32))
        gain_sum[0] = gain_sum[0] + groups_of_eight(partial * (center * scale))
        gain_sum[1] = gain_sum[1] + groups_of_eight(partial)
        one.second(chunk)
        feed.second(chunk)

        @pl.when(step == chunks - 2)
        def _():
            ups.step(0)
            downs.step(0)

        return carry

    lax.fori_loop(0, chunks, back, 0)

    split = firsts.refs[0].shape[2]
    for cut in cuts:
        firsts.put(every, dot_tn(act[:, cut], grad_proj[:, :split]), cut.start)
    firsts.go(0)
    for cut in cuts:
        lasts.put(slice(0, local), dot_tn(act[:, cut], grad_proj[:, split:]), cut.start)
        lasts.put(slice(local, 2 * local), dot_tn(hidden_one[:, cut].astype(BF16), mixed[mine]), cut.start)
    lasts.go(0)
    sums = [jnp.sum(gain_sum[at], axis=0, keepdims=True) for at in range(4)]
    sums = jnp.concatenate(sums[:2] + [found * (1.0 / shards) for found in sums[2:]], axis=0)
    gain_refs[0][...] = jnp.zeros(gain_refs[0].shape, F32)
    for at in range(parts):
        gain_refs[0][place(at, straight), 0:4, 0:own_rows] = sums[:, at * own_rows:(at + 1) * own_rows]
    gains.go(0)

    for level in range(1, levels):
        ups.step(level)
        downs.step(level)
        for each in (gains, firsts, lasts):
            each.step(level - 1)
    for each in (gains, firsts, lasts):
        each.step(levels - 1)

    final = firsts.refs[-1][0].astype(F32)
    exchange[mine, 0:8, :] = gain_refs[-1][0]
    exchange[mine, 8:8 + own_rows, :] = final[:, :BLOCK]

    def ex_copy(step, slot, peer):
        block = exchange.at[slot]
        return remote(block, block, ex_send.at[step], ex_recv.at[step], peer)

    for step, peer in enumerate(peers):
        ex_copy(step, mine, peer).start()

    def finish(step, carry):
        chunk = chunks - 1 - step
        rows = rows_at(chunk, CHUNK)
        one.third(chunk)
        center, scale = norm_stats(tokens[rows, :].astype(F32))
        unit = center * scale
        feed.third(chunk)
        one.ready(chunk)
        e = grad_in[rows, :].astype(F32) * gain_one[...].reshape(1, width)
        found = (
            hidden_one[rows, :]
            + scale
            * (e - jnp.mean(e, axis=-1, keepdims=True) - unit * jnp.mean(e * unit, axis=-1, keepdims=True))
        ).astype(BF16)
        one.sent(chunk, 2)
        grad_in[rows, :] = found
        return carry

    lax.fori_loop(0, chunks, finish, 0)

    out_up[...] = ups.refs[-1][0]
    out_down[...] = downs.refs[-1][0]
    out_out[...] = lasts.refs[-1][0, :, local:].astype(F32)
    for step, peer in enumerate(peers):
        ex_copy(step, mine ^ (step + 1), peer).wait_recv()
    total = exchange[0]
    for shard in range(1, shards):
        total = total + exchange[shard]
    out_gains[...] = total[0:8]
    extra = total[8:8 + own_rows] * (mine == 0).astype(F32)
    for at, found in enumerate((extra[:, :HEAD], extra[:, HEAD:])):
        base = final[:, BLOCK + at * local:BLOCK + (at + 1) * local]
        out_attn[at] = jnp.concatenate([base[:, :HEAD] + found, base[:, HEAD:]], axis=1)
    out_attn[2] = lasts.refs[-1][0, :, :local].astype(F32)

    def settle(chunk, carry):
        feed.ready(chunk)
        feed.sent(chunk, 0, 2)
        one.sent(chunk, 0)
        for lot in range(2):
            block = 2 * chunk + lot
            mix_copy(0, mine, block, across).wait_send()
            mix_copy(1, mine, block, twin).wait_send()
            mix_copy(2, mine ^ 2, block, twin).wait_send()
        return carry

    lax.fori_loop(0, chunks, settle, 0)
    for each in (ups, downs, firsts, lasts, gains):
        each.drain()
    for step, peer in enumerate(peers):
        ex_copy(step, mine, peer).wait_send()
    out_copy(0, mine, across).wait_send()
    out_copy(1, mine, twin).wait_send()
    out_copy(2, mine ^ 2, twin).wait_send()

    @pl.when(mine == 0)
    def _():
        zero_copy(0, across, head_rows).wait_send()
        zero_copy(1, twin, head_rows).wait_send()

    @pl.when(mine == 2)
    def _():
        zero_copy(0, twin, w_zero).wait_send()


VMEM = pl.BlockSpec(memory_space=pltpu.VMEM)
SMEM = pl.BlockSpec(memory_space=pltpu.SMEM)
ANY = pl.BlockSpec(memory_space=pl.ANY)
DMA = pltpu.SemaphoreType.DMA
LIMIT = 67_000_000


def layer_call(tokens, gain_one, bias_one, w_attn, w_out, gain_two, bias_two, w_up, w_down, lengths, cotangent):
    seq, width = tokens.shape
    local = w_attn.shape[1]
    units = w_up.shape[1]
    heads = local // HEAD
    parts = lax.axis_size("dp")
    levels = parts.bit_length() - 1
    own_rows = width // parts
    blocks, chunks = seq // BLOCK, seq // CHUNK
    shards = lax.axis_size("tensor")
    shape = jax.ShapeDtypeStruct
    packed = BLOCK + 3 * local
    outs = (
        shape((seq, width), BF16),
        shape((seq, width), BF16),
        shape((3, own_rows, local), F32),
        shape((own_rows, local), F32),
        shape((own_rows, units), BF16),
        shape((own_rows, units), BF16),
        shape((8, BLOCK), F32),
    )

    def scatter(columns, rows, dtype):
        return [
            pltpu.VMEM((max(parts >> level, 1), rows, columns), dtype) for level in range(levels + 1)
        ]

    low = lambda *dims: pltpu.VMEM(dims, BF16)
    wide = lambda *dims: pltpu.VMEM(dims, F32)
    high = -(-own_rows // 8) * 8
    stacked = heads * BLOCK
    scratch = (
        [low(seq, width), low(3, local, width), low(shards, local, width), low(2, HEAD, width)]
        + [low(width, units), low(units, width), wide(seq, width)]
        + [low(seq, width), low(seq, local), low(seq + PAD, local), low(seq + PAD, local)]
        + [low(seq, HEAD), low(seq + PAD, HEAD), low(blocks, stacked, BAND), low(seq + PAD, BAND)]
        + [low(shards, seq, local)]
        + [low(4, stacked, local), wide(2, stacked, BAND), low(2, stacked, BAND), wide(2, BLOCK, BAND), low(2, BLOCK, BAND)]
        + [wide(seq, width), low(seq, width), low(seq, units), low(seq, units), low(seq, local)]
        + [low(seq, width), low(chunks, BLOCK, width), low(chunks, BLOCK, width)]
        + [low(seq, width), low(chunks, BLOCK, width), low(chunks, BLOCK, width), low(chunks, BLOCK, width)]
        + [wide(seq + PAD, local)] * 2
        + [wide(seq + PAD, BAND), wide(seq + PAD, HEAD)]
        + [low(seq, packed), wide(4, 8, width), low(seq, HEAD)]
        + [wide(shards, 8 + high, BLOCK)]
        + scatter(units, own_rows, BF16)
        + scatter(units, own_rows, BF16)
        + scatter(BLOCK + 2 * local, own_rows, BF16)
        + scatter(2 * local, own_rows, BF16)
        + scatter(BLOCK, 8, F32)
        + [DMA((2,)), DMA((1,)), DMA((3,)), DMA((3,)), DMA((3, blocks)), DMA((3, blocks))]
        + [DMA((3, 3, chunks)), DMA((3, 3, chunks)), DMA((5, levels)), DMA((5, levels)), DMA((3,)), DMA((3,))]
        + [DMA((5,)), DMA((chunks,))]
    )
    operands = (
        lengths, gain_one, bias_one, gain_two, bias_two, tokens, w_attn, w_out, w_up, w_down, cotangent,
    )
    return pl.pallas_call(
        functools.partial(layer_kernel, lengths.shape[1], levels),
        out_shape=outs,
        in_specs=[SMEM] + [VMEM] * 4 + [ANY] * 6,
        out_specs=(VMEM,) * len(outs),
        scratch_shapes=scratch,
        compiler_params=pltpu.CompilerParams(
            collective_id=0, has_side_effects=True, vmem_limit_bytes=LIMIT
        ),
        name="layer",
    )(*operands)


def output_kernel(tokens, delta, grad, attn, out, up, down, gains, output, grad_in, to_attn, to_out, to_up, to_down, *to_gains):
    output[...] = tokens[...].astype(F32) + delta[...].astype(F32)
    grad_in[...] = grad[...].astype(F32)

    @pl.when(pl.program_id(0) == 0)
    def _():
        to_attn[...] = attn[...]
        to_out[...] = out[...].T
        to_up[...] = up[...].astype(F32)
        to_down[...] = down[...].astype(F32)
        for at, ref in enumerate(to_gains):
            ref[...] = gains[at, :ref.shape[0]]


def output_call(tokens, delta, grad, attn, out, up, down, gains):
    rows, width = tokens.shape
    own = up.shape[0]
    shape = jax.ShapeDtypeStruct
    outs = (
        [shape((rows, width), F32)] * 2
        + [shape(attn.shape, F32), shape(out.shape[::-1], F32), shape(up.shape, F32), shape(down.shape, F32)]
        + [shape((own,), F32)] * 4
    )
    block = pl.BlockSpec((CHUNK, width), lambda at: (at, 0))

    def whole(leaf):
        rank = len(leaf.shape)
        return pl.BlockSpec(leaf.shape, lambda at: (0,) * rank)

    return pl.pallas_call(
        output_kernel,
        grid=(rows // CHUNK,),
        out_shape=outs,
        in_specs=[block] * 3 + [whole(leaf) for leaf in (attn, out, up, down, gains)],
        out_specs=[block] * 2 + [whole(leaf) for leaf in outs[2:]],
        name="outputs",
    )(tokens, delta, grad, attn, out, up, down, gains)


def body(
    tokens, gain_one, bias_one, w_attn, w_out, gain_two, bias_two, w_up, w_down, piece_lengths, cotangent
):
    found = layer_call(
        tokens, gain_one, bias_one, jnp.swapaxes(w_attn, 1, 2), w_out, gain_two, bias_two,
        w_up, w_down, piece_lengths, cotangent,
    )
    output, grad_in, grad_attn, grad_out, grad_up, grad_down, *gains = output_call(tokens, *found)
    return (output, grad_in, grad_attn, grad_out, grad_up, grad_down.T, *gains)


def solution(mesh):
    placed = (
        P("dp", None), P(), P(), P(None, None, "tensor"), P("tensor", None), P(), P(),
        P(None, "tensor"), P("tensor", None), P("dp", None), P("dp", None),
    )
    return jax.shard_map(
        body,
        mesh=mesh,
        in_specs=placed,
        out_specs=(
            P("dp", None), P("dp", None), P(None, "dp", "tensor"), P("tensor", "dp"), P("dp", "tensor"),
            P("tensor", "dp"), P("dp"), P("dp"), P("dp"), P("dp"),
        ),
        check_vma=False,
    )
```

```python
import functools

import jax
import jax.numpy as jnp
from jax import lax
from jax.experimental import pallas as pl
from jax.experimental.pallas import tpu as pltpu
from jax.sharding import PartitionSpec as P

F32 = jnp.float32
BF16 = jnp.bfloat16
MESH = pl.DeviceIdType.MESH
HEAD = 64
EPSILON = 1e-05
BLOCK = 128
BAND = 384
PAD = BAND - BLOCK
CHUNK = 256
SCALING = HEAD ** (-0.5)
NT = (((1,), (1,)), ((), ()))
TN = (((0,), (0,)), ((), ()))


def dot(a, b):
    return jnp.dot(a, b, preferred_element_type=F32)


def dot_nt(a, b):
    return lax.dot_general(a, b, NT, preferred_element_type=F32)


def dot_tn(a, b):
    return lax.dot_general(a, b, TN, preferred_element_type=F32)


def rows_at(index, size):
    return pl.ds(pl.multiple_of(index * size, size), size)


def first_of(position, lengths, pieces):
    first = jnp.zeros_like(position)
    end = jnp.int32(0)
    for piece in range(pieces - 1):
        size = lengths[0, piece]
        end = end + size
        first = jnp.where(position >= end, end, first)
    return first, position < end


def norm_stats(x):
    center = x - jnp.mean(x, axis=-1, keepdims=True)
    spread = jnp.mean(center * center, axis=-1, keepdims=True)
    return center, lax.rsqrt(spread + EPSILON)


def remote(src, dst, send, recv, peer):
    return pltpu.make_async_remote_copy(
        src_ref=src, dst_ref=dst, send_sem=send, recv_sem=recv, device_id=peer, device_id_type=MESH
    )


def greet(peers):
    barrier = pltpu.get_barrier_semaphore()
    for peer in peers:
        pl.semaphore_signal(barrier, inc=1, device_id=peer, device_id_type=MESH)
    pl.semaphore_wait(barrier, len(peers))


GELU_ROOT = 0.7978845608028654
GELU_CUBE = 0.044715


def place(value, order):
    return sum(((value >> bit) & 1) << (len(order) - 1 - at) for at, bit in enumerate(order))


def groups_of_eight(x):
    return jnp.sum(x.reshape(x.shape[0] // 8, 8, x.shape[1]), axis=0)


class Sum:
    def __init__(self, source, pair, other, result, send, recv):
        self.refs = source, pair, other, result
        self.send, self.recv = send, recv
        mine = lax.axis_index("tensor")
        self.core = mine & 1
        self.twin, self.across = {"tensor": mine ^ 1}, {"tensor": mine ^ 2}

    def half(self, chunk, core):
        return pl.ds(pl.multiple_of(chunk * CHUNK + core * BLOCK, BLOCK), BLOCK)

    def copy(self, stage, chunk):
        source, pair, other, result = self.refs
        own, theirs = self.half(chunk, self.core), self.half(chunk, 1 - self.core)
        src, dst, peer = (
            (source.at[theirs], pair.at[chunk], self.twin),
            (pair.at[chunk], other.at[chunk], self.across),
            (result.at[own], result.at[own], self.twin),
        )[stage]
        return remote(src, dst, self.send.at[stage, chunk], self.recv.at[stage, chunk], peer)

    def first(self, chunk):
        self.copy(0, chunk).start()

    def second(self, chunk):
        source, pair, other, result = self.refs
        self.copy(0, chunk).wait_recv()
        own = source[self.half(chunk, self.core), :].astype(F32)
        pair[chunk] = (own + pair[chunk].astype(F32)).astype(BF16)
        self.copy(1, chunk).start()

    def third(self, chunk):
        source, pair, other, result = self.refs
        self.copy(1, chunk).wait_recv()
        self.copy(1, chunk).wait_send()
        total = pair[chunk].astype(F32) + other[chunk].astype(F32)
        result[self.half(chunk, self.core), :] = total.astype(BF16)
        self.copy(2, chunk).start()

    def ready(self, chunk):
        self.copy(2, chunk).wait_recv()

    def sent(self, chunk, *stages):
        for stage in stages:
            self.copy(stage, chunk).wait_send()


class Scatter:
    def __init__(self, refs, order, send, recv):
        self.refs, self.order = refs, order
        self.send, self.recv = send, recv
        self.parts = refs[0].shape[0]
        self.me = lax.axis_index("dp")

    def copy(self, level):
        size = self.parts >> (level + 1)
        bit = (self.me >> self.order[level]) & 1
        return remote(
            self.refs[level].at[pl.ds((1 - bit) * size, size)],
            self.refs[level + 1],
            self.send.at[level],
            self.recv.at[level],
            {"dp": self.me ^ (1 << self.order[level])},
        )

    def go(self, level):
        self.copy(level).start()

    def add(self, level):
        size = self.parts >> (level + 1)
        bit = (self.me >> self.order[level]) & 1
        here, landed = self.refs[level], self.refs[level + 1]
        self.copy(level).wait_recv()

        def one(part, carry):
            total = here[bit * size + part].astype(F32) + landed[part].astype(F32)
            landed[part] = total.astype(landed.dtype)
            return carry

        lax.fori_loop(0, size, one, 0)

    def put(self, columns, found, offset):
        rows = self.refs[0].shape[1]
        for at in range(found.shape[0] // rows):
            part = place(offset // rows + at, self.order)
            self.refs[0][part, :, columns] = found[at * rows:(at + 1) * rows].astype(BF16)

    def step(self, level):
        self.add(level)
        if level + 1 < len(self.order):
            self.go(level + 1)

    def drain(self):
        for level in range(len(self.refs) - 1):
            self.copy(level).wait_send()


def layer_kernel(
    pieces, levels,
    lengths, gain_one, bias_one, gain_two, bias_two,
    tokens_hbm, w_attn_hbm, w_out_hbm, w_up_hbm, w_down_hbm, cotangent_hbm,
    output_hbm, grad_hbm, out_attn, out_out, out_up, out_down, out_gains,
    out_delta, grad_in, tokens, w_attn, w_out_all, w_zero, w_up, w_down, cotangent,
    act, query, key, value, query0, key0, probs, selected, mixed,
    stacks, scores, chances, offsets, lost,
    hidden_one, act_two, hidden, grad_pre, grad_mixed,
    feed_s, feed_a, feed_b, two_s, two_a, two_b, one_b,
    grad_key, grad_value, grad_sel, grad_key0, grad_proj, gain_sum, grad_query0,
    exchange, *rest,
):
    seq, width = tokens.shape
    local = w_attn.shape[1]
    heads = local // HEAD
    blocks, chunks = seq // BLOCK, seq // CHUNK
    shards = mixed.shape[0]
    parts = 1 << levels
    own_rows = width // parts
    rest = list(rest)
    take = lambda count: [rest.pop(0) for _ in range(count)]
    scatter_refs = [take(levels + 1) for _ in range(8)]
    part_send, part_recv, zero_send, zero_recv, out_send, out_recv, mix_send, mix_recv = take(8)
    sums_send, sums_recv, scat_send, scat_recv, ex_send, ex_recv = take(6)
    load_sem, tokens_sem, store_sem = take(3)
    mine = lax.axis_index("tensor")
    me = lax.axis_index("dp")
    twin = {"tensor": mine ^ 1}
    across = {"tensor": mine ^ 2}
    peers = [{"tensor": mine ^ step} for step in (1, 2, 3)]

    loads = [
        pltpu.make_async_copy(source, target, load_sem.at[at])
        for at, (source, target) in enumerate((
            (w_attn_hbm, w_attn), (w_out_hbm, w_out_all.at[mine]),
            (w_up_hbm, w_up), (w_down_hbm, w_down), (cotangent_hbm, cotangent),
        ))
    ]
    attn_load, out_load, up_load, down_load, cot_load = loads

    def token_load(chunk):
        rows = rows_at(chunk, CHUNK)
        return pltpu.make_async_copy(tokens_hbm.at[rows], tokens.at[rows], tokens_sem.at[chunk])

    out_load.start()
    token_load(0).start()
    attn_load.start()
    for chunk in range(1, chunks):
        token_load(chunk).start()
    greet(tuple(peers) + tuple({"dp": me ^ (1 << level)} for level in range(levels)))
    for load in loads[2:]:
        load.start()

    def out_copy(stage, slot, peer):
        block = w_out_all.at[slot]
        return remote(block, block, out_send.at[stage], out_recv.at[stage], peer)

    def zero_copy(stage, peer, source):
        return remote(source, w_zero, zero_send.at[stage], zero_recv.at[0], peer)

    quarters = 4
    quarter = lax.rem(me, quarters)
    piece = local // quarters

    def part_copy(stage):
        slot = mine if stage == 0 else mine ^ 2
        start = (quarter, quarter, quarter // 2 * 2)[stage]
        peer = (across, {"dp": me ^ 1}, {"dp": me ^ 2})[stage]
        size = (piece, piece, 2 * piece)[stage]
        block = w_out_all.at[slot, pl.ds(pl.multiple_of(start * piece, piece), size)]
        return remote(block, block, part_send.at[stage], part_recv.at[stage], peer)

    head_rows = w_attn.at[pl.ds(0, 2), pl.ds(0, HEAD)]
    out_load.wait()
    out_copy(1, mine, twin).start()
    attn_load.wait()

    @pl.when(mine == 0)
    def _():
        zero_copy(0, across, head_rows).start()
        zero_copy(1, twin, head_rows).start()
        w_zero[...] = w_attn[0:2, 0:HEAD]

    part_copy(0).start()

    lane = lax.broadcasted_iota(jnp.int32, (1, local), 1)
    here = [(lane >= head * HEAD) & (lane < (head + 1) * HEAD) for head in range(heads)]
    row = lax.broadcasted_iota(jnp.int32, (BLOCK, 1), 0)
    column = lax.broadcasted_iota(jnp.int32, (1, BAND), 1) - PAD
    for ref in (key, value, key0, selected):
        ref[0:PAD, :] = jnp.zeros((PAD, ref.shape[1]), ref.dtype)
    def pick(found):
        total = found[(heads - 1) * BLOCK:]
        for head in range(heads - 1):
            total = jnp.where(here[head], found[head * BLOCK:(head + 1) * BLOCK], total)
        return total

    def stack(target, wide, scale):
        for head in range(heads):
            target[head * BLOCK:(head + 1) * BLOCK, :] = jnp.where(here[head], wide * scale, 0.0).astype(BF16)

    def project(step, carry):
        rows = rows_at(step, CHUNK)
        padded = pl.ds(pl.multiple_of(step * CHUNK + PAD, CHUNK), CHUNK)
        token_load(step).wait()
        center, scale = norm_stats(tokens[rows, :].astype(F32))
        low = (center * scale * gain_one[...].reshape(1, width) + bias_one[...].reshape(1, width)).astype(BF16)
        act[rows, :] = low
        query[rows, :] = dot_nt(low, w_attn[0]).astype(BF16)
        key[padded, :] = dot_nt(low, w_attn[1]).astype(BF16)
        value[padded, :] = dot_nt(low, w_attn[2]).astype(BF16)
        return carry

    lax.fori_loop(0, chunks, project, 0)

    part_copy(0).wait_recv()
    part_copy(1).start()

    for load in loads[2:]:
        load.wait()

    def back_down(step, carry):
        rows = rows_at(step, CHUNK)
        grad_pre[rows, :] = dot_nt(cotangent[rows, :].astype(BF16), w_down[...]).astype(BF16)
        return carry

    lax.fori_loop(0, chunks, back_down, 0)

    @pl.when(mine == 2)
    def _():
        zero_copy(0, twin, w_zero).wait_recv()
        zero_copy(0, twin, w_zero).start()

    for ref in (grad_key, grad_value, grad_sel, grad_key0):
        ref[...] = jnp.zeros(ref.shape, ref.dtype)
    gain_sum[...] = jnp.zeros(gain_sum.shape, F32)

    @pl.when((mine & 1) == 1)
    def _():
        zero_copy(0, twin, w_zero).wait_recv()

    def project0(step, carry):
        rows = rows_at(step, CHUNK)
        padded = pl.ds(pl.multiple_of(step * CHUNK + PAD, CHUNK), CHUNK)
        low = act[rows, :]
        found = dot_nt(low, w_zero[...].reshape(2 * HEAD, width)).astype(BF16).astype(F32)
        query0[rows, :] = (found[:, :HEAD] * SCALING).astype(BF16)
        key0[padded, :] = found[:, HEAD:].astype(BF16)
        return carry

    lax.fori_loop(0, chunks, project0, 0)

    def select(block, carry):
        rows = rows_at(block, BLOCK)
        first, _ = first_of(row + block * BLOCK, lengths, pieces)
        first = first - block * BLOCK
        score = dot_nt(query0[rows, :], key0[pl.ds(rows.start, BAND), :])
        keep = (column > first) & (column < row)
        own = pl.ds(pl.multiple_of(rows.start + PAD, BLOCK), BLOCK)
        selected[own, :] = jnp.where(keep, jnp.maximum(score, 0.0), 0.0).astype(BF16)
        return carry

    lax.fori_loop(0, blocks, select, 0)
    part_copy(1).wait_recv()
    part_copy(2).start()

    def mix_copy(stage, slot, block, peer):
        part = mixed.at[slot, rows_at(block, BLOCK)]
        return remote(part, part, mix_send.at[stage, block], mix_recv.at[stage, block], peer)

    def relay(chunk):
        for lot in (1, 0):
            block = 2 * chunk + lot
            mix_copy(0, mine ^ 2, block, across).wait_recv()
            mix_copy(2, mine ^ 2, block, twin).start()

    GROUP = 32
    places = BAND // BLOCK

    def attend_block(block, lot):
        rows = rows_at(block, BLOCK)
        band = rows.start
        first, valid = first_of(row + block * BLOCK, lengths, pieces)
        first = first - block * BLOCK
        inside = column >= first
        carried = (inside & (column < row)).astype(BF16)
        found = [
            dot(
                carried[:, part * BLOCK:(part + 1) * BLOCK],
                selected[pl.ds(pl.multiple_of(band + part * BLOCK, BLOCK), BLOCK), BAND - (part + 1) * BLOCK:],
            )
            for part in range(places)
        ]
        for at in range(places):
            cut = slice(at * BLOCK, (at + 1) * BLOCK)
            penalty = sum(found[part][:, cut] for part in range(at, places))
            offsets[lot, :, cut] = jnp.where((inside & (column <= row))[:, cut], -penalty, -1e30)
        stack(stacks.at[lot], query[rows, :].astype(F32), SCALING)
        scores[lot] = dot_nt(stacks[lot], key[pl.ds(band, BAND), :])
        for group in range(heads * BLOCK // GROUP):
            cut = slice(group * GROUP, (group + 1) * GROUP)
            at = group * GROUP % BLOCK
            logits = scores[lot, cut, :] + offsets[lot, at:at + GROUP, :]
            raised = jnp.exp(logits - jnp.max(logits, axis=-1, keepdims=True))
            chances[lot, cut, :] = (raised * (1.0 / jnp.sum(raised, axis=-1, keepdims=True))).astype(BF16)
        low = chances[lot]
        total = pick(dot(low, value[pl.ds(band, BAND), :]))
        return low, (total * valid.astype(F32)).astype(BF16)

    def attend(step, carry):
        chunk = chunks - 1 - step

        @pl.when(step == chunks - 1)
        def _():
            part_copy(2).wait_recv()
            out_copy(2, mine ^ 2, twin).start()

        done = [attend_block(2 * chunk + lot, lot) for lot in range(2)]
        for lot in (1, 0):
            block = 2 * chunk + lot
            probs[block] = done[lot][0]
            mixed[mine, rows_at(block, BLOCK), :] = done[lot][1]
            mix_copy(0, mine, block, across).start()
            mix_copy(1, mine, block, twin).start()

        return carry

    lax.fori_loop(0, chunks, attend, 0)

    relay(chunks - 1)
    out_copy(1, mine ^ 1, twin).wait_recv()
    out_copy(2, mine ^ 3, twin).wait_recv()

    feed = Sum(feed_s, feed_a, feed_b, out_delta, sums_send.at[0], sums_recv.at[0])
    two = Sum(two_s, two_a, two_b, grad_in, sums_send.at[1], sums_recv.at[1])
    one = Sum(two_s, two_a, one_b, grad_in, sums_send.at[2], sums_recv.at[2])
    straight = tuple(range(levels))
    turned = (1, 0, *straight[2:]) if levels > 1 else straight
    ups_a, ups_b, downs_a, downs_b, firsts, lasts, extras, gains = (
        Scatter(refs, order, scat_send.at[at], scat_recv.at[at])
        for at, (refs, order) in enumerate(zip(scatter_refs, (straight, straight, turned, turned, straight, turned, straight, straight)))
    )
    gain_refs = gains.refs

    def feed_forward(step, carry):
        chunk = chunks - 1 - step
        rows = rows_at(chunk, CHUNK)

        @pl.when(chunk > 0)
        def _():
            relay(chunk - 1)

        for lot in (1, 0):
            block = 2 * chunk + lot
            mix_copy(1, mine ^ 1, block, twin).wait_recv()
            mix_copy(2, mine ^ 3, block, twin).wait_recv()
        branch = sum(dot(mixed[shard, rows, :], w_out_all[shard]) for shard in range(shards))
        after = tokens[rows, :].astype(F32) + branch
        hidden_one[rows, :] = after
        center, scale = norm_stats(after)
        low = (center * scale * gain_two[...].reshape(1, width) + bias_two[...].reshape(1, width)).astype(BF16)
        act_two[rows, :] = low
        up = dot(low, w_up[...])

        @pl.when(step > 1)
        def _():
            two.second(chunk + 1)

        @pl.when(step > 1)
        def _():
            feed.second(chunk + 2)

        square = up * up
        bent = jnp.tanh(GELU_ROOT * (up + GELU_CUBE * (square * up)))
        units = (0.5 * up * (1.0 + bent)).astype(BF16)
        hidden[rows, :] = units
        slope = 0.5 * (1.0 + bent) + (0.5 * GELU_ROOT) * up * (1.0 - bent * bent) * (
            1.0 + (3.0 * GELU_CUBE) * square
        )
        before = (grad_pre[rows, :].astype(F32) * slope).astype(BF16)
        grad_pre[rows, :] = before
        two_s[rows, :] = dot_nt(before, w_up[...]).astype(BF16)
        two.first(chunk)
        feed_s[rows, :] = (dot(units, w_down[...]) + branch * (1.0 / shards)).astype(BF16)
        feed.first(chunk)

        @pl.when(step == 0)
        def _():
            two.second(chunk)

        return carry

    lax.fori_loop(0, chunks, feed_forward, 0)
    two.second(0)
    feed.second(1)

    half = width // 2
    units = w_up.shape[1]
    every = slice(None)
    cuts = [slice(strip * half, (strip + 1) * half) for strip in range(2)]
    fore, aft = slice(0, units // 2), slice(units // 2, units)
    for cut in cuts:
        found = dot_tn(act_two[:, cut], grad_pre[...])
        ups_a.put(every, found[:, fore], cut.start)
        ups_b.put(every, found[:, aft], cut.start)
    ups_a.go(0)
    two.third(chunks - 1)
    ups_b.go(0)
    for cut in cuts:
        found = dot_tn(cotangent[:, cut].astype(BF16), hidden[...])
        downs_a.put(every, found[:, fore], cut.start)
        downs_b.put(every, found[:, aft], cut.start)
    downs_a.go(0)
    downs_b.go(0)

    across_row = lax.broadcasted_iota(jnp.int32, (1, BLOCK), 1)
    down_band = lax.broadcasted_iota(jnp.int32, (BAND, 1), 0) - PAD

    def attend_back(block, lot):
        rows = rows_at(block, BLOCK)
        band = pl.ds(rows.start, BAND)
        first, _ = first_of(across_row + block * BLOCK, lengths, pieces)
        first = first - block * BLOCK
        carried = ((down_band >= first) & (down_band < across_row)).astype(BF16)
        stack(stacks.at[lot], grad_mixed[rows, :].astype(F32), 1.0)
        stack(stacks.at[2 + lot], query[rows, :].astype(F32), SCALING)
        scores[lot] = dot_nt(stacks[lot], value[band, :])
        for group in range(BLOCK // GROUP):
            loss = jnp.zeros((GROUP, BAND), F32)
            for head in range(heads):
                cut = slice(head * BLOCK + group * GROUP, head * BLOCK + (group + 1) * GROUP)
                chance = probs[block, cut, :].astype(F32)
                grad = scores[lot, cut, :]
                weighed = chance * grad
                logits = weighed - chance * jnp.sum(weighed, axis=-1, keepdims=True)
                loss = loss - logits
                chances[lot, cut, :] = logits.astype(BF16)
            lost[lot, group * GROUP:(group + 1) * GROUP, :] = loss.astype(BF16)
        logits = chances[lot]
        queried = pick(dot(logits, key[band, :]))
        keyed = dot_tn(logits, stacks[2 + lot])
        valued = dot_tn(probs[block], stacks[lot])
        selects = [
            dot(carried[part * BLOCK:(part + 1) * BLOCK], lost[lot, :, :(part + 1) * BLOCK])
            for part in range(places)
        ]
        return (queried * SCALING).astype(BF16), keyed, valued, selects

    def attend_add(block, lot, keyed, valued, selects):
        rows = rows_at(block, BLOCK)
        band = pl.ds(rows.start, BAND)
        grad_key[band, :] = grad_key[band, :] + keyed
        grad_value[band, :] = grad_value[band, :] + valued
        for part in range(places):
            reach = (part + 1) * BLOCK
            rows_k = pl.ds(pl.multiple_of(rows.start + part * BLOCK, BLOCK), BLOCK)
            grad_sel[rows_k, BAND - reach:] = grad_sel[rows_k, BAND - reach:] + selects[part]
        own = pl.ds(pl.multiple_of(rows.start + PAD, BLOCK), BLOCK)
        score = jnp.where(selected[own, :] > 0, grad_sel[own, :], 0.0).astype(BF16)
        from_key = dot(score, key0[band, :])
        grad_query0[rows, :] = (from_key * SCALING).astype(BF16)
        grad_key0[band, :] = grad_key0[band, :] + dot_tn(score, query0[rows, :])

    def back(step, carry):
        chunk = chunks - 1 - step
        rows = rows_at(chunk, CHUNK)
        padded = pl.ds(pl.multiple_of(chunk * CHUNK + PAD, CHUNK), CHUNK)
        center, scale = norm_stats(hidden_one[rows, :])
        unit = center * scale
        two.ready(chunk)
        grad = grad_in[rows, :].astype(F32)
        gain_sum[2] = gain_sum[2] + groups_of_eight(grad * unit)
        gain_sum[3] = gain_sum[3] + groups_of_eight(grad)
        e = grad * gain_two[...].reshape(1, width)
        total = cotangent[rows, :] + scale * (
            e - jnp.mean(e, axis=-1, keepdims=True) - unit * jnp.mean(e * unit, axis=-1, keepdims=True)
        )
        hidden_one[rows, :] = total
        position = lax.broadcasted_iota(jnp.int32, (CHUNK, 1), 0) + chunk * CHUNK
        _, valid = first_of(position, lengths, pieces)
        grad_mixed[rows, :] = (
            dot_nt(total.astype(BF16), w_out_all[mine]).astype(BF16).astype(F32) * valid.astype(F32)
        ).astype(BF16)

        @pl.when(step == chunks - 2)
        def _():
            ups_a.step(0)
            downs_a.step(0)

        @pl.when(step == chunks - 1)
        def _():
            ups_a.step(1)
            downs_a.step(1)

        upper, *upper_adds = attend_back(2 * chunk + 1, 1)
        lower, *lower_adds = attend_back(2 * chunk, 0)

        @pl.when(step > 0)
        def _():
            one.second(chunk + 1)

        @pl.when(step == 0)
        def _():
            feed.second(0)

        @pl.when(step == chunks - 1)
        def _():
            ups_b.step(1)
            downs_b.step(1)

        attend_add(2 * chunk + 1, 1, *upper_adds)
        attend_add(2 * chunk, 0, *lower_adds)
        grad_q = jnp.concatenate([lower, upper], axis=0)
        grad_k = grad_key[padded, :].astype(BF16)
        grad_v = grad_value[padded, :].astype(BF16)
        grad_q0 = grad_query0[rows, :]
        grad_k0 = grad_key0[padded, :]
        grad_proj[rows, :] = jnp.concatenate(
            [grad_q0.astype(F32), grad_k0, grad_q.astype(F32), grad_k.astype(F32), grad_v.astype(F32)], axis=1
        ).astype(BF16)
        partial = (
            dot(grad_q, w_attn[0])
            + dot(grad_k, w_attn[1])
            + dot(grad_v, w_attn[2])
            + dot(grad_q0, w_zero[0])
            + dot(grad_k0.astype(BF16), w_zero[1])
        )
        two.sent(chunk, 0, 2)
        two_s[rows, :] = partial.astype(BF16)
        one.first(chunk)
        center, scale = norm_stats(tokens[rows, :].astype(F32))
        gain_sum[0] = gain_sum[0] + groups_of_eight(partial * (center * scale))
        gain_sum[1] = gain_sum[1] + groups_of_eight(partial)

        @pl.when(step == chunks - 2)
        def _():
            ups_b.step(0)
            downs_b.step(0)

        @pl.when(step < chunks - 1)
        def _():
            two.third(chunk - 1)

        return carry

    lax.fori_loop(0, chunks, back, 0)

    for cut in cuts:
        extras.put(every, dot_tn(act[:, cut], grad_proj[:, :BLOCK]), cut.start)
    extras.go(0)
    one.second(0)
    sums = [jnp.sum(gain_sum[at], axis=0, keepdims=True) for at in range(4)]
    sums = jnp.concatenate(sums[:2] + [found * (1.0 / shards) for found in sums[2:]], axis=0)
    gain_refs[0][...] = jnp.zeros(gain_refs[0].shape, F32)
    for at in range(parts):
        gain_refs[0][place(at, straight), 0:4, 0:own_rows] = sums[:, at * own_rows:(at + 1) * own_rows]
    gains.go(0)
    for cut in cuts:
        lasts.put(slice(0, local), dot_tn(act[:, cut], grad_proj[:, BLOCK + 2 * local:]), cut.start)
        lasts.put(slice(local, 2 * local), dot_tn(hidden_one[:, cut].astype(BF16), mixed[mine]), cut.start)
    lasts.go(0)
    for cut in cuts:
        firsts.put(every, dot_tn(act[:, cut], grad_proj[:, BLOCK:BLOCK + 2 * local]), cut.start)
    firsts.go(0)

    def ex_copy(step, slot, peer):
        block = exchange.at[slot]
        return remote(block, block, ex_send.at[step], ex_recv.at[step], peer)

    def swap():
        exchange[mine, 0:8, :] = gain_refs[-1][0]
        exchange[mine, 8:8 + own_rows, :] = extras.refs[-1][0].astype(F32)
        for step, peer in enumerate(peers):
            ex_copy(step, mine, peer).start()

    def store(which, chunk):
        rows = rows_at(chunk, CHUNK)
        source, target = ((out_delta, output_hbm), (grad_in, grad_hbm))[which]
        return pltpu.make_async_copy(source.at[rows], target.at[rows], store_sem.at[which, chunk])

    def finish(chunk):
        rows = rows_at(chunk, CHUNK)
        one.third(chunk)
        center, scale = norm_stats(tokens[rows, :].astype(F32))
        unit = center * scale
        feed.third(chunk)
        one.ready(chunk)
        e = grad_in[rows, :].astype(F32) * gain_one[...].reshape(1, width)
        found = hidden_one[rows, :] + scale * (
            e - jnp.mean(e, axis=-1, keepdims=True) - unit * jnp.mean(e * unit, axis=-1, keepdims=True)
        )
        one.sent(chunk, 2)
        grad_in[rows, :] = found.astype(BF16)
        store(1, chunk).start()

    def give(chunk):
        rows = rows_at(chunk, CHUNK)
        feed.ready(chunk)
        found = tokens[rows, :].astype(F32) + out_delta[rows, :].astype(F32)
        feed.sent(chunk, 2)
        out_delta[rows, :] = found.astype(BF16)
        store(0, chunk).start()

    left = list(range(chunks))
    finish(left.pop())
    give(left[-1] + 1)
    finish(left.pop())
    for level in range(levels):
        for each in (extras, gains):
            each.step(level)
        if level == levels - 1:
            swap()
        for each in (lasts, firsts):
            each.step(level)
        if level >= 2:
            for each in (ups_a, downs_a, ups_b, downs_b):
                each.step(level)
        if left:
            give(left[-1] + 1)
            finish(left.pop())
    while left:
        give(left[-1] + 1)
        finish(left.pop())
    give(0)

    for ref, pair in ((out_up, (ups_a, ups_b)), (out_down, (downs_a, downs_b))):
        ref[:, fore] = pair[0].refs[-1][0]
        ref[:, aft] = pair[1].refs[-1][0]
    for step, peer in enumerate(peers):
        ex_copy(step, mine ^ (step + 1), peer).wait_recv()
    total = exchange[0]
    for shard in range(1, shards):
        total = total + exchange[shard]
    out_gains[...] = total[0:8]
    final = firsts.refs[-1][0].astype(F32)
    extra = total[8:8 + own_rows] * (mine == 0).astype(F32)
    for at, found in enumerate((extra[:, :HEAD], extra[:, HEAD:])):
        base = final[:, at * local:(at + 1) * local]
        out_attn[at] = jnp.concatenate([base[:, :HEAD] + found, base[:, HEAD:]], axis=1)
    out_attn[2] = lasts.refs[-1][0, :, :local].astype(F32)
    out_out[...] = lasts.refs[-1][0, :, local:].astype(F32)

    def settle(chunk, carry):
        feed.sent(chunk, 0)
        one.sent(chunk, 0)
        store(0, chunk).wait()
        store(1, chunk).wait()

        for lot in range(2):
            block = 2 * chunk + lot
            mix_copy(0, mine, block, across).wait_send()
            mix_copy(1, mine, block, twin).wait_send()
            mix_copy(2, mine ^ 2, block, twin).wait_send()
        return carry

    lax.fori_loop(0, chunks, settle, 0)
    for each in (ups_a, ups_b, downs_a, downs_b, firsts, lasts, extras, gains):
        each.drain()
    for step, peer in enumerate(peers):
        ex_copy(step, mine, peer).wait_send()
    for stage in range(3):
        part_copy(stage).wait_send()
    out_copy(1, mine, twin).wait_send()
    out_copy(2, mine ^ 2, twin).wait_send()

    @pl.when(mine == 0)
    def _():
        zero_copy(0, across, head_rows).wait_send()
        zero_copy(1, twin, head_rows).wait_send()

    @pl.when(mine == 2)
    def _():
        zero_copy(0, twin, w_zero).wait_send()


VMEM = pl.BlockSpec(memory_space=pltpu.VMEM)
SMEM = pl.BlockSpec(memory_space=pltpu.SMEM)
ANY = pl.BlockSpec(memory_space=pl.ANY)
DMA = pltpu.SemaphoreType.DMA
LIMIT = 67_000_000


def layer_call(tokens, gain_one, bias_one, w_attn, w_out, gain_two, bias_two, w_up, w_down, lengths, cotangent):
    seq, width = tokens.shape
    local = w_attn.shape[1]
    units = w_up.shape[1]
    heads = local // HEAD
    parts = lax.axis_size("dp")
    levels = parts.bit_length() - 1
    own_rows = width // parts
    blocks, chunks = seq // BLOCK, seq // CHUNK
    shards = lax.axis_size("tensor")
    shape = jax.ShapeDtypeStruct
    outs = (
        shape((seq, width), BF16),
        shape((seq, width), BF16),
        shape((3, own_rows, local), F32),
        shape((own_rows, local), F32),
        shape((own_rows, units), BF16),
        shape((own_rows, units), BF16),
        shape((8, BLOCK), F32),
    )

    def scatter(columns, rows, dtype):
        return [
            pltpu.VMEM((max(parts >> level, 1), rows, columns), dtype) for level in range(levels + 1)
        ]

    low = lambda *dims: pltpu.VMEM(dims, BF16)
    wide = lambda *dims: pltpu.VMEM(dims, F32)
    stacked = heads * BLOCK
    scratch = (
        [low(seq, width), low(seq, width), low(seq, width), low(3, local, width), low(shards, local, width), low(2, HEAD, width)]
        + [low(width, units), low(units, width), wide(seq, width)]
        + [low(seq, width), low(seq, local), low(seq + PAD, local), low(seq + PAD, local)]
        + [low(seq, HEAD), low(seq + PAD, HEAD), low(blocks, stacked, BAND), low(seq + PAD, BAND)]
        + [low(shards, seq, local)]
        + [low(4, stacked, local), wide(2, stacked, BAND), low(2, stacked, BAND), wide(2, BLOCK, BAND), low(2, BLOCK, BAND)]
        + [wide(seq, width), low(seq, width), low(seq, units), low(seq, units), low(seq, local)]
        + [low(seq, width), low(chunks, BLOCK, width), low(chunks, BLOCK, width)]
        + [low(seq, width), low(chunks, BLOCK, width), low(chunks, BLOCK, width), low(chunks, BLOCK, width)]
        + [wide(seq + PAD, local)] * 2
        + [wide(seq + PAD, BAND), wide(seq + PAD, HEAD)]
        + [low(seq, BLOCK + 3 * local), wide(4, 8, width), low(seq, HEAD)]
        + [wide(shards, 8 - own_rows // -8 * 8, BLOCK)]
        + scatter(units // 2, own_rows, BF16)
        + scatter(units // 2, own_rows, BF16)
        + scatter(units // 2, own_rows, BF16)
        + scatter(units // 2, own_rows, BF16)
        + scatter(2 * local, own_rows, BF16)
        + scatter(2 * local, own_rows, BF16)
        + scatter(BLOCK, own_rows, BF16)
        + scatter(BLOCK, 8, F32)
        + [DMA((3,)), DMA((3,)), DMA((2,)), DMA((1,)), DMA((3,)), DMA((3,)), DMA((3, blocks)), DMA((3, blocks))]
        + [DMA((3, 3, chunks)), DMA((3, 3, chunks)), DMA((8, levels)), DMA((8, levels)), DMA((3,)), DMA((3,))]
        + [DMA((5,)), DMA((chunks,)), DMA((2, chunks))]
    )
    operands = (
        lengths, gain_one, bias_one, gain_two, bias_two, tokens, w_attn, w_out, w_up, w_down, cotangent,
    )
    return pl.pallas_call(
        functools.partial(layer_kernel, lengths.shape[1], levels),
        out_shape=outs,
        in_specs=[SMEM] + [VMEM] * 4 + [ANY] * 6,
        out_specs=(ANY,) * 2 + (VMEM,) * (len(outs) - 2),
        scratch_shapes=scratch,
        compiler_params=pltpu.CompilerParams(
            collective_id=0, has_side_effects=True, vmem_limit_bytes=LIMIT
        ),
        name="layer",
    )(*operands)


def output_kernel(output, grad_in, attn, out, up, down, gains, to_output, to_grad, to_attn, to_out, to_up, to_down, *to_gains):
    to_output[...] = output[...].astype(F32)
    to_grad[...] = grad_in[...].astype(F32)

    @pl.when(pl.program_id(0) == 0)
    def _():
        to_attn[...] = attn[...]
        to_out[...] = out[...].T
        to_up[...] = up[...].astype(F32)
        to_down[...] = down[...].astype(F32)
        for at, ref in enumerate(to_gains):
            ref[...] = gains[at, :ref.shape[0]]


def output_call(output, grad_in, attn, out, up, down, gains):
    rows, width = output.shape
    own = up.shape[0]
    shape = jax.ShapeDtypeStruct
    outs = (
        [shape((rows, width), F32)] * 2
        + [shape(attn.shape, F32), shape(out.shape[::-1], F32), shape(up.shape, F32), shape(down.shape, F32)]
        + [shape((own,), F32)] * 4
    )
    block = pl.BlockSpec((CHUNK, width), lambda at: (at, 0))

    def whole(leaf):
        rank = len(leaf.shape)
        return pl.BlockSpec(leaf.shape, lambda at: (0,) * rank)

    return pl.pallas_call(
        output_kernel,
        grid=(rows // CHUNK,),
        out_shape=outs,
        in_specs=[block] * 2 + [whole(leaf) for leaf in (attn, out, up, down, gains)],
        out_specs=[block] * 2 + [whole(leaf) for leaf in outs[2:]],
        name="outputs",
    )(output, grad_in, attn, out, up, down, gains)


def body(
    tokens, gain_one, bias_one, w_attn, w_out, gain_two, bias_two, w_up, w_down, piece_lengths, cotangent
):
    found = layer_call(
        tokens, gain_one, bias_one, jnp.swapaxes(w_attn, 1, 2), w_out, gain_two, bias_two,
        w_up, w_down, piece_lengths, cotangent,
    )
    output, grad_in, grad_attn, grad_out, grad_up, grad_down, *gains = output_call(*found)
    return (output, grad_in, grad_attn, grad_out, grad_up, grad_down.T, *gains)


def solution(mesh):
    placed = (
        P("dp", None), P(), P(), P(None, None, "tensor"), P("tensor", None), P(), P(),
        P(None, "tensor"), P("tensor", None), P("dp", None), P("dp", None),
    )
    return jax.shard_map(
        body,
        mesh=mesh,
        in_specs=placed,
        out_specs=(
            P("dp", None), P("dp", None), P(None, "dp", "tensor"), P("tensor", "dp"), P("dp", "tensor"),
            P("tensor", "dp"), P("dp"), P("dp"), P("dp"), P("dp"),
        ),
        check_vma=False,
    )
```

```python
import functools

import jax
import jax.numpy as jnp
from jax import lax
from jax.experimental import pallas as pl
from jax.experimental.pallas import tpu as pltpu
from jax.sharding import PartitionSpec as P

F32 = jnp.float32
BF16 = jnp.bfloat16
MESH = pl.DeviceIdType.MESH
HEAD = 64
EPSILON = 1e-05
BLOCK = 128
BAND = 384
PAD = BAND - BLOCK
CHUNK = 256
SCALING = HEAD ** (-0.5)
NT = (((1,), (1,)), ((), ()))
TN = (((0,), (0,)), ((), ()))


def dot(a, b):
    return jnp.dot(a, b, preferred_element_type=F32)


def dot_nt(a, b):
    return lax.dot_general(a, b, NT, preferred_element_type=F32)


def dot_tn(a, b):
    return lax.dot_general(a, b, TN, preferred_element_type=F32)


def rows_at(index, size):
    return pl.ds(pl.multiple_of(index * size, size), size)


def first_of(position, lengths, pieces):
    first = jnp.zeros_like(position)
    end = jnp.int32(0)
    for piece in range(pieces - 1):
        size = lengths[0, piece]
        end = end + size
        first = jnp.where(position >= end, end, first)
    return first, position < end


def norm_stats(x):
    center = x - jnp.mean(x, axis=-1, keepdims=True)
    spread = jnp.mean(center * center, axis=-1, keepdims=True)
    return center, lax.rsqrt(spread + EPSILON)


def remote(src, dst, send, recv, peer):
    return pltpu.make_async_remote_copy(
        src_ref=src, dst_ref=dst, send_sem=send, recv_sem=recv, device_id=peer, device_id_type=MESH
    )


def greet(peers):
    barrier = pltpu.get_barrier_semaphore()
    for peer in peers:
        pl.semaphore_signal(barrier, inc=1, device_id=peer, device_id_type=MESH)
    pl.semaphore_wait(barrier, len(peers))


GELU_ROOT = 0.7978845608028654
GELU_CUBE = 0.044715


def place(value, order):
    return sum(((value >> bit) & 1) << (len(order) - 1 - at) for at, bit in enumerate(order))


def groups_of_eight(x):
    return jnp.sum(x.reshape(x.shape[0] // 8, 8, x.shape[1]), axis=0)


class Sum:
    def __init__(self, source, pair, other, result, send, recv):
        self.refs = source, pair, other, result
        self.send, self.recv = send, recv
        mine = lax.axis_index("tensor")
        self.core = mine & 1
        self.twin, self.across = {"tensor": mine ^ 1}, {"tensor": mine ^ 2}

    def half(self, chunk, core):
        return pl.ds(pl.multiple_of(chunk * CHUNK + core * BLOCK, BLOCK), BLOCK)

    def copy(self, stage, chunk):
        source, pair, other, result = self.refs
        own, theirs = self.half(chunk, self.core), self.half(chunk, 1 - self.core)
        src, dst, peer = (
            (source.at[theirs], pair.at[chunk], self.twin),
            (pair.at[chunk], other.at[chunk], self.across),
            (result.at[own], result.at[own], self.twin),
        )[stage]
        return remote(src, dst, self.send.at[stage, chunk], self.recv.at[stage, chunk], peer)

    def first(self, chunk):
        self.copy(0, chunk).start()

    def second(self, chunk):
        source, pair, other, result = self.refs
        self.copy(0, chunk).wait_recv()
        own = source[self.half(chunk, self.core), :].astype(F32)
        pair[chunk] = (own + pair[chunk].astype(F32)).astype(BF16)
        self.copy(1, chunk).start()

    def third(self, chunk):
        source, pair, other, result = self.refs
        self.copy(1, chunk).wait_recv()
        self.copy(1, chunk).wait_send()
        total = pair[chunk].astype(F32) + other[chunk].astype(F32)
        result[self.half(chunk, self.core), :] = total.astype(BF16)
        self.copy(2, chunk).start()

    def ready(self, chunk):
        self.copy(2, chunk).wait_recv()

    def sent(self, chunk, *stages):
        for stage in stages:
            self.copy(stage, chunk).wait_send()


class Scatter:
    def __init__(self, refs, order, send, recv):
        self.refs, self.order = refs, order
        self.send, self.recv = send, recv
        self.parts = refs[0].shape[0]
        self.me = lax.axis_index("dp")

    def copy(self, level):
        size = self.parts >> (level + 1)
        bit = (self.me >> self.order[level]) & 1
        return remote(
            self.refs[level].at[pl.ds((1 - bit) * size, size)],
            self.refs[level + 1],
            self.send.at[level],
            self.recv.at[level],
            {"dp": self.me ^ (1 << self.order[level])},
        )

    def go(self, level):
        self.copy(level).start()

    def add(self, level):
        size = self.parts >> (level + 1)
        bit = (self.me >> self.order[level]) & 1
        here, landed = self.refs[level], self.refs[level + 1]
        self.copy(level).wait_recv()

        def one(part, carry):
            total = here[bit * size + part].astype(F32) + landed[part].astype(F32)
            landed[part] = total.astype(landed.dtype)
            return carry

        lax.fori_loop(0, size, one, 0)

    def put(self, columns, found, offset):
        rows = self.refs[0].shape[1]
        for at in range(found.shape[0] // rows):
            part = place(offset // rows + at, self.order)
            self.refs[0][part, :, columns] = found[at * rows:(at + 1) * rows].astype(BF16)

    def step(self, level):
        self.add(level)
        if level + 1 < len(self.order):
            self.go(level + 1)

    def drain(self):
        for level in range(len(self.refs) - 1):
            self.copy(level).wait_send()


def layer_kernel(
    pieces, levels,
    lengths, gain_one, bias_one, gain_two, bias_two,
    tokens_hbm, w_attn_hbm, w_out_hbm, w_up_hbm, w_down_hbm, cotangent_hbm,
    output_hbm, grad_hbm, small_hbm, extra_hbm, gains_hbm,
    out_delta, grad_in, tokens, w_attn, w_out_all, w_zero, w_up, w_down, cotangent,
    act, query, key, value, query0, key0, probs, selected, mixed,
    stacks, scores, chances, offsets, lost,
    hidden_one, act_two, hidden, grad_pre, grad_mixed,
    feed_s, feed_a, feed_b, two_s, two_a, two_b, one_b,
    grad_key, grad_value, grad_sel, grad_key0, grad_proj, gain_sum, grad_query0,
    exchange, extra_parts, *rest,
):
    seq, width = tokens.shape
    local = w_attn.shape[1]
    heads = local // HEAD
    blocks, chunks = seq // BLOCK, seq // CHUNK
    shards = mixed.shape[0]
    parts = 1 << levels
    own_rows = width // parts
    rest = list(rest)
    take = lambda count: [rest.pop(0) for _ in range(count)]
    scatter_refs = [take(levels + 1) for _ in range(10)]
    part_send, part_recv, zero_send, zero_recv, out_send, out_recv, mix_send, mix_recv = take(8)
    sums_send, sums_recv, scat_send, scat_recv, ex_send, ex_recv = take(6)
    load_sem, tokens_sem, store_sem, small_sem, extra_send, extra_recv = take(6)
    mine = lax.axis_index("tensor")
    me = lax.axis_index("dp")
    twin = {"tensor": mine ^ 1}
    across = {"tensor": mine ^ 2}
    peers = [{"tensor": mine ^ step} for step in (1, 2, 3)]

    loads = [
        pltpu.make_async_copy(source, target, load_sem.at[at])
        for at, (source, target) in enumerate((
            (w_attn_hbm, w_attn), (w_out_hbm, w_out_all.at[mine]),
            (w_up_hbm, w_up), (w_down_hbm, w_down), (cotangent_hbm, cotangent),
        ))
    ]
    attn_load, out_load, up_load, down_load, cot_load = loads

    def token_load(chunk):
        rows = rows_at(chunk, CHUNK)
        return pltpu.make_async_copy(tokens_hbm.at[rows], tokens.at[rows], tokens_sem.at[chunk])

    out_load.start()
    token_load(0).start()
    attn_load.start()
    for chunk in range(1, chunks):
        token_load(chunk).start()
    extra_parts[...] = jnp.zeros(extra_parts.shape, BF16)
    greet(tuple(peers) + tuple({"dp": me ^ (1 << level)} for level in range(levels)))
    for load in loads[2:]:
        load.start()

    def out_copy(stage, slot, peer):
        block = w_out_all.at[slot]
        return remote(block, block, out_send.at[stage], out_recv.at[stage], peer)

    def zero_copy(stage, peer, source):
        return remote(source, w_zero, zero_send.at[stage], zero_recv.at[0], peer)

    quarters = 4
    quarter = lax.rem(me, quarters)
    piece = local // quarters

    def part_copy(stage):
        slot = mine if stage == 0 else mine ^ 2
        start = (quarter, quarter, quarter // 2 * 2)[stage]
        peer = (across, {"dp": me ^ 1}, {"dp": me ^ 2})[stage]
        size = (piece, piece, 2 * piece)[stage]
        block = w_out_all.at[slot, pl.ds(pl.multiple_of(start * piece, piece), size)]
        return remote(block, block, part_send.at[stage], part_recv.at[stage], peer)

    head_rows = w_attn.at[pl.ds(0, 2), pl.ds(0, HEAD)]
    out_load.wait()
    out_copy(1, mine, twin).start()
    attn_load.wait()

    @pl.when(mine == 0)
    def _():
        zero_copy(0, across, head_rows).start()
        zero_copy(1, twin, head_rows).start()
        w_zero[...] = w_attn[0:2, 0:HEAD]

    part_copy(0).start()

    lane = lax.broadcasted_iota(jnp.int32, (1, local), 1)
    here = [(lane >= head * HEAD) & (lane < (head + 1) * HEAD) for head in range(heads)]
    row = lax.broadcasted_iota(jnp.int32, (BLOCK, 1), 0)
    column = lax.broadcasted_iota(jnp.int32, (1, BAND), 1) - PAD
    for ref in (key, value, key0, selected):
        ref[0:PAD, :] = jnp.zeros((PAD, ref.shape[1]), ref.dtype)
    def pick(found):
        total = found[(heads - 1) * BLOCK:]
        for head in range(heads - 1):
            total = jnp.where(here[head], found[head * BLOCK:(head + 1) * BLOCK], total)
        return total

    def stack(target, wide, scale):
        for head in range(heads):
            target[head * BLOCK:(head + 1) * BLOCK, :] = jnp.where(here[head], wide * scale, 0.0).astype(BF16)

    def project(step, carry):
        rows = rows_at(step, CHUNK)
        padded = pl.ds(pl.multiple_of(step * CHUNK + PAD, CHUNK), CHUNK)
        token_load(step).wait()
        center, scale = norm_stats(tokens[rows, :].astype(F32))
        low = (center * scale * gain_one[...].reshape(1, width) + bias_one[...].reshape(1, width)).astype(BF16)
        act[rows, :] = low
        query[rows, :] = dot_nt(low, w_attn[0]).astype(BF16)
        key[padded, :] = dot_nt(low, w_attn[1]).astype(BF16)
        value[padded, :] = dot_nt(low, w_attn[2]).astype(BF16)
        return carry

    lax.fori_loop(0, chunks, project, 0)

    for load in loads[2:]:
        load.wait()

    def back_down(step, carry):
        rows = rows_at(step, CHUNK)
        grad_pre[rows, :] = dot_nt(cotangent[rows, :].astype(BF16), w_down[...]).astype(BF16)
        return carry

    lax.fori_loop(0, chunks, back_down, 0)

    @pl.when(mine == 2)
    def _():
        zero_copy(0, twin, w_zero).wait_recv()
        zero_copy(0, twin, w_zero).start()

    part_copy(0).wait_recv()
    part_copy(1).start()
    for ref in (grad_key, grad_value, grad_sel, grad_key0):
        ref[...] = jnp.zeros(ref.shape, ref.dtype)
    gain_sum[...] = jnp.zeros(gain_sum.shape, F32)

    @pl.when((mine & 1) == 1)
    def _():
        zero_copy(0, twin, w_zero).wait_recv()

    def project0(step, carry):
        rows = rows_at(step, CHUNK)
        padded = pl.ds(pl.multiple_of(step * CHUNK + PAD, CHUNK), CHUNK)
        low = act[rows, :]
        found = dot_nt(low, w_zero[...].reshape(2 * HEAD, width)).astype(BF16).astype(F32)
        query0[rows, :] = (found[:, :HEAD] * SCALING).astype(BF16)
        key0[padded, :] = found[:, HEAD:].astype(BF16)
        return carry

    lax.fori_loop(0, chunks, project0, 0)

    def select(block, carry):
        rows = rows_at(block, BLOCK)
        first, _ = first_of(row + block * BLOCK, lengths, pieces)
        first = first - block * BLOCK
        score = dot_nt(query0[rows, :], key0[pl.ds(rows.start, BAND), :])
        keep = (column > first) & (column < row)
        own = pl.ds(pl.multiple_of(rows.start + PAD, BLOCK), BLOCK)
        selected[own, :] = jnp.where(keep, jnp.maximum(score, 0.0), 0.0).astype(BF16)
        return carry

    lax.fori_loop(0, blocks, select, 0)
    part_copy(1).wait_recv()
    part_copy(2).start()

    def mix_copy(stage, slot, block, peer):
        part = mixed.at[slot, rows_at(block, BLOCK)]
        return remote(part, part, mix_send.at[stage, block], mix_recv.at[stage, block], peer)

    def relay(chunk):
        for lot in (1, 0):
            block = 2 * chunk + lot
            mix_copy(0, mine ^ 2, block, across).wait_recv()
            mix_copy(2, mine ^ 2, block, twin).start()

    GROUP = 32
    places = BAND // BLOCK

    def attend_block(block, lot):
        rows = rows_at(block, BLOCK)
        band = rows.start
        first, valid = first_of(row + block * BLOCK, lengths, pieces)
        first = first - block * BLOCK
        inside = column >= first
        carried = (inside & (column < row)).astype(BF16)
        found = [
            dot(
                carried[:, part * BLOCK:(part + 1) * BLOCK],
                selected[pl.ds(pl.multiple_of(band + part * BLOCK, BLOCK), BLOCK), BAND - (part + 1) * BLOCK:],
            )
            for part in range(places)
        ]
        for at in range(places):
            cut = slice(at * BLOCK, (at + 1) * BLOCK)
            penalty = sum(found[part][:, cut] for part in range(at, places))
            offsets[lot, :, cut] = jnp.where((inside & (column <= row))[:, cut], -penalty, -1e30)
        stack(stacks.at[lot], query[rows, :].astype(F32), SCALING)
        scores[lot] = dot_nt(stacks[lot], key[pl.ds(band, BAND), :])
        for group in range(heads * BLOCK // GROUP):
            cut = slice(group * GROUP, (group + 1) * GROUP)
            at = group * GROUP % BLOCK
            logits = scores[lot, cut, :] + offsets[lot, at:at + GROUP, :]
            raised = jnp.exp(logits - jnp.max(logits, axis=-1, keepdims=True))
            chances[lot, cut, :] = (raised * (1.0 / jnp.sum(raised, axis=-1, keepdims=True))).astype(BF16)
        low = chances[lot]
        total = pick(dot(low, value[pl.ds(band, BAND), :]))
        return low, (total * valid.astype(F32)).astype(BF16)

    def attend(step, carry):
        chunk = chunks - 1 - step

        @pl.when(step == chunks - 1)
        def _():
            part_copy(2).wait_recv()
            out_copy(2, mine ^ 2, twin).start()

        done = [attend_block(2 * chunk + lot, lot) for lot in range(2)]
        for lot in (1, 0):
            block = 2 * chunk + lot
            probs[block] = done[lot][0]
            mixed[mine, rows_at(block, BLOCK), :] = done[lot][1]
            mix_copy(0, mine, block, across).start()
            mix_copy(1, mine, block, twin).start()

        return carry

    lax.fori_loop(0, chunks, attend, 0)

    relay(chunks - 1)
    out_copy(1, mine ^ 1, twin).wait_recv()
    out_copy(2, mine ^ 3, twin).wait_recv()

    feed = Sum(feed_s, feed_a, feed_b, out_delta, sums_send.at[0], sums_recv.at[0])
    two = Sum(two_s, two_a, two_b, grad_in, sums_send.at[1], sums_recv.at[1])
    one = Sum(two_s, two_a, one_b, grad_in, sums_send.at[2], sums_recv.at[2])
    straight = tuple(range(levels))
    turned = (1, 0, *straight[2:]) if levels > 1 else straight
    ups_a, ups_b, downs_a, downs_b, firsts_a, firsts_b, lasts_a, lasts_b, extras, gains = (
        Scatter(refs, order, scat_send.at[at], scat_recv.at[at])
        for at, (refs, order) in enumerate(zip(scatter_refs, (straight,) * 2 + (turned,) + (straight,) * 3 + (turned,) + (straight,) * 3))
    )
    gain_refs = gains.refs

    def feed_forward(step, carry):
        chunk = chunks - 1 - step
        rows = rows_at(chunk, CHUNK)

        @pl.when(chunk > 0)
        def _():
            relay(chunk - 1)

        for lot in (1, 0):
            block = 2 * chunk + lot
            mix_copy(1, mine ^ 1, block, twin).wait_recv()
            mix_copy(2, mine ^ 3, block, twin).wait_recv()
        branch = sum(dot(mixed[shard, rows, :], w_out_all[shard]) for shard in range(shards))
        after = tokens[rows, :].astype(F32) + branch
        hidden_one[rows, :] = after
        feed_s[rows, :] = branch.astype(BF16)
        center, scale = norm_stats(after)
        low = (center * scale * gain_two[...].reshape(1, width) + bias_two[...].reshape(1, width)).astype(BF16)
        act_two[rows, :] = low
        up = dot(low, w_up[...])

        @pl.when(step > 1)
        def _():
            two.second(chunk + 1)

        square = up * up
        bent = jnp.tanh(GELU_ROOT * (up + GELU_CUBE * (square * up)))
        units = (0.5 * up * (1.0 + bent)).astype(BF16)
        hidden[rows, :] = units
        slope = 0.5 * (1.0 + bent) + (0.5 * GELU_ROOT) * up * (1.0 - bent * bent) * (
            1.0 + (3.0 * GELU_CUBE) * square
        )
        before = (grad_pre[rows, :].astype(F32) * slope).astype(BF16)
        grad_pre[rows, :] = before
        two_s[rows, :] = dot_nt(before, w_up[...]).astype(BF16)
        two.first(chunk)

        @pl.when(step == 0)
        def _():
            two.second(chunk)

        return carry

    lax.fori_loop(0, chunks, feed_forward, 0)
    two.second(0)

    half = width // 2
    units = w_up.shape[1]
    every = slice(None)
    cuts = [slice(strip * half, (strip + 1) * half) for strip in range(2)]
    fore, aft = slice(0, units // 2), slice(units // 2, units)
    for cut in cuts:
        found = dot_tn(cotangent[:, cut].astype(BF16), hidden[...])
        downs_a.put(every, found[:, fore], cut.start)
        downs_b.put(every, found[:, aft], cut.start)
    downs_a.go(0)
    downs_b.go(0)
    for cut in cuts:
        found = dot_tn(act_two[:, cut], grad_pre[...])
        ups_a.put(every, found[:, fore], cut.start)
        ups_b.put(every, found[:, aft], cut.start)
    ups_a.go(0)
    ups_b.go(0)
    two.third(chunks - 1)

    def feeding(chunk):
        rows = rows_at(chunk, CHUNK)
        branch = feed_s[rows, :].astype(F32)
        feed_s[rows, :] = (dot(hidden[rows, :], w_down[...]) + branch * (1.0 / shards)).astype(BF16)
        feed.first(chunk)

    def feed_early(step, carry):
        chunk = chunks - 1 - step
        feeding(chunk)

        @pl.when(step > 0)
        def _():
            feed.second(chunk + 1)

        return carry

    lax.fori_loop(0, chunks // 2, feed_early, 0)

    across_row = lax.broadcasted_iota(jnp.int32, (1, BLOCK), 1)
    down_band = lax.broadcasted_iota(jnp.int32, (BAND, 1), 0) - PAD

    def attend_back(block, lot):
        rows = rows_at(block, BLOCK)
        band = pl.ds(rows.start, BAND)
        first, _ = first_of(across_row + block * BLOCK, lengths, pieces)
        first = first - block * BLOCK
        carried = ((down_band >= first) & (down_band < across_row)).astype(BF16)
        stack(stacks.at[lot], grad_mixed[rows, :].astype(F32), 1.0)
        stack(stacks.at[2 + lot], query[rows, :].astype(F32), SCALING)
        scores[lot] = dot_nt(stacks[lot], value[band, :])
        for group in range(BLOCK // GROUP):
            loss = jnp.zeros((GROUP, BAND), F32)
            for head in range(heads):
                cut = slice(head * BLOCK + group * GROUP, head * BLOCK + (group + 1) * GROUP)
                chance = probs[block, cut, :].astype(F32)
                grad = scores[lot, cut, :]
                weighed = chance * grad
                logits = weighed - chance * jnp.sum(weighed, axis=-1, keepdims=True)
                loss = loss - logits
                chances[lot, cut, :] = logits.astype(BF16)
            lost[lot, group * GROUP:(group + 1) * GROUP, :] = loss.astype(BF16)
        logits = chances[lot]
        queried = pick(dot(logits, key[band, :]))
        keyed = dot_tn(logits, stacks[2 + lot])
        valued = dot_tn(probs[block], stacks[lot])
        selects = [
            dot(carried[part * BLOCK:(part + 1) * BLOCK], lost[lot, :, :(part + 1) * BLOCK])
            for part in range(places)
        ]
        return (queried * SCALING).astype(BF16), keyed, valued, selects

    def attend_add(block, lot, keyed, valued, selects):
        rows = rows_at(block, BLOCK)
        band = pl.ds(rows.start, BAND)
        grad_key[band, :] = grad_key[band, :] + keyed
        grad_value[band, :] = grad_value[band, :] + valued
        for part in range(places):
            reach = (part + 1) * BLOCK
            rows_k = pl.ds(pl.multiple_of(rows.start + part * BLOCK, BLOCK), BLOCK)
            grad_sel[rows_k, BAND - reach:] = grad_sel[rows_k, BAND - reach:] + selects[part]
        own = pl.ds(pl.multiple_of(rows.start + PAD, BLOCK), BLOCK)
        score = jnp.where(selected[own, :] > 0, grad_sel[own, :], 0.0).astype(BF16)
        from_key = dot(score, key0[band, :])
        grad_query0[rows, :] = (from_key * SCALING).astype(BF16)
        grad_key0[band, :] = grad_key0[band, :] + dot_tn(score, query0[rows, :])

    def back(step, carry):
        chunk = chunks - 1 - step
        rows = rows_at(chunk, CHUNK)
        padded = pl.ds(pl.multiple_of(chunk * CHUNK + PAD, CHUNK), CHUNK)
        center, scale = norm_stats(hidden_one[rows, :])
        unit = center * scale
        two.ready(chunk)
        grad = grad_in[rows, :].astype(F32)
        gain_sum[2] = gain_sum[2] + groups_of_eight(grad * unit)
        gain_sum[3] = gain_sum[3] + groups_of_eight(grad)
        e = grad * gain_two[...].reshape(1, width)
        total = cotangent[rows, :] + scale * (
            e - jnp.mean(e, axis=-1, keepdims=True) - unit * jnp.mean(e * unit, axis=-1, keepdims=True)
        )
        hidden_one[rows, :] = total
        position = lax.broadcasted_iota(jnp.int32, (CHUNK, 1), 0) + chunk * CHUNK
        _, valid = first_of(position, lengths, pieces)
        grad_mixed[rows, :] = (
            dot_nt(total.astype(BF16), w_out_all[mine]).astype(BF16).astype(F32) * valid.astype(F32)
        ).astype(BF16)

        upper, *upper_adds = attend_back(2 * chunk + 1, 1)
        lower, *lower_adds = attend_back(2 * chunk, 0)

        @pl.when(step > 0)
        def _():
            one.second(chunk + 1)

        @pl.when(step == 0)
        def _():
            feed.second(chunks // 2)

        @pl.when(step == 2)
        def _():
            ups_a.step(0)

        @pl.when(step == 3)
        def _():
            ups_b.step(0)

        attend_add(2 * chunk + 1, 1, *upper_adds)
        attend_add(2 * chunk, 0, *lower_adds)
        grad_q = jnp.concatenate([lower, upper], axis=0)
        grad_k = grad_key[padded, :].astype(BF16)
        grad_v = grad_value[padded, :].astype(BF16)
        grad_q0 = grad_query0[rows, :]
        grad_k0 = grad_key0[padded, :]
        grad_proj[rows, :] = jnp.concatenate(
            [grad_q0.astype(F32), grad_k0, grad_q.astype(F32), grad_k.astype(F32), grad_v.astype(F32)], axis=1
        ).astype(BF16)
        partial = (
            dot(grad_q, w_attn[0])
            + dot(grad_k, w_attn[1])
            + dot(grad_v, w_attn[2])
            + dot(grad_q0, w_zero[0])
            + dot(grad_k0.astype(BF16), w_zero[1])
        )
        two.sent(chunk, 0, 2)
        two_s[rows, :] = partial.astype(BF16)
        one.first(chunk)
        center, scale = norm_stats(tokens[rows, :].astype(F32))
        gain_sum[0] = gain_sum[0] + groups_of_eight(partial * (center * scale))
        gain_sum[1] = gain_sum[1] + groups_of_eight(partial)

        @pl.when(step == 0)
        def _():
            downs_b.step(0)
            downs_a.step(0)

        @pl.when(step == 1)
        def _():
            downs_b.step(1)

        @pl.when(step == 3)
        def _():
            ups_a.step(1)

        @pl.when(step < chunks - 1)
        def _():
            two.third(chunk - 1)

        return carry

    lax.fori_loop(0, chunks, back, 0)

    for cut in cuts:
        extras.put(every, dot_tn(act[:, cut], grad_proj[:, :BLOCK]), cut.start)
    extras.go(0)
    sums = [jnp.sum(gain_sum[at], axis=0, keepdims=True) for at in range(4)]
    sums = jnp.concatenate(sums[:2] + [found * (1.0 / shards) for found in sums[2:]], axis=0)
    gain_refs[0][...] = jnp.zeros(gain_refs[0].shape, F32)
    for at in range(parts):
        gain_refs[0][place(at, straight), 0:4, 0:own_rows] = sums[:, at * own_rows:(at + 1) * own_rows]
    gains.go(0)
    edge = 2 * BLOCK
    for cut in cuts:
        found = jnp.concatenate(
            [
                dot_tn(act[:, cut], grad_proj[:, BLOCK + 2 * local:]),
                dot_tn(hidden_one[:, cut].astype(BF16), mixed[mine]),
            ],
            axis=1,
        )
        lasts_a.put(every, found[:, :edge], cut.start)
        lasts_b.put(every, found[:, edge:], cut.start)
    lasts_a.go(0)
    lasts_b.go(0)
    for cut in cuts:
        found = dot_tn(act[:, cut], grad_proj[:, BLOCK:BLOCK + 2 * local])
        firsts_a.put(every, found[:, :edge], cut.start)
        firsts_b.put(every, found[:, edge:], cut.start)
    firsts_a.go(0)
    firsts_b.go(0)
    downs_a.step(1)
    ups_b.step(1)
    one.second(0)

    def ex_copy(step, slot, peer):
        block = exchange.at[slot]
        return remote(block, block, ex_send.at[step], ex_recv.at[step], peer)

    def extra_copy(step):
        return remote(
            extras.refs[-1].at[0], extra_parts.at[step], extra_send.at[0], extra_recv.at[step], {"tensor": 0}
        )

    def swap():
        exchange[mine] = gain_refs[-1][0]
        for step, peer in enumerate(peers):
            ex_copy(step, mine, peer).start()
        for step in range(3):

            @pl.when(mine == step + 1)
            def _():
                extra_copy(step).start()

    def feed_late(step, carry):
        chunk = chunks // 2 - 1 - step
        feeding(chunk)

        @pl.when(step > 0)
        def _():
            feed.second(chunk + 1)

        return carry

    lax.fori_loop(0, chunks // 2, feed_late, 0)
    feed.second(0)

    def store(which, chunk):
        rows = rows_at(chunk, CHUNK)
        source, target = ((out_delta, output_hbm), (grad_in, grad_hbm))[which]
        return pltpu.make_async_copy(source.at[rows], target.at[rows], store_sem.at[which, chunk])

    def finish(chunk):
        rows = rows_at(chunk, CHUNK)
        one.third(chunk)
        center, scale = norm_stats(tokens[rows, :].astype(F32))
        unit = center * scale
        feed.third(chunk)
        one.ready(chunk)
        e = grad_in[rows, :].astype(F32) * gain_one[...].reshape(1, width)
        found = hidden_one[rows, :] + scale * (
            e - jnp.mean(e, axis=-1, keepdims=True) - unit * jnp.mean(e * unit, axis=-1, keepdims=True)
        )
        one.sent(chunk, 2)
        grad_in[rows, :] = found.astype(BF16)
        store(1, chunk).start()

    def give(chunk):
        rows = rows_at(chunk, CHUNK)
        feed.ready(chunk)
        found = tokens[rows, :].astype(F32) + out_delta[rows, :].astype(F32)
        feed.sent(chunk, 2)
        out_delta[rows, :] = found.astype(BF16)
        store(0, chunk).start()

    small = (
        (ups_a, 0, every), (ups_b, 1, every), (downs_a, 2, every), (downs_b, 3, every),
        (firsts_a, 4, pl.ds(0, edge)), (firsts_b, 4, pl.ds(edge, 2 * local - edge)),
        (lasts_a, 5, pl.ds(0, edge)), (lasts_b, 5, pl.ds(edge, 2 * local - edge)),
    )

    def small_store(at):
        group, slot, columns = small[at]
        return pltpu.make_async_copy(group.refs[-1].at[0], small_hbm.at[slot, :, columns], small_sem.at[at])

    left = list(range(chunks))
    finish(left.pop())
    for each in (extras, gains):
        each.step(0)
    finish(left.pop())
    for level in range(levels):
        for each in (lasts_a, firsts_a, lasts_b, firsts_b) if level == 0 else (firsts_a, lasts_a, firsts_b, lasts_b):
            each.step(level)
        if level + 1 < levels:
            for each in (extras, gains):
                each.step(level + 1)
        if level + 2 == levels:
            swap()
        if level >= 2:
            for each in (ups_a, downs_a, ups_b, downs_b):
                each.step(level)
        if left:
            give(left[-1] + 2)
            finish(left.pop())
    for at in range(8):
        small_store(at).start()
    give(1)
    give(0)

    for step, peer in enumerate(peers):
        ex_copy(step, mine ^ (step + 1), peer).wait_recv()
    last = pltpu.make_async_copy(exchange, gains_hbm, small_sem.at[len(small)])
    last.start()
    for step in range(3):

        @pl.when(mine == 0)
        def _():
            extra_copy(step).wait_recv()

        @pl.when(mine == step + 1)
        def _():
            extra_copy(step).wait_send()

    parts_store = pltpu.make_async_copy(extra_parts, extra_hbm.at[pl.ds(0, 3)], small_sem.at[len(small) + 1])
    own_store = pltpu.make_async_copy(extras.refs[-1].at[0], extra_hbm.at[3], small_sem.at[len(small) + 2])
    parts_store.start()
    own_store.start()

    def settle(chunk, carry):
        feed.sent(chunk, 0)
        one.sent(chunk, 0)
        store(0, chunk).wait()
        store(1, chunk).wait()

        for lot in range(2):
            block = 2 * chunk + lot
            mix_copy(0, mine, block, across).wait_send()
            mix_copy(1, mine, block, twin).wait_send()
            mix_copy(2, mine ^ 2, block, twin).wait_send()
        return carry

    lax.fori_loop(0, chunks, settle, 0)
    for each in (ups_a, ups_b, downs_a, downs_b, firsts_a, firsts_b, lasts_a, lasts_b, extras, gains):
        each.drain()
    for at in range(len(small)):
        small_store(at).wait()
    for each in (last, parts_store, own_store):
        each.wait()
    for step, peer in enumerate(peers):
        ex_copy(step, mine, peer).wait_send()
    for stage in range(3):
        part_copy(stage).wait_send()
    out_copy(1, mine, twin).wait_send()
    out_copy(2, mine ^ 2, twin).wait_send()

    @pl.when(mine == 0)
    def _():
        zero_copy(0, across, head_rows).wait_send()
        zero_copy(1, twin, head_rows).wait_send()

    @pl.when(mine == 2)
    def _():
        zero_copy(0, twin, w_zero).wait_send()


VMEM = pl.BlockSpec(memory_space=pltpu.VMEM)
SMEM = pl.BlockSpec(memory_space=pltpu.SMEM)
ANY = pl.BlockSpec(memory_space=pl.ANY)
DMA = pltpu.SemaphoreType.DMA
LIMIT = 67_000_000


def layer_call(tokens, gain_one, bias_one, w_attn, w_out, gain_two, bias_two, w_up, w_down, lengths, cotangent):
    seq, width = tokens.shape
    local = w_attn.shape[1]
    units = w_up.shape[1]
    heads = local // HEAD
    parts = lax.axis_size("dp")
    levels = parts.bit_length() - 1
    own_rows = width // parts
    blocks, chunks = seq // BLOCK, seq // CHUNK
    shards = lax.axis_size("tensor")
    shape = jax.ShapeDtypeStruct
    outs = (
        shape((seq, width), BF16),
        shape((seq, width), BF16),
        shape((6, own_rows, 2 * local), BF16),
        shape((4, own_rows, BLOCK), BF16),
        shape((shards, 8, BLOCK), F32),
    )

    def scatter(columns, rows, dtype):
        return [
            pltpu.VMEM((max(parts >> level, 1), rows, columns), dtype) for level in range(levels + 1)
        ]

    low = lambda *dims: pltpu.VMEM(dims, BF16)
    wide = lambda *dims: pltpu.VMEM(dims, F32)
    stacked = heads * BLOCK
    scratch = (
        [low(seq, width), low(seq, width), low(seq, width), low(3, local, width), low(shards, local, width), low(2, HEAD, width)]
        + [low(width, units), low(units, width), wide(seq, width)]
        + [low(seq, width), low(seq, local), low(seq + PAD, local), low(seq + PAD, local)]
        + [low(seq, HEAD), low(seq + PAD, HEAD), low(blocks, stacked, BAND), low(seq + PAD, BAND)]
        + [low(shards, seq, local)]
        + [low(4, stacked, local), wide(2, stacked, BAND), low(2, stacked, BAND), wide(2, BLOCK, BAND), low(2, BLOCK, BAND)]
        + [wide(seq, width), low(seq, width), low(seq, units), low(seq, units), low(seq, local)]
        + [low(seq, width), low(chunks, BLOCK, width), low(chunks, BLOCK, width)]
        + [low(seq, width), low(chunks, BLOCK, width), low(chunks, BLOCK, width), low(chunks, BLOCK, width)]
        + [wide(seq + PAD, local)] * 2
        + [wide(seq + PAD, BAND), wide(seq + PAD, HEAD)]
        + [low(seq, BLOCK + 3 * local), wide(4, 8, width), low(seq, HEAD)]
        + [wide(shards, 8, BLOCK), low(3, own_rows, BLOCK)]
        + scatter(units // 2, own_rows, BF16)
        + scatter(units // 2, own_rows, BF16)
        + scatter(units // 2, own_rows, BF16)
        + scatter(units // 2, own_rows, BF16)
        + scatter(2 * BLOCK, own_rows, BF16)
        + scatter(2 * local - 2 * BLOCK, own_rows, BF16)
        + scatter(2 * BLOCK, own_rows, BF16)
        + scatter(2 * local - 2 * BLOCK, own_rows, BF16)
        + scatter(BLOCK, own_rows, BF16)
        + scatter(BLOCK, 8, F32)
        + [DMA((3,)), DMA((3,)), DMA((2,)), DMA((1,)), DMA((3,)), DMA((3,)), DMA((3, blocks)), DMA((3, blocks))]
        + [DMA((3, 3, chunks)), DMA((3, 3, chunks)), DMA((10, levels)), DMA((10, levels)), DMA((3,)), DMA((3,))]
        + [DMA((5,)), DMA((chunks,)), DMA((2, chunks)), DMA((11,)), DMA((1,)), DMA((3,))]
    )
    operands = (
        lengths, gain_one, bias_one, gain_two, bias_two, tokens, w_attn, w_out, w_up, w_down, cotangent,
    )
    return pl.pallas_call(
        functools.partial(layer_kernel, lengths.shape[1], levels),
        out_shape=outs,
        in_specs=[SMEM] + [VMEM] * 4 + [ANY] * 6,
        out_specs=(ANY,) * len(outs),
        scratch_shapes=scratch,
        compiler_params=pltpu.CompilerParams(
            collective_id=0, has_side_effects=True, vmem_limit_bytes=LIMIT
        ),
        name="layer",
    )(*operands)


def output_kernel(output, grad_in, small, extra, gains, to_output, to_grad, to_attn, to_out, to_up, to_down, *to_gains):
    to_output[...] = output[...].astype(F32)
    to_grad[...] = grad_in[...].astype(F32)
    first = lax.axis_index("tensor") == 0

    @pl.when(pl.program_id(0) == 0)
    def _():
        half = small.shape[2]
        local = half // 2
        for ref, start in ((to_up, 0), (to_down, 2)):
            ref[:, :half] = small[start].astype(F32)
            ref[:, half:] = small[start + 1].astype(F32)
        added = sum(extra[at].astype(F32) for at in range(4))
        added = jnp.where(first, added, 0.0)
        found = small[4].astype(F32)
        for at in range(2):
            base = found[:, at * local:(at + 1) * local]
            head = base[:, :HEAD] + added[:, at * HEAD:(at + 1) * HEAD]
            to_attn[at] = jnp.concatenate([head, base[:, HEAD:]], axis=1)
        found = small[5].astype(F32)
        to_attn[2] = found[:, :local]
        to_out[...] = found[:, local:].T
        total = gains[0]
        for shard in range(1, gains.shape[0]):
            total = total + gains[shard]
        for at, ref in enumerate(to_gains):
            ref[...] = total[at, :ref.shape[0]]


def output_call(output, grad_in, small, extra, gains):
    rows, width = output.shape
    own, half = small.shape[1:]
    shape = lambda *dims: jax.ShapeDtypeStruct(dims, F32)
    outs = (
        [shape(rows, width)] * 2
        + [shape(3, own, half // 2), shape(half // 2, own), shape(own, 2 * half), shape(own, 2 * half)]
        + [shape(own)] * 4
    )
    block = pl.BlockSpec((CHUNK, width), lambda at: (at, 0))

    def whole(leaf):
        rank = len(leaf.shape)
        return pl.BlockSpec(leaf.shape, lambda at: (0,) * rank)

    return pl.pallas_call(
        output_kernel,
        grid=(rows // CHUNK,),
        out_shape=outs,
        in_specs=[block] * 2 + [whole(small), whole(extra), whole(gains)],
        out_specs=[block] * 2 + [whole(leaf) for leaf in outs[2:]],
        name="outputs",
    )(output, grad_in, small, extra, gains)


def body(
    tokens, gain_one, bias_one, w_attn, w_out, gain_two, bias_two, w_up, w_down, piece_lengths, cotangent
):
    found = layer_call(
        tokens, gain_one, bias_one, jnp.swapaxes(w_attn, 1, 2), w_out, gain_two, bias_two,
        w_up, w_down, piece_lengths, cotangent,
    )
    output, grad_in, grad_attn, grad_out, grad_up, grad_down, *gains = output_call(*found)
    return (output, grad_in, grad_attn, grad_out, grad_up, grad_down.T, *gains)


def solution(mesh):
    placed = (
        P("dp", None), P(), P(), P(None, None, "tensor"), P("tensor", None), P(), P(),
        P(None, "tensor"), P("tensor", None), P("dp", None), P("dp", None),
    )
    return jax.shard_map(
        body,
        mesh=mesh,
        in_specs=placed,
        out_specs=(
            P("dp", None), P("dp", None), P(None, "dp", "tensor"), P("tensor", "dp"), P("dp", "tensor"),
            P("tensor", "dp"), P("dp"), P("dp"), P("dp"), P("dp"),
        ),
        check_vma=False,
    )
```

```python
import functools

import jax
import jax.numpy as jnp
from jax import lax
from jax.experimental import pallas as pl
from jax.experimental.pallas import tpu as pltpu
from jax.sharding import PartitionSpec as P

F32 = jnp.float32
BF16 = jnp.bfloat16
MESH = pl.DeviceIdType.MESH
HEAD = 64
EPSILON = 1e-05
BLOCK = 128
BAND = 384
PAD = BAND - BLOCK
CHUNK = 256
SCALING = HEAD ** (-0.5)
NT = (((1,), (1,)), ((), ()))
TN = (((0,), (0,)), ((), ()))


def dot(a, b):
    return jnp.dot(a, b, preferred_element_type=F32)


def dot_nt(a, b):
    return lax.dot_general(a, b, NT, preferred_element_type=F32)


def dot_tn(a, b):
    return lax.dot_general(a, b, TN, preferred_element_type=F32)


def rows_at(index, size):
    return pl.ds(pl.multiple_of(index * size, size), size)


def first_of(position, lengths, pieces):
    first = jnp.zeros_like(position)
    end = jnp.int32(0)
    for piece in range(pieces - 1):
        size = lengths[0, piece]
        end = end + size
        first = jnp.where(position >= end, end, first)
    return first, position < end


def norm_stats(x):
    center = x - jnp.mean(x, axis=-1, keepdims=True)
    spread = jnp.mean(center * center, axis=-1, keepdims=True)
    return center, lax.rsqrt(spread + EPSILON)


def remote(src, dst, send, recv, peer):
    return pltpu.make_async_remote_copy(
        src_ref=src, dst_ref=dst, send_sem=send, recv_sem=recv, device_id=peer, device_id_type=MESH
    )


def greet(peers):
    barrier = pltpu.get_barrier_semaphore()
    for peer in peers:
        pl.semaphore_signal(barrier, inc=1, device_id=peer, device_id_type=MESH)
    pl.semaphore_wait(barrier, len(peers))


GELU_ROOT = 0.7978845608028654
GELU_CUBE = 0.044715


def place(value, order):
    return sum(((value >> bit) & 1) << (len(order) - 1 - at) for at, bit in enumerate(order))


def groups_of_eight(x):
    return jnp.sum(x.reshape(x.shape[0] // 8, 8, x.shape[1]), axis=0)


class Sum:
    def __init__(self, source, pair, other, result, send, recv):
        self.refs = source, pair, other, result
        self.send, self.recv = send, recv
        mine = lax.axis_index("tensor")
        self.core = mine & 1
        self.twin, self.across = {"tensor": mine ^ 1}, {"tensor": mine ^ 2}

    def half(self, chunk, core):
        return pl.ds(pl.multiple_of(chunk * CHUNK + core * BLOCK, BLOCK), BLOCK)

    def copy(self, stage, chunk):
        source, pair, other, result = self.refs
        own, theirs = self.half(chunk, self.core), self.half(chunk, 1 - self.core)
        src, dst, peer = (
            (source.at[theirs], pair.at[chunk], self.twin),
            (pair.at[chunk], other.at[chunk], self.across),
            (result.at[own], result.at[own], self.twin),
        )[stage]
        return remote(src, dst, self.send.at[stage, chunk], self.recv.at[stage, chunk], peer)

    def first(self, chunk):
        self.copy(0, chunk).start()

    def second(self, chunk):
        source, pair, other, result = self.refs
        self.copy(0, chunk).wait_recv()
        own = source[self.half(chunk, self.core), :].astype(F32)
        pair[chunk] = (own + pair[chunk].astype(F32)).astype(BF16)
        self.copy(1, chunk).start()

    def third(self, chunk):
        source, pair, other, result = self.refs
        self.copy(1, chunk).wait_recv()
        self.copy(1, chunk).wait_send()
        total = pair[chunk].astype(F32) + other[chunk].astype(F32)
        result[self.half(chunk, self.core), :] = total.astype(BF16)
        self.copy(2, chunk).start()

    def ready(self, chunk):
        self.copy(2, chunk).wait_recv()

    def sent(self, chunk, *stages):
        for stage in stages:
            self.copy(stage, chunk).wait_send()


class Scatter:
    def __init__(self, refs, order, send, recv):
        self.refs, self.order = refs, order
        self.send, self.recv = send, recv
        self.parts = refs[0].shape[0]
        self.me = lax.axis_index("dp")

    def copy(self, level):
        size = self.parts >> (level + 1)
        bit = (self.me >> self.order[level]) & 1
        return remote(
            self.refs[level].at[pl.ds((1 - bit) * size, size)],
            self.refs[level + 1],
            self.send.at[level],
            self.recv.at[level],
            {"dp": self.me ^ (1 << self.order[level])},
        )

    def go(self, level):
        self.copy(level).start()

    def add(self, level):
        size = self.parts >> (level + 1)
        bit = (self.me >> self.order[level]) & 1
        here, landed = self.refs[level], self.refs[level + 1]
        self.copy(level).wait_recv()

        def one(part, carry):
            total = here[bit * size + part].astype(F32) + landed[part].astype(F32)
            landed[part] = total.astype(landed.dtype)
            return carry

        lax.fori_loop(0, size, one, 0)

    def put(self, columns, found, offset):
        rows = self.refs[0].shape[1]
        for at in range(found.shape[0] // rows):
            part = place(offset // rows + at, self.order)
            self.refs[0][part, :, columns] = found[at * rows:(at + 1) * rows].astype(BF16)

    def step(self, level):
        self.add(level)
        if level + 1 < len(self.order):
            self.go(level + 1)

    def drain(self):
        for level in range(len(self.refs) - 1):
            self.copy(level).wait_send()


def layer_kernel(
    pieces, levels,
    lengths, gain_one, bias_one, gain_two, bias_two,
    tokens_hbm, w_attn_hbm, w_out_hbm, w_up_hbm, w_down_hbm, cotangent_hbm,
    output_hbm, grad_hbm, small_hbm, extra_hbm, gains_hbm,
    out_delta, grad_in, tokens, w_attn, w_out_all, w_zero, w_up, w_down, cotangent,
    act, query, key, value, query0, key0, probs, selected, mixed,
    stacks, scores, chances, offsets, lost,
    hidden_one, act_two, hidden, grad_pre, grad_mixed,
    feed_s, feed_a, feed_b, two_s, two_a, two_b, one_b,
    grad_key, grad_value, grad_sel, grad_key0, grad_proj, gain_sum, grad_query0,
    exchange, extra_parts, w_joined, *rest,
):
    seq, width = tokens.shape
    local = w_attn.shape[1]
    heads = local // HEAD
    blocks, chunks = seq // BLOCK, seq // CHUNK
    shards = mixed.shape[0]
    parts = 1 << levels
    own_rows = width // parts
    rest = list(rest)
    take = lambda count: [rest.pop(0) for _ in range(count)]
    scatter_refs = [take(levels + 1) for _ in range(10)]
    part_send, part_recv, zero_send, zero_recv, out_send, out_recv, mix_send, mix_recv = take(8)
    sums_send, sums_recv, scat_send, scat_recv, ex_send, ex_recv = take(6)
    load_sem, tokens_sem, store_sem, small_sem, extra_send, extra_recv = take(6)
    mine = lax.axis_index("tensor")
    me = lax.axis_index("dp")
    twin = {"tensor": mine ^ 1}
    across = {"tensor": mine ^ 2}
    peers = [{"tensor": mine ^ step} for step in (1, 2, 3)]

    loads = [
        pltpu.make_async_copy(source, target, load_sem.at[at])
        for at, (source, target) in enumerate((
            (w_attn_hbm, w_attn), (w_out_hbm, w_out_all.at[mine]),
            (w_up_hbm, w_up), (w_down_hbm, w_down), (cotangent_hbm, cotangent),
        ))
    ]
    attn_load, out_load, up_load, down_load, cot_load = loads

    def token_load(chunk):
        rows = rows_at(chunk, CHUNK)
        return pltpu.make_async_copy(tokens_hbm.at[rows], tokens.at[rows], tokens_sem.at[chunk])

    out_load.start()
    token_load(0).start()
    attn_load.start()
    for chunk in range(1, chunks):
        token_load(chunk).start()
    extra_parts[...] = jnp.zeros(extra_parts.shape, BF16)
    greet(tuple(peers) + tuple({"dp": me ^ (1 << level)} for level in range(levels)))
    for load in loads[2:]:
        load.start()

    def out_copy(stage, slot, peer):
        block = w_out_all.at[slot]
        return remote(block, block, out_send.at[stage], out_recv.at[stage], peer)

    def zero_copy(stage, peer, source):
        return remote(source, w_zero, zero_send.at[stage], zero_recv.at[0], peer)

    quarters = 4
    quarter = lax.rem(me, quarters)
    piece = local // quarters

    def part_copy(stage):
        slot = mine if stage == 0 else mine ^ 2
        start = (quarter, quarter, quarter // 2 * 2)[stage]
        peer = (across, {"dp": me ^ 1}, {"dp": me ^ 2})[stage]
        size = (piece, piece, 2 * piece)[stage]
        block = w_out_all.at[slot, pl.ds(pl.multiple_of(start * piece, piece), size)]
        return remote(block, block, part_send.at[stage], part_recv.at[stage], peer)

    head_rows = w_attn.at[pl.ds(0, 2), pl.ds(0, HEAD)]
    out_load.wait()
    out_copy(1, mine, twin).start()
    attn_load.wait()

    @pl.when(mine == 0)
    def _():
        zero_copy(0, across, head_rows).start()
        zero_copy(1, twin, head_rows).start()
        w_zero[...] = w_attn[0:2, 0:HEAD]

    part_copy(0).start()

    lane = lax.broadcasted_iota(jnp.int32, (1, local), 1)
    here = [(lane >= head * HEAD) & (lane < (head + 1) * HEAD) for head in range(heads)]
    row = lax.broadcasted_iota(jnp.int32, (BLOCK, 1), 0)
    column = lax.broadcasted_iota(jnp.int32, (1, BAND), 1) - PAD
    for ref in (key, value, key0, selected):
        ref[0:PAD, :] = jnp.zeros((PAD, ref.shape[1]), ref.dtype)
    def pick(found):
        total = found[(heads - 1) * BLOCK:]
        for head in range(heads - 1):
            total = jnp.where(here[head], found[head * BLOCK:(head + 1) * BLOCK], total)
        return total

    def stack(target, wide, scale):
        for head in range(heads):
            target[head * BLOCK:(head + 1) * BLOCK, :] = jnp.where(here[head], wide * scale, 0.0).astype(BF16)

    def project(step, carry):
        rows = rows_at(step, CHUNK)
        padded = pl.ds(pl.multiple_of(step * CHUNK + PAD, CHUNK), CHUNK)
        token_load(step).wait()
        center, scale = norm_stats(tokens[rows, :].astype(F32))
        low = (center * scale * gain_one[...].reshape(1, width) + bias_one[...].reshape(1, width)).astype(BF16)
        act[rows, :] = low
        query[rows, :] = dot_nt(low, w_attn[0]).astype(BF16)
        key[padded, :] = dot_nt(low, w_attn[1]).astype(BF16)
        value[padded, :] = dot_nt(low, w_attn[2]).astype(BF16)
        return carry

    lax.fori_loop(0, chunks, project, 0)

    @pl.when(mine != 2)
    def _():
        part_copy(0).wait_recv()
        part_copy(1).start()

    for load in loads[2:]:
        load.wait()

    def back_down(step, carry):
        rows = rows_at(step, CHUNK)
        grad_pre[rows, :] = dot_nt(cotangent[rows, :].astype(BF16), w_down[...]).astype(BF16)
        return carry

    lax.fori_loop(0, chunks, back_down, 0)

    @pl.when(mine == 2)
    def _():
        zero_copy(0, twin, w_zero).wait_recv()
        zero_copy(0, twin, w_zero).start()
        part_copy(0).wait_recv()
        part_copy(1).start()

    for ref in (grad_key, grad_value, grad_sel, grad_key0):
        ref[...] = jnp.zeros(ref.shape, ref.dtype)
    gain_sum[...] = jnp.zeros(gain_sum.shape, F32)

    @pl.when((mine & 1) == 1)
    def _():
        zero_copy(0, twin, w_zero).wait_recv()

    w_joined[:BLOCK, :] = w_zero[...].reshape(BLOCK, width)
    w_joined[BLOCK:, :] = w_attn[...].reshape(3 * local, width)

    def project0(step, carry):
        rows = rows_at(step, CHUNK)
        padded = pl.ds(pl.multiple_of(step * CHUNK + PAD, CHUNK), CHUNK)
        low = act[rows, :]
        found = dot_nt(low, w_zero[...].reshape(2 * HEAD, width)).astype(BF16).astype(F32)
        query0[rows, :] = (found[:, :HEAD] * SCALING).astype(BF16)
        key0[padded, :] = found[:, HEAD:].astype(BF16)
        return carry

    lax.fori_loop(0, chunks, project0, 0)

    @pl.when(mine != 2)
    def _():
        part_copy(1).wait_recv()
        part_copy(2).start()

    def select(block, carry):
        rows = rows_at(block, BLOCK)
        first, _ = first_of(row + block * BLOCK, lengths, pieces)
        first = first - block * BLOCK
        score = dot_nt(query0[rows, :], key0[pl.ds(rows.start, BAND), :])
        keep = (column > first) & (column < row)
        own = pl.ds(pl.multiple_of(rows.start + PAD, BLOCK), BLOCK)
        selected[own, :] = jnp.where(keep, jnp.maximum(score, 0.0), 0.0).astype(BF16)
        return carry

    lax.fori_loop(0, blocks, select, 0)

    @pl.when(mine == 2)
    def _():
        part_copy(1).wait_recv()
        part_copy(2).start()

    def mix_copy(stage, slot, block, peer):
        part = mixed.at[slot, rows_at(block, BLOCK)]
        return remote(part, part, mix_send.at[stage, block], mix_recv.at[stage, block], peer)

    def relay(chunk):
        for lot in (1, 0):
            block = 2 * chunk + lot
            mix_copy(0, mine ^ 2, block, across).wait_recv()
            mix_copy(2, mine ^ 2, block, twin).start()

    GROUP = 32
    places = BAND // BLOCK

    def attend_block(block, lot):
        rows = rows_at(block, BLOCK)
        band = rows.start
        first, valid = first_of(row + block * BLOCK, lengths, pieces)
        first = first - block * BLOCK
        inside = column >= first
        carried = (inside & (column < row)).astype(BF16)
        found = [
            dot(
                carried[:, part * BLOCK:(part + 1) * BLOCK],
                selected[pl.ds(pl.multiple_of(band + part * BLOCK, BLOCK), BLOCK), BAND - (part + 1) * BLOCK:],
            )
            for part in range(places)
        ]
        for at in range(places):
            cut = slice(at * BLOCK, (at + 1) * BLOCK)
            penalty = sum(found[part][:, cut] for part in range(at, places))
            offsets[lot, :, cut] = jnp.where((inside & (column <= row))[:, cut], -penalty, -1e30)
        stack(stacks.at[lot], query[rows, :].astype(F32), SCALING)
        scores[lot] = dot_nt(stacks[lot], key[pl.ds(band, BAND), :])
        for group in range(heads * BLOCK // GROUP):
            cut = slice(group * GROUP, (group + 1) * GROUP)
            at = group * GROUP % BLOCK
            logits = scores[lot, cut, :] + offsets[lot, at:at + GROUP, :]
            raised = jnp.exp(logits - jnp.max(logits, axis=-1, keepdims=True))
            chances[lot, cut, :] = (raised * (1.0 / jnp.sum(raised, axis=-1, keepdims=True))).astype(BF16)
        low = chances[lot]
        total = pick(dot(low, value[pl.ds(band, BAND), :]))
        return low, (total * valid.astype(F32)).astype(BF16)

    def attend(step, carry):
        chunk = chunks - 1 - step

        @pl.when(step == chunks - 1)
        def _():
            part_copy(2).wait_recv()
            out_copy(2, mine ^ 2, twin).start()

        done = [attend_block(2 * chunk + lot, lot) for lot in range(2)]
        for lot in (1, 0):
            block = 2 * chunk + lot
            probs[block] = done[lot][0]
            mixed[mine, rows_at(block, BLOCK), :] = done[lot][1]
            mix_copy(0, mine, block, across).start()
            mix_copy(1, mine, block, twin).start()

        return carry

    lax.fori_loop(0, chunks, attend, 0)

    relay(chunks - 1)
    out_copy(1, mine ^ 1, twin).wait_recv()
    out_copy(2, mine ^ 3, twin).wait_recv()

    feed = Sum(feed_s, feed_a, feed_b, out_delta, sums_send.at[0], sums_recv.at[0])
    two = Sum(two_s, two_a, two_b, grad_in, sums_send.at[1], sums_recv.at[1])
    one = Sum(two_s, two_a, one_b, grad_in, sums_send.at[2], sums_recv.at[2])
    straight = tuple(range(levels))
    turned = (1, 0, *straight[2:]) if levels > 1 else straight
    ups_a, ups_b, downs_a, downs_b, firsts_a, firsts_b, lasts_a, lasts_b, extras, gains = (
        Scatter(refs, order, scat_send.at[at], scat_recv.at[at])
        for at, (refs, order) in enumerate(zip(scatter_refs, (straight,) * 2 + (turned,) + (straight,) * 3 + (turned,) + (straight,) * 3))
    )
    gain_refs = gains.refs

    def feed_forward(step, carry):
        chunk = chunks - 1 - step
        rows = rows_at(chunk, CHUNK)

        @pl.when(chunk > 0)
        def _():
            relay(chunk - 1)

        for lot in (1, 0):
            block = 2 * chunk + lot
            mix_copy(1, mine ^ 1, block, twin).wait_recv()
            mix_copy(2, mine ^ 3, block, twin).wait_recv()
        joined = jnp.concatenate([mixed[shard, rows, :] for shard in range(shards)], axis=1)
        branch = dot(joined, w_out_all[...].reshape(shards * local, width))
        after = tokens[rows, :].astype(F32) + branch
        hidden_one[rows, :] = after
        feed_s[rows, :] = branch.astype(BF16)
        center, scale = norm_stats(after)
        low = (center * scale * gain_two[...].reshape(1, width) + bias_two[...].reshape(1, width)).astype(BF16)
        act_two[rows, :] = low
        up = dot(low, w_up[...])

        @pl.when(step > 1)
        def _():
            two.second(chunk + 1)

        square = up * up
        bent = jnp.tanh(up * (GELU_ROOT + (GELU_ROOT * GELU_CUBE) * square))
        share = 0.5 + 0.5 * bent
        active = up * share
        units = active.astype(BF16)
        hidden[rows, :] = units
        slope = share + active * (1.0 - bent) * (GELU_ROOT + (3.0 * GELU_ROOT * GELU_CUBE) * square)
        before = (grad_pre[rows, :].astype(F32) * slope).astype(BF16)
        grad_pre[rows, :] = before
        two_s[rows, :] = dot_nt(before, w_up[...]).astype(BF16)
        two.first(chunk)

        @pl.when(step == 0)
        def _():
            two.second(chunk)

        return carry

    lax.fori_loop(0, chunks, feed_forward, 0)
    two.second(0)

    half = width // 2
    units = w_up.shape[1]
    every = slice(None)
    cuts = [slice(strip * half, (strip + 1) * half) for strip in range(2)]
    fore, aft = slice(0, units // 2), slice(units // 2, units)
    for cut in cuts:
        found = dot_tn(cotangent[:, cut].astype(BF16), hidden[...])
        downs_a.put(every, found[:, fore], cut.start)
        downs_b.put(every, found[:, aft], cut.start)
    downs_a.go(0)
    downs_b.go(0)
    for cut in cuts:
        found = dot_tn(act_two[:, cut], grad_pre[...])
        ups_a.put(every, found[:, fore], cut.start)
        ups_b.put(every, found[:, aft], cut.start)
    ups_a.go(0)
    ups_b.go(0)
    two.third(chunks - 1)

    def feeding(chunk):
        rows = rows_at(chunk, CHUNK)
        branch = feed_s[rows, :].astype(F32)
        feed_s[rows, :] = (dot(hidden[rows, :], w_down[...]) + branch * (1.0 / shards)).astype(BF16)
        feed.first(chunk)

    def feed_early(step, carry):
        feeding(chunks - 1 - step)
        return carry

    lax.fori_loop(0, chunks // 2, feed_early, 0)

    across_row = lax.broadcasted_iota(jnp.int32, (1, BLOCK), 1)
    down_band = lax.broadcasted_iota(jnp.int32, (BAND, 1), 0) - PAD

    def attend_back(block, lot):
        rows = rows_at(block, BLOCK)
        band = pl.ds(rows.start, BAND)
        first, _ = first_of(across_row + block * BLOCK, lengths, pieces)
        first = first - block * BLOCK
        carried = ((down_band >= first) & (down_band < across_row)).astype(BF16)
        stack(stacks.at[lot], grad_mixed[rows, :].astype(F32), 1.0)
        stack(stacks.at[2 + lot], query[rows, :].astype(F32), SCALING)
        scores[lot] = dot_nt(stacks[lot], value[band, :])
        for group in range(BLOCK // GROUP):
            loss = jnp.zeros((GROUP, BAND), F32)
            for head in range(heads):
                cut = slice(head * BLOCK + group * GROUP, head * BLOCK + (group + 1) * GROUP)
                chance = probs[block, cut, :].astype(F32)
                grad = scores[lot, cut, :]
                weighed = chance * grad
                logits = weighed - chance * jnp.sum(weighed, axis=-1, keepdims=True)
                loss = loss - logits
                chances[lot, cut, :] = logits.astype(BF16)
            lost[lot, group * GROUP:(group + 1) * GROUP, :] = loss.astype(BF16)
        logits = chances[lot]
        queried = pick(dot(logits, key[band, :]))
        keyed = dot_tn(logits, stacks[2 + lot])
        valued = dot_tn(probs[block], stacks[lot])
        selects = [
            dot(carried[part * BLOCK:(part + 1) * BLOCK], lost[lot, :, :(part + 1) * BLOCK])
            for part in range(places)
        ]
        return (queried * SCALING).astype(BF16), keyed, valued, selects

    def attend_add(block, lot, keyed, valued, selects):
        rows = rows_at(block, BLOCK)
        band = pl.ds(rows.start, BAND)
        grad_key[band, :] = grad_key[band, :] + keyed
        grad_value[band, :] = grad_value[band, :] + valued
        for part in range(places):
            reach = (part + 1) * BLOCK
            rows_k = pl.ds(pl.multiple_of(rows.start + part * BLOCK, BLOCK), BLOCK)
            grad_sel[rows_k, BAND - reach:] = grad_sel[rows_k, BAND - reach:] + selects[part]
        own = pl.ds(pl.multiple_of(rows.start + PAD, BLOCK), BLOCK)
        score = jnp.where(selected[own, :] > 0, grad_sel[own, :], 0.0).astype(BF16)
        from_key = dot(score, key0[band, :])
        grad_query0[rows, :] = (from_key * SCALING).astype(BF16)
        grad_key0[band, :] = grad_key0[band, :] + dot_tn(score, query0[rows, :])

    def back(step, carry):
        chunk = chunks - 1 - step
        rows = rows_at(chunk, CHUNK)
        padded = pl.ds(pl.multiple_of(chunk * CHUNK + PAD, CHUNK), CHUNK)
        center, scale = norm_stats(hidden_one[rows, :])
        unit = center * scale
        two.ready(chunk)
        grad = grad_in[rows, :].astype(F32)
        gain_sum[2] = gain_sum[2] + groups_of_eight(grad * unit)
        gain_sum[3] = gain_sum[3] + groups_of_eight(grad)
        e = grad * gain_two[...].reshape(1, width)
        total = cotangent[rows, :] + scale * (
            e - jnp.mean(e, axis=-1, keepdims=True) - unit * jnp.mean(e * unit, axis=-1, keepdims=True)
        )
        hidden_one[rows, :] = total
        position = lax.broadcasted_iota(jnp.int32, (CHUNK, 1), 0) + chunk * CHUNK
        _, valid = first_of(position, lengths, pieces)
        grad_mixed[rows, :] = (
            dot_nt(total.astype(BF16), w_out_all[mine]).astype(BF16).astype(F32) * valid.astype(F32)
        ).astype(BF16)

        @pl.when(step == 1)
        def _():
            downs_b.step(0)
            downs_a.step(0)

        upper, *upper_adds = attend_back(2 * chunk + 1, 1)
        lower, *lower_adds = attend_back(2 * chunk, 0)

        @pl.when(step > 0)
        def _():
            one.second(chunk + 1)

        @pl.when(step == 0)
        def _():
            for late in range(chunks - 1, chunks // 2 - 1, -1):
                feed.second(late)

        @pl.when(step == 2)
        def _():
            ups_a.step(0)

        @pl.when(step == 3)
        def _():
            ups_b.step(0)

        attend_add(2 * chunk + 1, 1, *upper_adds)
        attend_add(2 * chunk, 0, *lower_adds)
        grad_q = jnp.concatenate([lower, upper], axis=0)
        grad_k = grad_key[padded, :].astype(BF16)
        grad_v = grad_value[padded, :].astype(BF16)
        grad_q0 = grad_query0[rows, :]
        grad_k0 = grad_key0[padded, :]
        grad_proj[rows, :] = jnp.concatenate(
            [grad_q0.astype(F32), grad_k0, grad_q.astype(F32), grad_k.astype(F32), grad_v.astype(F32)], axis=1
        ).astype(BF16)
        partial = dot(grad_proj[rows, :], w_joined[...])
        two.sent(chunk, 0, 2)
        two_s[rows, :] = partial.astype(BF16)
        one.first(chunk)
        center, scale = norm_stats(tokens[rows, :].astype(F32))
        gain_sum[0] = gain_sum[0] + groups_of_eight(partial * (center * scale))
        gain_sum[1] = gain_sum[1] + groups_of_eight(partial)

        @pl.when(step == 1)
        def _():
            downs_b.step(1)

        @pl.when(step == 3)
        def _():
            ups_a.step(1)

        @pl.when(step < chunks - 1)
        def _():
            two.third(chunk - 1)

        return carry

    lax.fori_loop(0, chunks, back, 0)

    for cut in cuts:
        extras.put(every, dot_tn(act[:, cut], grad_proj[:, :BLOCK]), cut.start)
    extras.go(0)
    sums = [jnp.sum(gain_sum[at], axis=0, keepdims=True) for at in range(4)]
    sums = jnp.concatenate(sums[:2] + [found * (1.0 / shards) for found in sums[2:]], axis=0)
    gain_refs[0][...] = jnp.zeros(gain_refs[0].shape, F32)
    for at in range(parts):
        gain_refs[0][place(at, straight), 0:4, 0:own_rows] = sums[:, at * own_rows:(at + 1) * own_rows]
    gains.go(0)
    edge = 2 * BLOCK
    for cut in cuts:
        found = jnp.concatenate(
            [
                dot_tn(act[:, cut], grad_proj[:, BLOCK + 2 * local:]),
                dot_tn(hidden_one[:, cut].astype(BF16), mixed[mine]),
            ],
            axis=1,
        )
        lasts_a.put(every, found[:, :edge], cut.start)
        lasts_b.put(every, found[:, edge:], cut.start)
    lasts_a.go(0)
    lasts_b.go(0)
    for cut in cuts:
        found = dot_tn(act[:, cut], grad_proj[:, BLOCK:BLOCK + 2 * local])
        firsts_a.put(every, found[:, :edge], cut.start)
        firsts_b.put(every, found[:, edge:], cut.start)
    firsts_a.go(0)
    firsts_b.go(0)
    downs_a.step(1)
    one.second(0)

    def ex_copy(step, slot, peer):
        block = exchange.at[slot]
        return remote(block, block, ex_send.at[step], ex_recv.at[step], peer)

    def extra_copy(step):
        return remote(
            extras.refs[-1].at[0], extra_parts.at[step], extra_send.at[0], extra_recv.at[step], {"tensor": 0}
        )

    def swap():
        exchange[mine] = gain_refs[-1][0]
        for step, peer in enumerate(peers):
            ex_copy(step, mine, peer).start()
        for step in range(3):

            @pl.when(mine == step + 1)
            def _():
                extra_copy(step).start()

    def feed_late(step, carry):
        chunk = chunks // 2 - 1 - step
        feeding(chunk)

        @pl.when(step > 0)
        def _():
            feed.second(chunk + 1)

        return carry

    lax.fori_loop(0, chunks // 2, feed_late, 0)
    ups_b.step(1)
    feed.second(0)

    def store(which, chunk):
        rows = rows_at(chunk, CHUNK)
        source, target = ((out_delta, output_hbm), (grad_in, grad_hbm))[which]
        return pltpu.make_async_copy(source.at[rows], target.at[rows], store_sem.at[which, chunk])

    def finish(chunk):
        rows = rows_at(chunk, CHUNK)
        one.third(chunk)
        center, scale = norm_stats(tokens[rows, :].astype(F32))
        unit = center * scale
        feed.third(chunk)
        one.ready(chunk)
        e = grad_in[rows, :].astype(F32) * gain_one[...].reshape(1, width)
        found = hidden_one[rows, :] + scale * (
            e - jnp.mean(e, axis=-1, keepdims=True) - unit * jnp.mean(e * unit, axis=-1, keepdims=True)
        )
        one.sent(chunk, 2)
        grad_in[rows, :] = found.astype(BF16)
        store(1, chunk).start()

    def give(chunk):
        rows = rows_at(chunk, CHUNK)
        feed.ready(chunk)
        found = tokens[rows, :].astype(F32) + out_delta[rows, :].astype(F32)
        feed.sent(chunk, 2)
        out_delta[rows, :] = found.astype(BF16)
        store(0, chunk).start()

    small = (
        (ups_a, 0, every), (ups_b, 1, every), (downs_a, 2, every), (downs_b, 3, every),
        (firsts_a, 4, pl.ds(0, edge)), (firsts_b, 4, pl.ds(edge, 2 * local - edge)),
        (lasts_a, 5, pl.ds(0, edge)), (lasts_b, 5, pl.ds(edge, 2 * local - edge)),
    )

    def small_store(at):
        group, slot, columns = small[at]
        return pltpu.make_async_copy(group.refs[-1].at[0], small_hbm.at[slot, :, columns], small_sem.at[at])

    left = list(range(chunks))
    finish(left.pop())
    for each in (extras, gains):
        each.step(0)
    finish(left.pop())
    for level in range(levels):
        for each in (lasts_a, firsts_a, lasts_b, firsts_b) if level == 0 else (firsts_a, lasts_a, firsts_b, lasts_b):
            each.step(level)
        if level + 1 < levels:
            for each in (extras, gains):
                each.step(level + 1)
        if level + 2 == levels:
            swap()
        if level >= 2:
            for each in (ups_a, downs_a, ups_b, downs_b):
                each.step(level)
        if left:
            give(left[-1] + 2)
            finish(left.pop())
    for at in range(8):
        small_store(at).start()
    give(1)
    give(0)

    for step, peer in enumerate(peers):
        ex_copy(step, mine ^ (step + 1), peer).wait_recv()
    last = pltpu.make_async_copy(exchange, gains_hbm, small_sem.at[len(small)])
    last.start()
    for step in range(3):

        @pl.when(mine == 0)
        def _():
            extra_copy(step).wait_recv()

        @pl.when(mine == step + 1)
        def _():
            extra_copy(step).wait_send()

    parts_store = pltpu.make_async_copy(extra_parts, extra_hbm.at[pl.ds(0, 3)], small_sem.at[len(small) + 1])
    own_store = pltpu.make_async_copy(extras.refs[-1].at[0], extra_hbm.at[3], small_sem.at[len(small) + 2])
    parts_store.start()
    own_store.start()

    def settle(chunk, carry):
        feed.sent(chunk, 0)
        one.sent(chunk, 0)
        store(0, chunk).wait()
        store(1, chunk).wait()

        for lot in range(2):
            block = 2 * chunk + lot
            mix_copy(0, mine, block, across).wait_send()
            mix_copy(1, mine, block, twin).wait_send()
            mix_copy(2, mine ^ 2, block, twin).wait_send()
        return carry

    lax.fori_loop(0, chunks, settle, 0)
    for each in (ups_a, ups_b, downs_a, downs_b, firsts_a, firsts_b, lasts_a, lasts_b, extras, gains):
        each.drain()
    for at in range(len(small)):
        small_store(at).wait()
    for each in (last, parts_store, own_store):
        each.wait()
    for step, peer in enumerate(peers):
        ex_copy(step, mine, peer).wait_send()
    for stage in range(3):
        part_copy(stage).wait_send()
    out_copy(1, mine, twin).wait_send()
    out_copy(2, mine ^ 2, twin).wait_send()

    @pl.when(mine == 0)
    def _():
        zero_copy(0, across, head_rows).wait_send()
        zero_copy(1, twin, head_rows).wait_send()

    @pl.when(mine == 2)
    def _():
        zero_copy(0, twin, w_zero).wait_send()


VMEM = pl.BlockSpec(memory_space=pltpu.VMEM)
SMEM = pl.BlockSpec(memory_space=pltpu.SMEM)
ANY = pl.BlockSpec(memory_space=pl.ANY)
DMA = pltpu.SemaphoreType.DMA
LIMIT = 67_000_000


def layer_call(tokens, gain_one, bias_one, w_attn, w_out, gain_two, bias_two, w_up, w_down, lengths, cotangent):
    seq, width = tokens.shape
    local = w_attn.shape[1]
    units = w_up.shape[1]
    heads = local // HEAD
    parts = lax.axis_size("dp")
    levels = parts.bit_length() - 1
    own_rows = width // parts
    blocks, chunks = seq // BLOCK, seq // CHUNK
    shards = lax.axis_size("tensor")
    shape = jax.ShapeDtypeStruct
    outs = (
        shape((seq, width), BF16),
        shape((seq, width), BF16),
        shape((6, own_rows, 2 * local), BF16),
        shape((4, own_rows, BLOCK), BF16),
        shape((shards, 8, BLOCK), F32),
    )

    def scatter(columns, rows, dtype):
        return [
            pltpu.VMEM((max(parts >> level, 1), rows, columns), dtype) for level in range(levels + 1)
        ]

    low = lambda *dims: pltpu.VMEM(dims, BF16)
    wide = lambda *dims: pltpu.VMEM(dims, F32)
    stacked = heads * BLOCK
    scratch = (
        [low(seq, width), low(seq, width), low(seq, width), low(3, local, width), low(shards, local, width), low(2, HEAD, width)]
        + [low(width, units), low(units, width), wide(seq, width)]
        + [low(seq, width), low(seq, local), low(seq + PAD, local), low(seq + PAD, local)]
        + [low(seq, HEAD), low(seq + PAD, HEAD), low(blocks, stacked, BAND), low(seq + PAD, BAND)]
        + [low(shards, seq, local)]
        + [low(4, stacked, local), wide(2, stacked, BAND), low(2, stacked, BAND), wide(2, BLOCK, BAND), low(2, BLOCK, BAND)]
        + [wide(seq, width), low(seq, width), low(seq, units), low(seq, units), low(seq, local)]
        + [low(seq, width), low(chunks, BLOCK, width), low(chunks, BLOCK, width)]
        + [low(seq, width), low(chunks, BLOCK, width), low(chunks, BLOCK, width), low(chunks, BLOCK, width)]
        + [wide(seq + PAD, local)] * 2
        + [wide(seq + PAD, BAND), wide(seq + PAD, HEAD)]
        + [low(seq, BLOCK + 3 * local), wide(4, 8, width), low(seq, HEAD)]
        + [wide(shards, 8, BLOCK), low(3, own_rows, BLOCK), low(BLOCK + 3 * local, width)]
        + scatter(units // 2, own_rows, BF16)
        + scatter(units // 2, own_rows, BF16)
        + scatter(units // 2, own_rows, BF16)
        + scatter(units // 2, own_rows, BF16)
        + scatter(2 * BLOCK, own_rows, BF16)
        + scatter(2 * local - 2 * BLOCK, own_rows, BF16)
        + scatter(2 * BLOCK, own_rows, BF16)
        + scatter(2 * local - 2 * BLOCK, own_rows, BF16)
        + scatter(BLOCK, own_rows, BF16)
        + scatter(BLOCK, 8, F32)
        + [DMA((3,)), DMA((3,)), DMA((2,)), DMA((1,)), DMA((3,)), DMA((3,)), DMA((3, blocks)), DMA((3, blocks))]
        + [DMA((3, 3, chunks)), DMA((3, 3, chunks)), DMA((10, levels)), DMA((10, levels)), DMA((3,)), DMA((3,))]
        + [DMA((5,)), DMA((chunks,)), DMA((2, chunks)), DMA((11,)), DMA((1,)), DMA((3,))]
    )
    operands = (
        lengths, gain_one, bias_one, gain_two, bias_two, tokens, w_attn, w_out, w_up, w_down, cotangent,
    )
    return pl.pallas_call(
        functools.partial(layer_kernel, lengths.shape[1], levels),
        out_shape=outs,
        in_specs=[SMEM] + [VMEM] * 4 + [ANY] * 6,
        out_specs=(ANY,) * len(outs),
        scratch_shapes=scratch,
        compiler_params=pltpu.CompilerParams(
            collective_id=0, has_side_effects=True, vmem_limit_bytes=LIMIT
        ),
        name="layer",
    )(*operands)


def output_kernel(output, grad_in, small, extra, gains, to_output, to_grad, to_attn, to_out, to_up, to_down, *to_gains):
    to_output[...] = output[...].astype(F32)
    to_grad[...] = grad_in[...].astype(F32)
    first = lax.axis_index("tensor") == 0

    @pl.when(pl.program_id(0) == 0)
    def _():
        half = small.shape[2]
        local = half // 2
        for ref, start in ((to_up, 0), (to_down, 2)):
            ref[:, :half] = small[start].astype(F32)
            ref[:, half:] = small[start + 1].astype(F32)
        added = sum(extra[at].astype(F32) for at in range(4))
        added = jnp.where(first, added, 0.0)
        found = small[4].astype(F32)
        for at in range(2):
            base = found[:, at * local:(at + 1) * local]
            head = base[:, :HEAD] + added[:, at * HEAD:(at + 1) * HEAD]
            to_attn[at] = jnp.concatenate([head, base[:, HEAD:]], axis=1)
        found = small[5].astype(F32)
        to_attn[2] = found[:, :local]
        to_out[...] = found[:, local:].T
        total = gains[0]
        for shard in range(1, gains.shape[0]):
            total = total + gains[shard]
        for at, ref in enumerate(to_gains):
            ref[...] = total[at, :ref.shape[0]]


def output_call(output, grad_in, small, extra, gains):
    rows, width = output.shape
    own, half = small.shape[1:]
    shape = lambda *dims: jax.ShapeDtypeStruct(dims, F32)
    outs = (
        [shape(rows, width)] * 2
        + [shape(3, own, half // 2), shape(half // 2, own), shape(own, 2 * half), shape(own, 2 * half)]
        + [shape(own)] * 4
    )
    block = pl.BlockSpec((CHUNK, width), lambda at: (at, 0))

    def whole(leaf):
        rank = len(leaf.shape)
        return pl.BlockSpec(leaf.shape, lambda at: (0,) * rank)

    return pl.pallas_call(
        output_kernel,
        grid=(rows // CHUNK,),
        out_shape=outs,
        in_specs=[block] * 2 + [whole(small), whole(extra), whole(gains)],
        out_specs=[block] * 2 + [whole(leaf) for leaf in outs[2:]],
        name="outputs",
    )(output, grad_in, small, extra, gains)


def body(
    tokens, gain_one, bias_one, w_attn, w_out, gain_two, bias_two, w_up, w_down, piece_lengths, cotangent
):
    found = layer_call(
        tokens, gain_one, bias_one, jnp.swapaxes(w_attn, 1, 2), w_out, gain_two, bias_two,
        w_up, w_down, piece_lengths, cotangent,
    )
    output, grad_in, grad_attn, grad_out, grad_up, grad_down, *gains = output_call(*found)
    return (output, grad_in, grad_attn, grad_out, grad_up, grad_down.T, *gains)


def solution(mesh):
    placed = (
        P("dp", None), P(), P(), P(None, None, "tensor"), P("tensor", None), P(), P(),
        P(None, "tensor"), P("tensor", None), P("dp", None), P("dp", None),
    )
    return jax.shard_map(
        body,
        mesh=mesh,
        in_specs=placed,
        out_specs=(
            P("dp", None), P("dp", None), P(None, "dp", "tensor"), P("tensor", "dp"), P("dp", "tensor"),
            P("tensor", "dp"), P("dp"), P("dp"), P("dp"), P("dp"),
        ),
        check_vma=False,
    )
```
